256 devices in a mesh: img: 8 (over x, core), vol: 32 (over y, z).
Axes of the slice: x: 4, y: 4, z: 8, core: 2. Of those that a mesh axis runs over, the one named last changes fastest.
Arguments:
- images: bfloat16 [2, 3072, 256, 128], P(None, 'img', 'vol'), may hold values from -6 to 6
- defocus: float32 [3072], P('img'), may hold values from 20 to 200
- candidates: int32 [3072, 8], P('img'), may hold values from 0 to 63, all different within a row
- counts: int32 [3072], P('img'), may hold values from 1 to 8
- noise_weight: float32 [256, 128], P('vol'), may hold values from 0.002 to 0.02
- volume: float32 [2, 256, 256, 128], P(None, 'vol'), may hold values from -6 to 6
- row_plane: int32 [64, 256], replicated, may hold values from 0 to 255
- row_line: int32 [64, 256], replicated, may hold values from 0 to 254
- row_weight: float32 [64, 256], replicated, may hold values from 0 to 1
- regularizer: float32 [256, 256, 128], P('vol', 'img'), may hold values from 0.05 to 0.5
Outputs:
- new_volume: float32 [2, 256, 256, 128], P(None, 'vol', 'img')
The draws below stay inside these ranges and needn't reach their ends.
Inputs may be any that keep to these rules, and one draw needn't show every extreme that they name: The entries of one row of candidates are distinct; only the first counts entries are used.
All inputs are finite; a program needn't handle non-finite values.
Results may differ from the reference program's by a relative error of at most 0.0066.
Values may be sent and summed in bfloat16 or wider, within the bound.
A program may use at most 128 MiB of HBM per device.

```python
import math
import jax
import jax.numpy as jnp
from jax import lax

ROWS = 256
COLS = 128
K = 64
LMAX = 8
TRANS = 4
IMG_DEV = 384
IMAGES = 3072
N_IMG = 8


def draw_row_plane(key, part):
    slope = jax.random.randint(key, (K, 1), -(ROWS - 1), ROWS)
    row_ids = jnp.arange(ROWS).astype(jnp.int32)[None, :]
    return (ROWS // 2 + (row_ids - ROWS // 2) * slope // ROWS).astype(jnp.int32)


def place_ends(values, own_key, least, largest):
    spot = [jax.random.randint(jax.random.fold_in(own_key, axis), (), 0, length) for axis, length in enumerate(values.shape)]
    main_axis = values.shape.index(max(values.shape))
    neighbour = spot[:main_axis] + [(spot[main_axis] + 1) % values.shape[main_axis]] + spot[main_axis + 1:]
    return values.at[tuple(spot)].set(least).at[tuple(neighbour)].set(largest)


def levels(rng, extent, split, low, top_value):
    factor_of = 1.0
    for axis_at, shards_of in split:
        draws = jax.random.uniform(jax.random.fold_in(jax.random.fold_in(rng, 6), axis_at), (shards_of,), jnp.float32, low / len(split), top_value / len(split))
        factor_of = factor_of * jnp.repeat(jnp.exp(draws), extent[axis_at] // shards_of).reshape((-1,) + (1,) * (len(extent) - 1 - axis_at))
    return factor_of


def distinct(rng, rows, count, top, lift):
    ranking = jax.random.permutation(jax.random.fold_in(rng, 1), count)
    pull = ranking
    for power in range(3):
        pull = pull * pull // count
    pull = pull * lift // count
    chance = jax.random.randint(jax.random.fold_in(rng, 2), (rows, count), 0, 4096) + pull
    holders = jax.random.permutation(jax.random.fold_in(rng, 3), rows)[jnp.arange(count) % rows]
    chance = jnp.where(jnp.arange(rows)[:, None] == holders[None, :], 1 << 14, chance)
    score = chance * count + jnp.arange(count)
    return lax.top_k(score.astype(jnp.int32), top)[1].astype(jnp.int32)


def noise(rng, extent, spread, most, pieces=(), held_as=jnp.bfloat16):
    loudness = levels(rng, extent, pieces, -0.22, 0.18) if pieces else 1.0
    result = jax.random.normal(rng, extent, jnp.float32) * spread * loudness
    return jnp.minimum(jnp.maximum(result, -most), most).astype(held_as)


def setup_inputs(seed: int = 0) -> dict:
    key_list = jax.random.split(jax.random.key(seed), 11)
    images = noise(key_list[0], (2, IMAGES, ROWS, COLS), 1.0, 6.0, ((1, 8), (2, 32)))
    defocus = jnp.clip(20.0 + 180.0 * jax.random.uniform(key_list[1], (IMAGES,), jnp.float32) ** levels(key_list[1], (IMAGES,), ((0, 8),), -0.2, 0.2), 20.0, 200.0)
    candidates = distinct(key_list[2], IMAGES, K, LMAX, 2048)
    counts = place_ends(jax.random.randint(key_list[3], (IMAGES,), 1, LMAX + 1), jax.random.fold_in(key_list[3], 1), 1, LMAX).astype(jnp.int32)
    noise_weight = jnp.clip(jnp.exp(math.log(0.02) - 2.30258502 * jax.random.uniform(key_list[4], (ROWS, COLS), jnp.float32) ** levels(key_list[4], (ROWS, COLS), ((0, 32),), -0.2, 0.2)), 0.002, 0.02)
    volume = noise(key_list[5], (2, ROWS, ROWS, COLS), 1.0, 6.0, ((1, 32),), jnp.float32)
    row_plane = draw_row_plane(jax.random.fold_in(key_list[10], 71), 0)
    row_line = place_ends(jax.random.randint(key_list[7], (K, ROWS), 0, ROWS - 1), jax.random.fold_in(key_list[7], 1), 0, (ROWS - 1) - 1).astype(jnp.int32)
    row_weight = jnp.clip(jax.random.uniform(key_list[8], (K, ROWS), jnp.float32, 0.0, 1.0), 0.0, 1.0)
    regularizer = jnp.clip(jnp.exp(math.log(0.5) - 2.3025851 * jax.random.uniform(key_list[9], (ROWS, ROWS, COLS), jnp.float32) ** levels(key_list[9], (ROWS, ROWS, COLS), ((0, 32), (1, 8)), -0.2, 0.2)), 0.05, 0.5)
    return dict(images=images, defocus=defocus, candidates=candidates, counts=counts, noise_weight=noise_weight, volume=volume, row_plane=row_plane, row_line=row_line, row_weight=row_weight, regularizer=regularizer)


AMPLITUDE = 0.1

def contrast_of(defocus, row_freq, col_freq):
    radius_sq = row_freq[:, None] * row_freq[:, None] + col_freq[None, :] * col_freq[None, :]
    angle = defocus[:, None, None] * radius_sq[None]
    return -(math.sqrt(1.0 - AMPLITUDE * AMPLITUDE) * jnp.sin(angle) + AMPLITUDE * jnp.cos(angle))

def shift_phases(row_freq, col_freq, number):
    shift_ids = jnp.arange(number)
    shift_x = (shift_ids % 2).astype(jnp.float32) - 0.5
    shift_y = (shift_ids // 2).astype(jnp.float32) - 0.5
    angle = -2.0 * math.pi * (shift_x[:, None, None] * col_freq[None, None, :] + shift_y[:, None, None] * row_freq[None, :, None])
    return (jnp.cos(angle), jnp.sin(angle))

def make_references(slices, cosine, sine):
    real_part = slices[0].astype(jnp.float32)
    imag_part = slices[1].astype(jnp.float32)
    shift_re = cosine[:, None] * real_part[None] - sine[:, None] * imag_part[None]
    shift_im = sine[:, None] * real_part[None] + cosine[:, None] * imag_part[None]
    shifted = jnp.stack([shift_re, shift_im], axis=2).astype(jnp.bfloat16)
    power = (real_part * real_part + imag_part * imag_part).astype(jnp.bfloat16)
    return (shifted, power)

def posterior_of(logits, candidates, counts):
    orientation = jnp.arange(logits.shape[2]).astype(jnp.int32)
    in_list = jnp.arange(candidates.shape[1]).astype(jnp.int32)[None, :] < counts[:, None]
    listed = jnp.any((candidates[:, :, None] == orientation[None, None, :]) & in_list[:, :, None], axis=1)
    allowed = listed[:, None, :]
    masked = jnp.where(allowed, logits, -1e+30)
    highest = lax.optimization_barrier(jnp.max(masked, axis=(1, 2), keepdims=True))
    exponent = jnp.where(allowed, jnp.exp(masked - highest), 0.0)
    return (exponent / lax.optimization_barrier(jnp.sum(exponent, axis=(1, 2), keepdims=True))).astype(jnp.bfloat16)

def reference(images, defocus, candidates, counts, noise_weight, volume, row_plane, row_line, row_weight, regularizer):
    row_freq = (jnp.arange(ROWS).astype(jnp.float32) - ROWS // 2) / ROWS
    col_freq = jnp.arange(COLS).astype(jnp.float32) / (2 * COLS)
    flat = volume.reshape(2, ROWS * ROWS, COLS)
    line_index = row_plane * ROWS + row_line
    lower = jnp.take(flat, line_index, axis=1)
    upper = jnp.take(flat, line_index + 1, axis=1)
    weight = row_weight[None, :, :, None]
    slices = (weight * lower + (1.0 - weight) * upper).astype(jnp.bfloat16)
    cosine, sine = shift_phases(row_freq, col_freq, TRANS)
    shifted, power = make_references(slices, cosine, sine)
    shifted_f = shifted.astype(jnp.float32)
    power_f = power.astype(jnp.float32)

    def block_step(carry, block_id):
        begin = (block_id * IMG_DEV).astype(jnp.int32)
        image_block = lax.dynamic_slice_in_dim(images, begin, IMG_DEV, 1)
        defocus_block = lax.dynamic_slice_in_dim(defocus, begin, IMG_DEV, 0)
        cand_block = lax.dynamic_slice_in_dim(candidates, begin, IMG_DEV, 0)
        count_block = lax.dynamic_slice_in_dim(counts, begin, IMG_DEV, 0)
        contrast = contrast_of(defocus_block, row_freq, col_freq)
        weighted = ((contrast * noise_weight)[None] * image_block).astype(jnp.bfloat16)
        squared = (contrast * contrast * noise_weight).astype(jnp.bfloat16)
        weighted_f = weighted.astype(jnp.float32)
        squared_f = squared.astype(jnp.float32)
        cross = jnp.einsum('jbrc,tkjrc->btk', weighted_f, shifted_f)
        quadratic = jnp.einsum('brc,krc->bk', squared_f, power_f)
        weights = posterior_of(cross - 0.5 * quadratic[:, None, :], cand_block, count_block).astype(jnp.float32)
        y_sum = carry[0] + jnp.einsum('btk,jbrc->tkrjc', weights, weighted_f)
        d_sum = carry[1] + jnp.einsum('btk,brc->tkrc', weights, squared_f)
        return ((y_sum, d_sum), None)
    start = (jnp.zeros((TRANS, K, ROWS, 2, COLS), jnp.float32), jnp.zeros((TRANS, K, ROWS, COLS), jnp.float32))
    (y_sum, d_sum), unused = lax.scan(block_step, start, jnp.arange(N_IMG).astype(jnp.int32))
    num_re = lax.optimization_barrier(jnp.sum(cosine[:, None] * y_sum[:, :, :, 0] + sine[:, None] * y_sum[:, :, :, 1], axis=0))
    num_im = lax.optimization_barrier(jnp.sum(cosine[:, None] * y_sum[:, :, :, 1] - sine[:, None] * y_sum[:, :, :, 0], axis=0))
    den = lax.optimization_barrier(jnp.sum(d_sum, axis=0))
    values = jnp.stack([num_re, num_im, den], axis=2).reshape(K * ROWS, 3 * COLS)
    flat_index = line_index.reshape(-1)
    flat_weight = row_weight.reshape(-1, 1)
    accum = jnp.zeros((ROWS * ROWS, 3 * COLS), jnp.float32)
    accum = accum.at[flat_index].add(flat_weight * values)
    accum = accum.at[flat_index + 1].add((1.0 - flat_weight) * values)
    accum = accum.reshape(ROWS, ROWS, 3, COLS)
    denom = accum[:, :, 2] + regularizer
    return jnp.stack([accum[:, :, 0] / denom, accum[:, :, 1] / denom], axis=0)
```

```python
import math

import jax
import jax.numpy as jnp
from jax import lax
from jax.sharding import PartitionSpec as P

ROWS = 256
COLS = 128
K = 64
TRANS = 4


AMPLITUDE = 0.1


def contrast_of(defocus, row_freq, col_freq):
    radius_sq = row_freq[:, None] * row_freq[:, None] + col_freq[None, :] * col_freq[None, :]
    angle = defocus[:, None, None] * radius_sq[None]
    return -(math.sqrt(1.0 - AMPLITUDE * AMPLITUDE) * jnp.sin(angle) + AMPLITUDE * jnp.cos(angle))


def shift_phases(row_freq, col_freq, number):
    shift_ids = jnp.arange(number)
    shift_x = (shift_ids % 2).astype(jnp.float32) - 0.5
    shift_y = (shift_ids // 2).astype(jnp.float32) - 0.5
    angle = (
        -2.0
        * math.pi
        * (
            shift_x[:, None, None] * col_freq[None, None, :]
            + shift_y[:, None, None] * row_freq[None, :, None]
        )
    )
    return (jnp.cos(angle), jnp.sin(angle))


def make_references(slices, cosine, sine):
    real_part = slices[0].astype(jnp.float32)
    imag_part = slices[1].astype(jnp.float32)
    shift_re = cosine[:, None] * real_part[None] - sine[:, None] * imag_part[None]
    shift_im = sine[:, None] * real_part[None] + cosine[:, None] * imag_part[None]
    shifted = jnp.stack([shift_re, shift_im], axis=2).astype(jnp.bfloat16)
    power = (real_part * real_part + imag_part * imag_part).astype(jnp.bfloat16)
    return (shifted, power)


def posterior_of(logits, counts):
    allowed = (jnp.arange(logits.shape[2])[None, :] < counts[:, None])[:, None, :]
    masked = jnp.where(allowed, logits, -1e30)
    highest = jnp.max(masked, axis=(1, 2), keepdims=True)
    exponent = jnp.where(allowed, jnp.exp(masked - highest), 0.0)
    return (exponent / jnp.sum(exponent, axis=(1, 2), keepdims=True)).astype(jnp.bfloat16)


def extract_rows(volume, plane_part, line_part, weight_part, slab_id):
    planes_here = volume.shape[1]
    flat = volume.reshape(2, planes_here * ROWS, COLS)
    local_plane = plane_part - slab_id * planes_here
    owned = (local_plane >= 0) & (local_plane < planes_here)
    line_index = jnp.clip(local_plane, 0, planes_here - 1) * ROWS + line_part
    lower = jnp.take(flat, line_index, axis=1)
    upper = jnp.take(flat, line_index + 1, axis=1)
    weight = weight_part[None, :, :, None]
    values = weight * lower + (1.0 - weight) * upper
    rounded = jnp.where(owned[None, :, :, None], values, 0.0).astype(jnp.bfloat16)
    return lax.optimization_barrier(rounded).astype(jnp.float32)


def insert_into(
    carry, piece, planes_all, lines_all, weights_all, slab_id, planes_here, line_first, line_count
):
    orient_count = piece.shape[0]
    number = piece.shape[1]
    local_plane = planes_all - slab_id * planes_here
    local_line = lines_all - line_first
    in_slab = (local_plane >= 0) & (local_plane < planes_here)
    lower_ok = in_slab & (local_line >= 0) & (local_line < line_count)
    upper_ok = in_slab & (local_line + 1 >= 0) & (local_line + 1 < line_count)
    dump_row = planes_here * line_count
    lower_index = jnp.where(lower_ok, local_plane * line_count + local_line, dump_row).reshape(-1)
    upper_index = jnp.where(upper_ok, local_plane * line_count + local_line + 1, dump_row).reshape(
        -1
    )
    values = piece.reshape(orient_count * number, 3 * COLS)
    weight = weights_all.reshape(-1, 1)
    carry = carry.at[lower_index].add(weight * values)
    return carry.at[upper_index].add((1.0 - weight) * values)


def body(
    images,
    defocus,
    candidates,
    counts,
    noise_weight,
    volume,
    row_plane,
    row_line,
    row_weight,
    regularizer,
):
    local_rows = noise_weight.shape[0]
    slab_id = lax.axis_index("vol")
    global_rows = slab_id * local_rows + jnp.arange(local_rows)
    row_freq = (global_rows.astype(jnp.float32) - ROWS // 2) / ROWS
    col_freq = jnp.arange(COLS).astype(jnp.float32) / (2 * COLS)
    img_count = lax.axis_size("img")
    group_id = lax.axis_index("img")
    share = K // img_count
    first = group_id * share
    plane_share = lax.dynamic_slice_in_dim(row_plane, first, share, 0)
    line_share = lax.dynamic_slice_in_dim(row_line, first, share, 0)
    weight_share = lax.dynamic_slice_in_dim(row_weight, first, share, 0)
    masked = extract_rows(volume, plane_share, line_share, weight_share, slab_id)
    own_rows = lax.psum_scatter(masked.astype(jnp.bfloat16), "vol", scatter_dimension=2, tiled=True)
    slices = lax.all_gather(own_rows, "img", axis=1, tiled=True)
    cosine, sine = shift_phases(row_freq, col_freq, TRANS)
    shifted, power = make_references(slices, cosine, sine)
    contrast = contrast_of(defocus, row_freq, col_freq)
    weighted = ((contrast * noise_weight)[None] * images).astype(jnp.bfloat16)
    squared = (contrast * contrast * noise_weight).astype(jnp.bfloat16)
    cross = jnp.einsum("jbrc,tkjrc->btk", weighted, shifted, preferred_element_type=jnp.float32)
    quadratic = jnp.einsum("brc,krc->bk", squared, power, preferred_element_type=jnp.float32)
    partial_logits = cross - 0.5 * quadratic[:, None, :]
    orientation = jnp.arange(K, dtype=jnp.int32)
    pick = candidates[:, :, None] == orientation[None, None, :]
    chosen = jnp.sum(
        jnp.where(pick[:, None, :, :], partial_logits[:, :, None, :], 0.0), axis=3
    )
    logits = lax.psum(chosen, "vol")
    listed = posterior_of(logits, counts)
    weights = jnp.sum(
        jnp.where(pick[:, None, :, :], listed[:, :, :, None], jnp.zeros((), jnp.bfloat16)),
        axis=2,
    )
    planes_here = volume.shape[1]
    y_part = jnp.einsum("btk,jbrc->tkrjc", weights, weighted, preferred_element_type=jnp.float32)
    d_part = jnp.einsum("btk,brc->tkrc", weights, squared, preferred_element_type=jnp.float32)
    num_re = jnp.sum(
        cosine[:, None] * y_part[:, :, :, 0] + sine[:, None] * y_part[:, :, :, 1], axis=0
    )
    num_im = jnp.sum(
        cosine[:, None] * y_part[:, :, :, 1] - sine[:, None] * y_part[:, :, :, 0], axis=0
    )
    partial_value = lax.psum_scatter(
        jnp.stack([num_re, num_im, jnp.sum(d_part, axis=0)], axis=2),
        "img",
        scatter_dimension=0,
        tiled=True,
    )
    initial = jnp.zeros((planes_here * ROWS + 1, 3 * COLS), jnp.float32)
    inserted = insert_into(
        initial,
        lax.all_gather(partial_value, "vol", axis=1, tiled=True),
        plane_share,
        line_share,
        weight_share,
        slab_id,
        planes_here,
        0,
        ROWS,
    )
    slab = inserted[: planes_here * ROWS].reshape(planes_here, ROWS, 3, COLS)
    summed = lax.psum_scatter(slab, "img", scatter_dimension=1, tiled=True)
    denom = summed[:, :, 2] + regularizer
    return jnp.stack([summed[:, :, 0] / denom, summed[:, :, 1] / denom], axis=0)


def solution(mesh):
    return jax.shard_map(
        body,
        mesh=mesh,
        in_specs=(
            P(None, "img", "vol", None),
            P("img"),
            P("img", None),
            P("img"),
            P("vol", None),
            P(None, "vol", None, None),
            P(),
            P(),
            P(),
            P("vol", "img", None),
        ),
        out_specs=P(None, "vol", "img", None),
        check_vma=False,
    )
```

```python
import math

import jax
import jax.numpy as jnp
from jax import lax
from jax.sharding import PartitionSpec as P

ROWS = 256
COLS = 128
K = 64
TRANS = 4


AMPLITUDE = 0.1


def contrast_of(defocus, row_freq, col_freq):
    radius_sq = row_freq[:, None] * row_freq[:, None] + col_freq[None, :] * col_freq[None, :]
    angle = defocus[:, None, None] * radius_sq[None]
    return -(math.sqrt(1.0 - AMPLITUDE * AMPLITUDE) * jnp.sin(angle) + AMPLITUDE * jnp.cos(angle))


def shift_phases(row_freq, col_freq, number):
    shift_ids = jnp.arange(number)
    shift_x = (shift_ids % 2).astype(jnp.float32) - 0.5
    shift_y = (shift_ids // 2).astype(jnp.float32) - 0.5
    angle = (
        -2.0
        * math.pi
        * (
            shift_x[:, None, None] * col_freq[None, None, :]
            + shift_y[:, None, None] * row_freq[None, :, None]
        )
    )
    return (jnp.cos(angle), jnp.sin(angle))


def make_references(slices, cosine, sine):
    real_part = slices[0].astype(jnp.float32)
    imag_part = slices[1].astype(jnp.float32)
    shift_re = cosine[:, None] * real_part[None] - sine[:, None] * imag_part[None]
    shift_im = sine[:, None] * real_part[None] + cosine[:, None] * imag_part[None]
    shifted = jnp.stack([shift_re, shift_im], axis=2).astype(jnp.bfloat16)
    power = (real_part * real_part + imag_part * imag_part).astype(jnp.bfloat16)
    return (shifted, power)


def posterior_of(logits, counts):
    allowed = (jnp.arange(logits.shape[2])[None, :] < counts[:, None])[:, None, :]
    masked = jnp.where(allowed, logits, -1e30)
    highest = jnp.max(masked, axis=(1, 2), keepdims=True)
    exponent = jnp.where(allowed, jnp.exp(masked - highest), 0.0)
    return (exponent / jnp.sum(exponent, axis=(1, 2), keepdims=True)).astype(jnp.bfloat16)


def extract_rows(volume, plane_part, line_part, weight_part, slab_id):
    planes_here = volume.shape[1]
    flat = volume.reshape(2, planes_here * ROWS, COLS)
    local_plane = plane_part - slab_id * planes_here
    owned = (local_plane >= 0) & (local_plane < planes_here)
    line_index = jnp.clip(local_plane, 0, planes_here - 1) * ROWS + line_part
    lower = jnp.take(flat, line_index, axis=1)
    upper = jnp.take(flat, line_index + 1, axis=1)
    weight = weight_part[None, :, :, None]
    values = weight * lower + (1.0 - weight) * upper
    rounded = jnp.where(owned[None, :, :, None], values, 0.0).astype(jnp.bfloat16)
    return lax.optimization_barrier(rounded).astype(jnp.float32)


def insert_into(
    carry, piece, planes_all, lines_all, weights_all, slab_id, planes_here, line_first, line_count
):
    orient_count = piece.shape[0]
    number = piece.shape[1]
    local_plane = planes_all - slab_id * planes_here
    local_line = lines_all - line_first
    in_slab = (local_plane >= 0) & (local_plane < planes_here)
    lower_ok = in_slab & (local_line >= 0) & (local_line < line_count)
    upper_ok = in_slab & (local_line + 1 >= 0) & (local_line + 1 < line_count)
    dump_row = planes_here * line_count
    lower_index = jnp.where(lower_ok, local_plane * line_count + local_line, dump_row).reshape(-1)
    upper_index = jnp.where(upper_ok, local_plane * line_count + local_line + 1, dump_row).reshape(
        -1
    )
    values = piece.reshape(orient_count * number, 3 * COLS)
    weight = weights_all.reshape(-1, 1)
    carry = carry.at[lower_index].add(weight * values)
    return carry.at[upper_index].add((1.0 - weight) * values)


def scatter_sum(x, axis_name, dim):
    count = lax.axis_size(axis_name)
    shape = x.shape
    split = x.reshape(shape[:dim] + (count, shape[dim] // count) + shape[dim + 1 :])
    received = lax.all_to_all(split, axis_name, dim, dim, tiled=True)
    return jnp.sum(received, axis=dim)


def gather_all(x, axis_name, dim):
    count = lax.axis_size(axis_name)
    copies = jnp.broadcast_to(x[None], (count,) + x.shape)
    received = jnp.moveaxis(lax.all_to_all(copies, axis_name, 0, 0, tiled=True), 0, dim)
    return received.reshape(x.shape[:dim] + (count * x.shape[dim],) + x.shape[dim + 1 :])


def body(
    images,
    defocus,
    candidates,
    counts,
    noise_weight,
    volume,
    row_plane,
    row_line,
    row_weight,
    regularizer,
):
    local_rows = noise_weight.shape[0]
    slab_id = lax.axis_index("vol")
    global_rows = slab_id * local_rows + jnp.arange(local_rows)
    row_freq = (global_rows.astype(jnp.float32) - ROWS // 2) / ROWS
    col_freq = jnp.arange(COLS).astype(jnp.float32) / (2 * COLS)
    img_count = lax.axis_size("img")
    group_id = lax.axis_index("img")
    share = K // img_count
    first = group_id * share
    plane_share = lax.dynamic_slice_in_dim(row_plane, first, share, 0)
    line_share = lax.dynamic_slice_in_dim(row_line, first, share, 0)
    weight_share = lax.dynamic_slice_in_dim(row_weight, first, share, 0)
    masked = extract_rows(volume, plane_share, line_share, weight_share, slab_id)
    own_rows = scatter_sum(masked.astype(jnp.bfloat16), "vol", 2)
    slices = gather_all(own_rows, "img", 1)
    cosine, sine = shift_phases(row_freq, col_freq, TRANS)
    shifted, power = make_references(slices, cosine, sine)
    contrast = contrast_of(defocus, row_freq, col_freq)
    weighted = ((contrast * noise_weight)[None] * images).astype(jnp.bfloat16)
    squared = (contrast * contrast * noise_weight).astype(jnp.bfloat16)
    cross = jnp.einsum("jbrc,tkjrc->btk", weighted, shifted, preferred_element_type=jnp.float32)
    quadratic = jnp.einsum("brc,krc->bk", squared, power, preferred_element_type=jnp.float32)
    partial_logits = cross - 0.5 * quadratic[:, None, :]
    orientation = jnp.arange(K, dtype=jnp.int32)
    pick = candidates[:, :, None] == orientation[None, None, :]
    chosen = jnp.sum(
        jnp.where(pick[:, None, :, :], partial_logits[:, :, None, :], 0.0), axis=3
    )
    logits = gather_all(scatter_sum(chosen, "vol", 0), "vol", 0)
    listed = posterior_of(logits, counts)
    weights = jnp.sum(
        jnp.where(pick[:, None, :, :], listed[:, :, :, None], jnp.zeros((), jnp.bfloat16)),
        axis=2,
    )
    planes_here = volume.shape[1]
    y_part = jnp.einsum("btk,jbrc->tkrjc", weights, weighted, preferred_element_type=jnp.float32)
    d_part = jnp.einsum("btk,brc->tkrc", weights, squared, preferred_element_type=jnp.float32)
    num_re = jnp.sum(
        cosine[:, None] * y_part[:, :, :, 0] + sine[:, None] * y_part[:, :, :, 1], axis=0
    )
    num_im = jnp.sum(
        cosine[:, None] * y_part[:, :, :, 1] - sine[:, None] * y_part[:, :, :, 0], axis=0
    )
    partial_value = scatter_sum(
        jnp.stack([num_re, num_im, jnp.sum(d_part, axis=0)], axis=2), "img", 0
    )
    initial = jnp.zeros((planes_here * ROWS + 1, 3 * COLS), jnp.float32)
    inserted = insert_into(
        initial,
        gather_all(partial_value, "vol", 1),
        plane_share,
        line_share,
        weight_share,
        slab_id,
        planes_here,
        0,
        ROWS,
    )
    slab = inserted[: planes_here * ROWS].reshape(planes_here, ROWS, 3, COLS)
    summed = scatter_sum(slab, "img", 1)
    denom = summed[:, :, 2] + regularizer
    return jnp.stack([summed[:, :, 0] / denom, summed[:, :, 1] / denom], axis=0)


def solution(mesh):
    return jax.shard_map(
        body,
        mesh=mesh,
        in_specs=(
            P(None, "img", "vol", None),
            P("img"),
            P("img", None),
            P("img"),
            P("vol", None),
            P(None, "vol", None, None),
            P(),
            P(),
            P(),
            P("vol", "img", None),
        ),
        out_specs=P(None, "vol", "img", None),
        check_vma=False,
    )
```

```python
import math

import jax
import jax.numpy as jnp
from jax import lax
from jax.sharding import PartitionSpec as P

ROWS = 256
COLS = 128
K = 64
TRANS = 4


AMPLITUDE = 0.1


def contrast_of(defocus, row_freq, col_freq):
    radius_sq = row_freq[:, None] * row_freq[:, None] + col_freq[None, :] * col_freq[None, :]
    angle = defocus[:, None, None] * radius_sq[None]
    return -(math.sqrt(1.0 - AMPLITUDE * AMPLITUDE) * jnp.sin(angle) + AMPLITUDE * jnp.cos(angle))


def shift_phases(row_freq, col_freq, number):
    shift_ids = jnp.arange(number)
    shift_x = (shift_ids % 2).astype(jnp.float32) - 0.5
    shift_y = (shift_ids // 2).astype(jnp.float32) - 0.5
    angle = (
        -2.0
        * math.pi
        * (
            shift_x[:, None, None] * col_freq[None, None, :]
            + shift_y[:, None, None] * row_freq[None, :, None]
        )
    )
    return (jnp.cos(angle), jnp.sin(angle))


def make_references(slices, cosine, sine):
    real_part = slices[0].astype(jnp.float32)
    imag_part = slices[1].astype(jnp.float32)
    shift_re = cosine[:, None] * real_part[None] - sine[:, None] * imag_part[None]
    shift_im = sine[:, None] * real_part[None] + cosine[:, None] * imag_part[None]
    shifted = jnp.stack([shift_re, shift_im], axis=2).astype(jnp.bfloat16)
    power = (real_part * real_part + imag_part * imag_part).astype(jnp.bfloat16)
    return (shifted, power)


def posterior_of(logits, counts):
    allowed = (jnp.arange(logits.shape[2])[None, :] < counts[:, None])[:, None, :]
    masked = jnp.where(allowed, logits, -1e30)
    highest = jnp.max(masked, axis=(1, 2), keepdims=True)
    exponent = jnp.where(allowed, jnp.exp(masked - highest), 0.0)
    return (exponent / jnp.sum(exponent, axis=(1, 2), keepdims=True)).astype(jnp.bfloat16)


def extract_rows(volume, plane_part, line_part, weight_part, slab_id):
    planes_here = volume.shape[1]
    flat = volume.reshape(2, planes_here * ROWS, COLS)
    local_plane = plane_part - slab_id * planes_here
    owned = (local_plane >= 0) & (local_plane < planes_here)
    line_index = jnp.clip(local_plane, 0, planes_here - 1) * ROWS + line_part
    lower = jnp.take(flat, line_index, axis=1)
    upper = jnp.take(flat, line_index + 1, axis=1)
    weight = weight_part[None, :, :, None]
    values = weight * lower + (1.0 - weight) * upper
    rounded = jnp.where(owned[None, :, :, None], values, 0.0).astype(jnp.bfloat16)
    return lax.optimization_barrier(rounded).astype(jnp.float32)


def insert_into(
    carry, piece, planes_all, lines_all, weights_all, slab_id, planes_here, line_first, line_count
):
    orient_count = piece.shape[0]
    number = piece.shape[1]
    local_plane = planes_all - slab_id * planes_here
    local_line = lines_all - line_first
    in_slab = (local_plane >= 0) & (local_plane < planes_here)
    lower_ok = in_slab & (local_line >= 0) & (local_line < line_count)
    upper_ok = in_slab & (local_line + 1 >= 0) & (local_line + 1 < line_count)
    dump_row = planes_here * line_count
    lower_index = jnp.where(lower_ok, local_plane * line_count + local_line, dump_row).reshape(-1)
    upper_index = jnp.where(upper_ok, local_plane * line_count + local_line + 1, dump_row).reshape(
        -1
    )
    values = piece.reshape(orient_count * number, 3 * COLS)
    weight = weights_all.reshape(-1, 1)
    carry = carry.at[lower_index].add(weight * values)
    return carry.at[upper_index].add((1.0 - weight) * values)


def scatter_sum(x, axis_name, dim):
    count = lax.axis_size(axis_name)
    shape = x.shape
    split = x.reshape(shape[:dim] + (count, shape[dim] // count) + shape[dim + 1 :])
    received = lax.all_to_all(split, axis_name, dim, dim, tiled=True)
    return jnp.sum(received, axis=dim)


def gather_all(x, axis_name, dim):
    count = lax.axis_size(axis_name)
    copies = jnp.broadcast_to(x[None], (count,) + x.shape)
    received = jnp.moveaxis(lax.all_to_all(copies, axis_name, 0, 0, tiled=True), 0, dim)
    return received.reshape(x.shape[:dim] + (count * x.shape[dim],) + x.shape[dim + 1 :])


def body(
    images,
    defocus,
    candidates,
    counts,
    noise_weight,
    volume,
    row_plane,
    row_line,
    row_weight,
    regularizer,
):
    local_rows = noise_weight.shape[0]
    slab_id = lax.axis_index("vol")
    global_rows = slab_id * local_rows + jnp.arange(local_rows)
    row_freq = (global_rows.astype(jnp.float32) - ROWS // 2) / ROWS
    col_freq = jnp.arange(COLS).astype(jnp.float32) / (2 * COLS)
    img_count = lax.axis_size("img")
    group_id = lax.axis_index("img")
    share = K // img_count
    first = group_id * share
    plane_share = lax.dynamic_slice_in_dim(row_plane, first, share, 0)
    line_share = lax.dynamic_slice_in_dim(row_line, first, share, 0)
    weight_share = lax.dynamic_slice_in_dim(row_weight, first, share, 0)
    masked = extract_rows(volume, plane_share, line_share, weight_share, slab_id)
    own_rows = scatter_sum(masked.astype(jnp.bfloat16), "vol", 2)
    slices = gather_all(own_rows, "img", 1)
    cosine, sine = shift_phases(row_freq, col_freq, TRANS)
    shifted, power = make_references(slices, cosine, sine)
    contrast = contrast_of(defocus, row_freq, col_freq)
    weighted = ((contrast * noise_weight)[None] * images).astype(jnp.bfloat16)
    squared = (contrast * contrast * noise_weight).astype(jnp.bfloat16)
    cross = jnp.einsum("jbrc,tkjrc->btk", weighted, shifted, preferred_element_type=jnp.float32)
    quadratic = jnp.einsum("brc,krc->bk", squared, power, preferred_element_type=jnp.float32)
    partial_logits = cross - 0.5 * quadratic[:, None, :]
    orientation = jnp.arange(K, dtype=jnp.int32)
    pick = candidates[:, :, None] == orientation[None, None, :]
    chosen = jnp.sum(
        jnp.where(pick[:, None, :, :], partial_logits[:, :, None, :], 0.0), axis=3
    )
    logits = gather_all(scatter_sum(chosen, "vol", 0), "vol", 0)
    listed = posterior_of(logits, counts)
    weights = jnp.sum(
        jnp.where(pick[:, None, :, :], listed[:, :, :, None], jnp.zeros((), jnp.bfloat16)),
        axis=2,
    )
    planes_here = volume.shape[1]
    y_part = jnp.einsum("btk,jbrc->tkrjc", weights, weighted, preferred_element_type=jnp.float32)
    d_part = jnp.einsum("btk,brc->tkrc", weights, squared, preferred_element_type=jnp.float32)
    num_re = jnp.sum(
        cosine[:, None] * y_part[:, :, :, 0] + sine[:, None] * y_part[:, :, :, 1], axis=0
    )
    num_im = jnp.sum(
        cosine[:, None] * y_part[:, :, :, 1] - sine[:, None] * y_part[:, :, :, 0], axis=0
    )
    partial_value = scatter_sum(
        jnp.stack([num_re, num_im, jnp.sum(d_part, axis=0)], axis=2), "img", 0
    )
    initial = jnp.zeros((planes_here * ROWS + 1, 3 * COLS), jnp.float32)
    inserted = insert_into(
        initial,
        gather_all(partial_value.astype(jnp.bfloat16), "vol", 1).astype(jnp.float32),
        plane_share,
        line_share,
        weight_share,
        slab_id,
        planes_here,
        0,
        ROWS,
    )
    slab = inserted[: planes_here * ROWS].reshape(planes_here, ROWS, 3, COLS)
    summed = scatter_sum(slab, "img", 1)
    denom = summed[:, :, 2] + regularizer
    return jnp.stack([summed[:, :, 0] / denom, summed[:, :, 1] / denom], axis=0)


def solution(mesh):
    return jax.shard_map(
        body,
        mesh=mesh,
        in_specs=(
            P(None, "img", "vol", None),
            P("img"),
            P("img", None),
            P("img"),
            P("vol", None),
            P(None, "vol", None, None),
            P(),
            P(),
            P(),
            P("vol", "img", None),
        ),
        out_specs=P(None, "vol", "img", None),
        check_vma=False,
    )
```

```python
import math

import jax
import jax.numpy as jnp
from jax import lax
from jax.experimental import pallas as pl
from jax.experimental.pallas import tpu as pltpu
from jax.sharding import PartitionSpec as P

ROWS = 256
COLS = 128
K = 64
TRANS = 4


AMPLITUDE = 0.1


def contrast_of(defocus, row_freq, col_freq):
    radius_sq = row_freq[:, None] * row_freq[:, None] + col_freq[None, :] * col_freq[None, :]
    angle = defocus[:, None, None] * radius_sq[None]
    return -(math.sqrt(1.0 - AMPLITUDE * AMPLITUDE) * jnp.sin(angle) + AMPLITUDE * jnp.cos(angle))


def shift_phases(row_freq, col_freq, number):
    shift_ids = jnp.arange(number)
    shift_x = (shift_ids % 2).astype(jnp.float32) - 0.5
    shift_y = (shift_ids // 2).astype(jnp.float32) - 0.5
    angle = (
        -2.0
        * math.pi
        * (
            shift_x[:, None, None] * col_freq[None, None, :]
            + shift_y[:, None, None] * row_freq[None, :, None]
        )
    )
    return (jnp.cos(angle), jnp.sin(angle))


def make_references(slices, cosine, sine):
    real_part = slices[0].astype(jnp.float32)
    imag_part = slices[1].astype(jnp.float32)
    shift_re = cosine[:, None] * real_part[None] - sine[:, None] * imag_part[None]
    shift_im = sine[:, None] * real_part[None] + cosine[:, None] * imag_part[None]
    shifted = jnp.stack([shift_re, shift_im], axis=2).astype(jnp.bfloat16)
    power = (real_part * real_part + imag_part * imag_part).astype(jnp.bfloat16)
    return (shifted, power)


def posterior_of(logits, counts):
    allowed = (jnp.arange(logits.shape[2])[None, :] < counts[:, None])[:, None, :]
    masked = jnp.where(allowed, logits, -1e30)
    highest = jnp.max(masked, axis=(1, 2), keepdims=True)
    exponent = jnp.where(allowed, jnp.exp(masked - highest), 0.0)
    return (exponent / jnp.sum(exponent, axis=(1, 2), keepdims=True)).astype(jnp.bfloat16)


def extract_rows(volume, plane_part, line_part, weight_part, slab_id):
    planes_here = volume.shape[1]
    flat = volume.reshape(2, planes_here * ROWS, COLS)
    local_plane = plane_part - slab_id * planes_here
    owned = (local_plane >= 0) & (local_plane < planes_here)
    line_index = jnp.clip(local_plane, 0, planes_here - 1) * ROWS + line_part
    lower = jnp.take(flat, line_index, axis=1)
    upper = jnp.take(flat, line_index + 1, axis=1)
    weight = weight_part[None, :, :, None]
    values = weight * lower + (1.0 - weight) * upper
    rounded = jnp.where(owned[None, :, :, None], values, 0.0).astype(jnp.bfloat16)
    return lax.optimization_barrier(rounded).astype(jnp.float32)


def insert_into(
    carry, piece, planes_all, lines_all, weights_all, slab_id, planes_here, line_first, line_count
):
    orient_count = piece.shape[0]
    number = piece.shape[1]
    local_plane = planes_all - slab_id * planes_here
    local_line = lines_all - line_first
    in_slab = (local_plane >= 0) & (local_plane < planes_here)
    lower_ok = in_slab & (local_line >= 0) & (local_line < line_count)
    upper_ok = in_slab & (local_line + 1 >= 0) & (local_line + 1 < line_count)
    dump_row = planes_here * line_count
    lower_index = jnp.where(lower_ok, local_plane * line_count + local_line, dump_row).reshape(-1)
    upper_index = jnp.where(upper_ok, local_plane * line_count + local_line + 1, dump_row).reshape(
        -1
    )
    values = piece.reshape(orient_count * number, 3 * COLS)
    weight = weights_all.reshape(-1, 1)
    carry = carry.at[lower_index].add(weight * values)
    return carry.at[upper_index].add((1.0 - weight) * values)


def scatter_sum(x, axis_name, dim):
    count = lax.axis_size(axis_name)
    shape = x.shape
    split = x.reshape(shape[:dim] + (count, shape[dim] // count) + shape[dim + 1 :])
    received = lax.all_to_all(split, axis_name, dim, dim, tiled=True)
    return jnp.sum(received, axis=dim)


def gather_all(x, axis_name, dim):
    count = lax.axis_size(axis_name)
    copies = jnp.broadcast_to(x[None], (count,) + x.shape)
    received = jnp.moveaxis(lax.all_to_all(copies, axis_name, 0, 0, tiled=True), 0, dim)
    return received.reshape(x.shape[:dim] + (count * x.shape[dim],) + x.shape[dim + 1 :])


def insert_kernel(start_ref, weight_ref, value_ref, out_ref):
    lines = out_ref.shape[0]
    rows = value_ref.shape[0]
    chunk = 512
    first_slot = pl.program_id(0) * lines
    slot = first_slot + lax.broadcasted_iota(jnp.int32, (lines, chunk), 0)
    total = jnp.zeros(out_ref.shape, jnp.float32)
    for part in range(rows // chunk):
        cols = pl.ds(part * chunk, chunk)
        start = start_ref[:, cols]
        weight = weight_ref[:, cols]
        spread = jnp.where(slot == start, weight, jnp.where(slot == start + 1, 1.0 - weight, 0.0))
        high = spread.astype(jnp.bfloat16)
        low = (spread - high.astype(jnp.float32)).astype(jnp.bfloat16)
        block = value_ref[cols, :]
        total += jnp.dot(high, block, preferred_element_type=jnp.float32)
        total += jnp.dot(low, block, preferred_element_type=jnp.float32)
    out_ref[...] = total


def insert_rows(values, start, weight, planes_here):
    rows, width = values.shape
    return pl.pallas_call(
        insert_kernel,
        grid=(planes_here,),
        in_specs=[
            pl.BlockSpec((1, rows), lambda q: (0, 0)),
            pl.BlockSpec((1, rows), lambda q: (0, 0)),
            pl.BlockSpec((rows, width), lambda q: (0, 0)),
        ],
        out_specs=pl.BlockSpec((ROWS, width), lambda q: (q, 0)),
        out_shape=jax.ShapeDtypeStruct((planes_here * ROWS, width), jnp.float32),
        compiler_params=pltpu.CompilerParams(vmem_limit_bytes=48 * 1024 * 1024),
        cost_estimate=pl.CostEstimate(
            flops=4 * planes_here * ROWS * rows * width,
            bytes_accessed=rows * width * 2 + planes_here * ROWS * width * 4,
            transcendentals=0,
        ),
    )(start.reshape(1, rows), weight.reshape(1, rows), values)


def body(
    images,
    defocus,
    candidates,
    counts,
    noise_weight,
    volume,
    row_plane,
    row_line,
    row_weight,
    regularizer,
):
    local_rows = noise_weight.shape[0]
    slab_id = lax.axis_index("vol")
    global_rows = slab_id * local_rows + jnp.arange(local_rows)
    row_freq = (global_rows.astype(jnp.float32) - ROWS // 2) / ROWS
    col_freq = jnp.arange(COLS).astype(jnp.float32) / (2 * COLS)
    img_count = lax.axis_size("img")
    group_id = lax.axis_index("img")
    share = K // img_count
    first = group_id * share
    plane_share = lax.dynamic_slice_in_dim(row_plane, first, share, 0)
    line_share = lax.dynamic_slice_in_dim(row_line, first, share, 0)
    weight_share = lax.dynamic_slice_in_dim(row_weight, first, share, 0)
    masked = extract_rows(volume, plane_share, line_share, weight_share, slab_id)
    own_rows = scatter_sum(masked.astype(jnp.bfloat16), "vol", 2)
    slices = gather_all(own_rows, "img", 1)
    cosine, sine = shift_phases(row_freq, col_freq, TRANS)
    shifted, power = make_references(slices, cosine, sine)
    contrast = contrast_of(defocus, row_freq, col_freq)
    weighted = ((contrast * noise_weight)[None] * images).astype(jnp.bfloat16)
    squared = (contrast * contrast * noise_weight).astype(jnp.bfloat16)
    cross = jnp.einsum("jbrc,tkjrc->btk", weighted, shifted, preferred_element_type=jnp.float32)
    quadratic = jnp.einsum("brc,krc->bk", squared, power, preferred_element_type=jnp.float32)
    partial_logits = cross - 0.5 * quadratic[:, None, :]
    orientation = jnp.arange(K, dtype=jnp.int32)
    pick = candidates[:, :, None] == orientation[None, None, :]
    chosen = jnp.sum(
        jnp.where(pick[:, None, :, :], partial_logits[:, :, None, :], 0.0), axis=3
    )
    logits = gather_all(scatter_sum(chosen, "vol", 0), "vol", 0)
    listed = posterior_of(logits, counts)
    weights = jnp.sum(
        jnp.where(pick[:, None, :, :], listed[:, :, :, None], jnp.zeros((), jnp.bfloat16)),
        axis=2,
    )
    planes_here = volume.shape[1]
    y_part = jnp.einsum("btk,jbrc->tkrjc", weights, weighted, preferred_element_type=jnp.float32)
    d_part = jnp.einsum("btk,brc->tkrc", weights, squared, preferred_element_type=jnp.float32)
    num_re = jnp.sum(
        cosine[:, None] * y_part[:, :, :, 0] + sine[:, None] * y_part[:, :, :, 1], axis=0
    )
    num_im = jnp.sum(
        cosine[:, None] * y_part[:, :, :, 1] - sine[:, None] * y_part[:, :, :, 0], axis=0
    )
    partial_value = scatter_sum(
        jnp.stack([num_re, num_im, jnp.sum(d_part, axis=0)], axis=2), "img", 0
    )
    local_plane = plane_share - slab_id * planes_here
    in_slab = (local_plane >= 0) & (local_plane < planes_here)
    start = jnp.where(in_slab, local_plane * ROWS + line_share, -2)
    piece = gather_all(partial_value.astype(jnp.bfloat16), "vol", 1)
    inserted = insert_rows(
        piece.reshape(share * ROWS, 3 * COLS), start.reshape(-1), weight_share.reshape(-1), planes_here
    )
    slab = inserted.reshape(planes_here, ROWS, 3, COLS)
    summed = scatter_sum(slab, "img", 1)
    denom = summed[:, :, 2] + regularizer
    return jnp.stack([summed[:, :, 0] / denom, summed[:, :, 1] / denom], axis=0)


def solution(mesh):
    return jax.shard_map(
        body,
        mesh=mesh,
        in_specs=(
            P(None, "img", "vol", None),
            P("img"),
            P("img", None),
            P("img"),
            P("vol", None),
            P(None, "vol", None, None),
            P(),
            P(),
            P(),
            P("vol", "img", None),
        ),
        out_specs=P(None, "vol", "img", None),
        check_vma=False,
    )
```

```python
import math

import jax
import jax.numpy as jnp
from jax import lax
from jax.experimental import pallas as pl
from jax.experimental.pallas import tpu as pltpu
from jax.sharding import PartitionSpec as P

ROWS = 256
COLS = 128
K = 64
TRANS = 4


AMPLITUDE = 0.1


def contrast_of(defocus, row_freq, col_freq):
    radius_sq = row_freq[:, None] * row_freq[:, None] + col_freq[None, :] * col_freq[None, :]
    angle = defocus[:, None, None] * radius_sq[None]
    return -(math.sqrt(1.0 - AMPLITUDE * AMPLITUDE) * jnp.sin(angle) + AMPLITUDE * jnp.cos(angle))


def shift_phases(row_freq, col_freq, number):
    shift_ids = jnp.arange(number)
    shift_x = (shift_ids % 2).astype(jnp.float32) - 0.5
    shift_y = (shift_ids // 2).astype(jnp.float32) - 0.5
    angle = (
        -2.0
        * math.pi
        * (
            shift_x[:, None, None] * col_freq[None, None, :]
            + shift_y[:, None, None] * row_freq[None, :, None]
        )
    )
    return (jnp.cos(angle), jnp.sin(angle))


def make_references(slices, cosine, sine):
    real_part = slices[0].astype(jnp.float32)
    imag_part = slices[1].astype(jnp.float32)
    shift_re = cosine[:, None] * real_part[None] - sine[:, None] * imag_part[None]
    shift_im = sine[:, None] * real_part[None] + cosine[:, None] * imag_part[None]
    shifted = jnp.stack([shift_re, shift_im], axis=2).astype(jnp.bfloat16)
    power = (real_part * real_part + imag_part * imag_part).astype(jnp.bfloat16)
    return (shifted, power)


def posterior_of(logits, counts):
    allowed = (jnp.arange(logits.shape[2])[None, :] < counts[:, None])[:, None, :]
    masked = jnp.where(allowed, logits, -1e30)
    highest = jnp.max(masked, axis=(1, 2), keepdims=True)
    exponent = jnp.where(allowed, jnp.exp(masked - highest), 0.0)
    return (exponent / jnp.sum(exponent, axis=(1, 2), keepdims=True)).astype(jnp.bfloat16)


def extract_rows(volume, plane_part, line_part, weight_part, slab_id):
    planes_here = volume.shape[1]
    flat = volume.reshape(2, planes_here * ROWS, COLS)
    local_plane = plane_part - slab_id * planes_here
    owned = (local_plane >= 0) & (local_plane < planes_here)
    line_index = jnp.clip(local_plane, 0, planes_here - 1) * ROWS + line_part
    lower = jnp.take(flat, line_index, axis=1)
    upper = jnp.take(flat, line_index + 1, axis=1)
    weight = weight_part[None, :, :, None]
    values = weight * lower + (1.0 - weight) * upper
    rounded = jnp.where(owned[None, :, :, None], values, 0.0).astype(jnp.bfloat16)
    return lax.optimization_barrier(rounded).astype(jnp.float32)


def insert_into(
    carry, piece, planes_all, lines_all, weights_all, slab_id, planes_here, line_first, line_count
):
    orient_count = piece.shape[0]
    number = piece.shape[1]
    local_plane = planes_all - slab_id * planes_here
    local_line = lines_all - line_first
    in_slab = (local_plane >= 0) & (local_plane < planes_here)
    lower_ok = in_slab & (local_line >= 0) & (local_line < line_count)
    upper_ok = in_slab & (local_line + 1 >= 0) & (local_line + 1 < line_count)
    dump_row = planes_here * line_count
    lower_index = jnp.where(lower_ok, local_plane * line_count + local_line, dump_row).reshape(-1)
    upper_index = jnp.where(upper_ok, local_plane * line_count + local_line + 1, dump_row).reshape(
        -1
    )
    values = piece.reshape(orient_count * number, 3 * COLS)
    weight = weights_all.reshape(-1, 1)
    carry = carry.at[lower_index].add(weight * values)
    return carry.at[upper_index].add((1.0 - weight) * values)


def scatter_sum(x, axis_name, dim):
    count = lax.axis_size(axis_name)
    shape = x.shape
    split = x.reshape(shape[:dim] + (count, shape[dim] // count) + shape[dim + 1 :])
    received = lax.all_to_all(split, axis_name, dim, dim, tiled=True)
    return jnp.sum(received, axis=dim)


def gather_all(x, axis_name, dim):
    count = lax.axis_size(axis_name)
    copies = jnp.broadcast_to(x[None], (count,) + x.shape)
    received = jnp.moveaxis(lax.all_to_all(copies, axis_name, 0, 0, tiled=True), 0, dim)
    return received.reshape(x.shape[:dim] + (count * x.shape[dim],) + x.shape[dim + 1 :])


def insert_kernel(start_ref, weight_ref, value_ref, out_ref):
    lines = out_ref.shape[0]
    rows = value_ref.shape[0]
    chunk = 512
    first_slot = pl.program_id(0) * lines
    slot = first_slot + lax.broadcasted_iota(jnp.int32, (lines, chunk), 0)
    total = jnp.zeros(out_ref.shape, jnp.float32)
    for part in range(rows // chunk):
        cols = pl.ds(part * chunk, chunk)
        start = start_ref[:, cols]
        weight = weight_ref[:, cols]
        spread = jnp.where(slot == start, weight, jnp.where(slot == start + 1, 1.0 - weight, 0.0))
        high = spread.astype(jnp.bfloat16)
        low = (spread - high.astype(jnp.float32)).astype(jnp.bfloat16)
        block = value_ref[cols, :]
        total += jnp.dot(high, block, preferred_element_type=jnp.float32)
        total += jnp.dot(low, block, preferred_element_type=jnp.float32)
    out_ref[...] = total


def insert_rows(values, start, weight, planes_here):
    rows, width = values.shape
    return pl.pallas_call(
        insert_kernel,
        grid=(planes_here,),
        in_specs=[
            pl.BlockSpec((1, rows), lambda q: (0, 0)),
            pl.BlockSpec((1, rows), lambda q: (0, 0)),
            pl.BlockSpec((rows, width), lambda q: (0, 0)),
        ],
        out_specs=pl.BlockSpec((ROWS, width), lambda q: (q, 0)),
        out_shape=jax.ShapeDtypeStruct((planes_here * ROWS, width), jnp.float32),
        compiler_params=pltpu.CompilerParams(vmem_limit_bytes=48 * 1024 * 1024),
        cost_estimate=pl.CostEstimate(
            flops=4 * planes_here * ROWS * rows * width,
            bytes_accessed=rows * width * 2 + planes_here * ROWS * width * 4,
            transcendentals=0,
        ),
    )(start.reshape(1, rows), weight.reshape(1, rows), values)


def extract_kernel(start_ref, weight_ref, high_ref, low_ref, out_ref):
    rows = out_ref.shape[1]
    slots = high_ref.shape[1]
    chunk = 512
    start = start_ref[...]
    weight = weight_ref[...]
    totals = [jnp.zeros((rows, COLS), jnp.float32) for _ in range(2)]
    for part in range(slots // chunk):
        slot = part * chunk + lax.broadcasted_iota(jnp.int32, (rows, chunk), 1)
        spread = jnp.where(slot == start, weight, jnp.where(slot == start + 1, 1.0 - weight, 0.0))
        high = spread.astype(jnp.bfloat16)
        low = (spread - high.astype(jnp.float32)).astype(jnp.bfloat16)
        cols = pl.ds(part * chunk, chunk)
        for j in range(2):
            vol_high = high_ref[j, cols, :]
            vol_low = low_ref[j, cols, :]
            totals[j] += jnp.dot(high, vol_high, preferred_element_type=jnp.float32)
            totals[j] += jnp.dot(high, vol_low, preferred_element_type=jnp.float32)
            totals[j] += jnp.dot(low, vol_high, preferred_element_type=jnp.float32)
    for j in range(2):
        out_ref[j] = totals[j].astype(out_ref.dtype)


def extract_share(volume, start, weight):
    slots = volume.shape[1] * ROWS
    flat = volume.reshape(2, slots, COLS)
    high = flat.astype(jnp.bfloat16)
    low = (flat - high.astype(jnp.float32)).astype(jnp.bfloat16)
    rows = start.size
    return pl.pallas_call(
        extract_kernel,
        grid=(rows // ROWS,),
        in_specs=[
            pl.BlockSpec((ROWS, 1), lambda q: (q, 0)),
            pl.BlockSpec((ROWS, 1), lambda q: (q, 0)),
            pl.BlockSpec((2, slots, COLS), lambda q: (0, 0, 0)),
            pl.BlockSpec((2, slots, COLS), lambda q: (0, 0, 0)),
        ],
        out_specs=pl.BlockSpec((2, ROWS, COLS), lambda q: (0, q, 0)),
        out_shape=jax.ShapeDtypeStruct((2, rows, COLS), jnp.bfloat16),
        compiler_params=pltpu.CompilerParams(vmem_limit_bytes=48 * 1024 * 1024),
        cost_estimate=pl.CostEstimate(
            flops=12 * rows * slots * COLS,
            bytes_accessed=2 * 2 * slots * COLS * 2 + 2 * rows * COLS * 2,
            transcendentals=0,
        ),
    )(start.reshape(rows, 1), weight.reshape(rows, 1), high, low)


def body(
    images,
    defocus,
    candidates,
    counts,
    noise_weight,
    volume,
    row_plane,
    row_line,
    row_weight,
    regularizer,
):
    local_rows = noise_weight.shape[0]
    slab_id = lax.axis_index("vol")
    global_rows = slab_id * local_rows + jnp.arange(local_rows)
    row_freq = (global_rows.astype(jnp.float32) - ROWS // 2) / ROWS
    col_freq = jnp.arange(COLS).astype(jnp.float32) / (2 * COLS)
    img_count = lax.axis_size("img")
    group_id = lax.axis_index("img")
    share = K // img_count
    first = group_id * share
    plane_share = lax.dynamic_slice_in_dim(row_plane, first, share, 0)
    line_share = lax.dynamic_slice_in_dim(row_line, first, share, 0)
    weight_share = lax.dynamic_slice_in_dim(row_weight, first, share, 0)
    planes_here = volume.shape[1]
    local_plane = plane_share - slab_id * planes_here
    in_slab = (local_plane >= 0) & (local_plane < planes_here)
    start = jnp.where(in_slab, local_plane * ROWS + line_share, -2)
    masked = extract_share(volume, start.reshape(-1), weight_share.reshape(-1))
    own_rows = scatter_sum(masked.reshape(2, share, ROWS, COLS), "vol", 2)
    slices = gather_all(own_rows, "img", 1)
    cosine, sine = shift_phases(row_freq, col_freq, TRANS)
    shifted, power = make_references(slices, cosine, sine)
    contrast = contrast_of(defocus, row_freq, col_freq)
    weighted = ((contrast * noise_weight)[None] * images).astype(jnp.bfloat16)
    squared = (contrast * contrast * noise_weight).astype(jnp.bfloat16)
    cross = jnp.einsum("jbrc,tkjrc->btk", weighted, shifted, preferred_element_type=jnp.float32)
    quadratic = jnp.einsum("brc,krc->bk", squared, power, preferred_element_type=jnp.float32)
    partial_logits = cross - 0.5 * quadratic[:, None, :]
    orientation = jnp.arange(K, dtype=jnp.int32)
    pick = candidates[:, :, None] == orientation[None, None, :]
    chosen = jnp.sum(
        jnp.where(pick[:, None, :, :], partial_logits[:, :, None, :], 0.0), axis=3
    )
    logits = gather_all(scatter_sum(chosen, "vol", 0), "vol", 0)
    listed = posterior_of(logits, counts)
    weights = jnp.sum(
        jnp.where(pick[:, None, :, :], listed[:, :, :, None], jnp.zeros((), jnp.bfloat16)),
        axis=2,
    )
    y_part = jnp.einsum("btk,jbrc->tkrjc", weights, weighted, preferred_element_type=jnp.float32)
    d_part = jnp.einsum("btk,brc->tkrc", weights, squared, preferred_element_type=jnp.float32)
    num_re = jnp.sum(
        cosine[:, None] * y_part[:, :, :, 0] + sine[:, None] * y_part[:, :, :, 1], axis=0
    )
    num_im = jnp.sum(
        cosine[:, None] * y_part[:, :, :, 1] - sine[:, None] * y_part[:, :, :, 0], axis=0
    )
    partial_value = scatter_sum(
        jnp.stack([num_re, num_im, jnp.sum(d_part, axis=0)], axis=2), "img", 0
    )
    piece = gather_all(partial_value.astype(jnp.bfloat16), "vol", 1)
    inserted = insert_rows(
        piece.reshape(share * ROWS, 3 * COLS), start.reshape(-1), weight_share.reshape(-1), planes_here
    )
    slab = inserted.reshape(planes_here, ROWS, 3, COLS)
    summed = scatter_sum(slab, "img", 1)
    denom = summed[:, :, 2] + regularizer
    return jnp.stack([summed[:, :, 0] / denom, summed[:, :, 1] / denom], axis=0)


def solution(mesh):
    return jax.shard_map(
        body,
        mesh=mesh,
        in_specs=(
            P(None, "img", "vol", None),
            P("img"),
            P("img", None),
            P("img"),
            P("vol", None),
            P(None, "vol", None, None),
            P(),
            P(),
            P(),
            P("vol", "img", None),
        ),
        out_specs=P(None, "vol", "img", None),
        check_vma=False,
    )
```

```python
import math

import jax
import jax.numpy as jnp
from jax import lax
from jax.experimental import pallas as pl
from jax.experimental.pallas import tpu as pltpu
from jax.sharding import PartitionSpec as P

ROWS = 256
COLS = 128
K = 64
TRANS = 4


AMPLITUDE = 0.1


def contrast_of(defocus, row_freq, col_freq):
    radius_sq = row_freq[:, None] * row_freq[:, None] + col_freq[None, :] * col_freq[None, :]
    angle = defocus[:, None, None] * radius_sq[None]
    return -(math.sqrt(1.0 - AMPLITUDE * AMPLITUDE) * jnp.sin(angle) + AMPLITUDE * jnp.cos(angle))


def shift_phases(row_freq, col_freq, number):
    shift_ids = jnp.arange(number)
    shift_x = (shift_ids % 2).astype(jnp.float32) - 0.5
    shift_y = (shift_ids // 2).astype(jnp.float32) - 0.5
    angle = (
        -2.0
        * math.pi
        * (
            shift_x[:, None, None] * col_freq[None, None, :]
            + shift_y[:, None, None] * row_freq[None, :, None]
        )
    )
    return (jnp.cos(angle), jnp.sin(angle))


def make_references(slices, cosine, sine):
    real_part = slices[0].astype(jnp.float32)
    imag_part = slices[1].astype(jnp.float32)
    shift_re = cosine[:, None] * real_part[None] - sine[:, None] * imag_part[None]
    shift_im = sine[:, None] * real_part[None] + cosine[:, None] * imag_part[None]
    shifted = jnp.stack([shift_re, shift_im], axis=2).astype(jnp.bfloat16)
    power = (real_part * real_part + imag_part * imag_part).astype(jnp.bfloat16)
    return (shifted, power)


def posterior_of(logits, counts):
    allowed = (jnp.arange(logits.shape[2])[None, :] < counts[:, None])[:, None, :]
    masked = jnp.where(allowed, logits, -1e30)
    highest = jnp.max(masked, axis=(1, 2), keepdims=True)
    exponent = jnp.where(allowed, jnp.exp(masked - highest), 0.0)
    return (exponent / jnp.sum(exponent, axis=(1, 2), keepdims=True)).astype(jnp.bfloat16)


def extract_rows(volume, plane_part, line_part, weight_part, slab_id):
    planes_here = volume.shape[1]
    flat = volume.reshape(2, planes_here * ROWS, COLS)
    local_plane = plane_part - slab_id * planes_here
    owned = (local_plane >= 0) & (local_plane < planes_here)
    line_index = jnp.clip(local_plane, 0, planes_here - 1) * ROWS + line_part
    lower = jnp.take(flat, line_index, axis=1)
    upper = jnp.take(flat, line_index + 1, axis=1)
    weight = weight_part[None, :, :, None]
    values = weight * lower + (1.0 - weight) * upper
    rounded = jnp.where(owned[None, :, :, None], values, 0.0).astype(jnp.bfloat16)
    return lax.optimization_barrier(rounded).astype(jnp.float32)


def insert_into(
    carry, piece, planes_all, lines_all, weights_all, slab_id, planes_here, line_first, line_count
):
    orient_count = piece.shape[0]
    number = piece.shape[1]
    local_plane = planes_all - slab_id * planes_here
    local_line = lines_all - line_first
    in_slab = (local_plane >= 0) & (local_plane < planes_here)
    lower_ok = in_slab & (local_line >= 0) & (local_line < line_count)
    upper_ok = in_slab & (local_line + 1 >= 0) & (local_line + 1 < line_count)
    dump_row = planes_here * line_count
    lower_index = jnp.where(lower_ok, local_plane * line_count + local_line, dump_row).reshape(-1)
    upper_index = jnp.where(upper_ok, local_plane * line_count + local_line + 1, dump_row).reshape(
        -1
    )
    values = piece.reshape(orient_count * number, 3 * COLS)
    weight = weights_all.reshape(-1, 1)
    carry = carry.at[lower_index].add(weight * values)
    return carry.at[upper_index].add((1.0 - weight) * values)


def scatter_sum(x, axis_name, dim):
    count = lax.axis_size(axis_name)
    shape = x.shape
    split = x.reshape(shape[:dim] + (count, shape[dim] // count) + shape[dim + 1 :])
    received = lax.all_to_all(split, axis_name, dim, dim, tiled=True)
    return jnp.sum(received, axis=dim)


def gather_all(x, axis_name, dim):
    count = lax.axis_size(axis_name)
    copies = jnp.broadcast_to(x[None], (count,) + x.shape)
    received = jnp.moveaxis(lax.all_to_all(copies, axis_name, 0, 0, tiled=True), 0, dim)
    return received.reshape(x.shape[:dim] + (count * x.shape[dim],) + x.shape[dim + 1 :])


def insert_kernel(start_ref, weight_ref, value_ref, out_ref):
    lines = out_ref.shape[0]
    rows = value_ref.shape[0]
    chunk = 512
    first_slot = pl.program_id(0) * lines
    slot = first_slot + lax.broadcasted_iota(jnp.int32, (lines, chunk), 0)
    total = jnp.zeros(out_ref.shape, jnp.float32)
    for part in range(rows // chunk):
        cols = pl.ds(part * chunk, chunk)
        start = start_ref[:, cols]
        weight = weight_ref[:, cols]
        spread = jnp.where(slot == start, weight, jnp.where(slot == start + 1, 1.0 - weight, 0.0))
        high = spread.astype(jnp.bfloat16)
        low = (spread - high.astype(jnp.float32)).astype(jnp.bfloat16)
        block = value_ref[cols, :]
        total += jnp.dot(high, block, preferred_element_type=jnp.float32)
        total += jnp.dot(low, block, preferred_element_type=jnp.float32)
    out_ref[...] = total


def insert_rows(values, start, weight, planes_here):
    rows, width = values.shape
    return pl.pallas_call(
        insert_kernel,
        grid=(planes_here,),
        in_specs=[
            pl.BlockSpec((1, rows), lambda q: (0, 0)),
            pl.BlockSpec((1, rows), lambda q: (0, 0)),
            pl.BlockSpec((rows, width), lambda q: (0, 0)),
        ],
        out_specs=pl.BlockSpec((ROWS, width), lambda q: (q, 0)),
        out_shape=jax.ShapeDtypeStruct((planes_here * ROWS, width), jnp.float32),
        compiler_params=pltpu.CompilerParams(vmem_limit_bytes=48 * 1024 * 1024),
        cost_estimate=pl.CostEstimate(
            flops=4 * planes_here * ROWS * rows * width,
            bytes_accessed=rows * width * 2 + planes_here * ROWS * width * 4,
            transcendentals=0,
        ),
    )(start.reshape(1, rows), weight.reshape(1, rows), values)


def extract_kernel(start_ref, weight_ref, high_ref, middle_ref, low_ref, out_ref):
    rows = out_ref.shape[1]
    slots = high_ref.shape[0]
    chunk = 512
    start = start_ref[...]
    total = jnp.zeros((rows, high_ref.shape[1]), jnp.float32)
    for part in range(slots // chunk):
        slot = part * chunk + lax.broadcasted_iota(jnp.int32, (rows, chunk), 1)
        pick = (slot == start).astype(jnp.bfloat16)
        cols = pl.ds(part * chunk, chunk)
        for piece_ref in (high_ref, middle_ref, low_ref):
            total += jnp.dot(pick, piece_ref[cols, :], preferred_element_type=jnp.float32)
    weight = weight_ref[...]
    for j in range(2):
        lower = total[:, j * COLS : (j + 1) * COLS]
        upper = total[:, (2 + j) * COLS : (3 + j) * COLS]
        out_ref[j] = (weight * lower + (1.0 - weight) * upper).astype(out_ref.dtype)


def extract_share(volume, start, weight):
    slots = volume.shape[1] * ROWS
    flat = volume.reshape(2, slots, COLS)
    following = jnp.concatenate([flat[:, 1:], jnp.zeros_like(flat[:, :1])], axis=1)
    pairs = jnp.concatenate([flat, following], axis=0).transpose(1, 0, 2).reshape(slots, 4 * COLS)
    high = pairs.astype(jnp.bfloat16)
    rest = pairs - high.astype(jnp.float32)
    middle = rest.astype(jnp.bfloat16)
    low = (rest - middle.astype(jnp.float32)).astype(jnp.bfloat16)
    rows = start.size
    return pl.pallas_call(
        extract_kernel,
        grid=(rows // ROWS,),
        in_specs=[
            pl.BlockSpec((ROWS, 1), lambda q: (q, 0)),
            pl.BlockSpec((ROWS, 1), lambda q: (q, 0)),
            pl.BlockSpec((slots, 4 * COLS), lambda q: (0, 0)),
            pl.BlockSpec((slots, 4 * COLS), lambda q: (0, 0)),
            pl.BlockSpec((slots, 4 * COLS), lambda q: (0, 0)),
        ],
        out_specs=pl.BlockSpec((2, ROWS, COLS), lambda q: (0, q, 0)),
        out_shape=jax.ShapeDtypeStruct((2, rows, COLS), jnp.bfloat16),
        compiler_params=pltpu.CompilerParams(vmem_limit_bytes=48 * 1024 * 1024),
        cost_estimate=pl.CostEstimate(
            flops=24 * rows * slots * COLS,
            bytes_accessed=3 * slots * 4 * COLS * 2 + 2 * rows * COLS * 2,
            transcendentals=0,
        ),
    )(start.reshape(rows, 1), weight.reshape(rows, 1), high, middle, low)


def body(
    images,
    defocus,
    candidates,
    counts,
    noise_weight,
    volume,
    row_plane,
    row_line,
    row_weight,
    regularizer,
):
    local_rows = noise_weight.shape[0]
    slab_id = lax.axis_index("vol")
    global_rows = slab_id * local_rows + jnp.arange(local_rows)
    row_freq = (global_rows.astype(jnp.float32) - ROWS // 2) / ROWS
    col_freq = jnp.arange(COLS).astype(jnp.float32) / (2 * COLS)
    img_count = lax.axis_size("img")
    group_id = lax.axis_index("img")
    share = K // img_count
    first = group_id * share
    plane_share = lax.dynamic_slice_in_dim(row_plane, first, share, 0)
    line_share = lax.dynamic_slice_in_dim(row_line, first, share, 0)
    weight_share = lax.dynamic_slice_in_dim(row_weight, first, share, 0)
    planes_here = volume.shape[1]
    local_plane = plane_share - slab_id * planes_here
    in_slab = (local_plane >= 0) & (local_plane < planes_here)
    start = jnp.where(in_slab, local_plane * ROWS + line_share, -2)
    masked = extract_share(volume, start.reshape(-1), weight_share.reshape(-1))
    own_rows = scatter_sum(masked.reshape(2, share, ROWS, COLS), "vol", 2)
    slices = gather_all(own_rows, "img", 1)
    cosine, sine = shift_phases(row_freq, col_freq, TRANS)
    shifted, power = make_references(slices, cosine, sine)
    contrast = contrast_of(defocus, row_freq, col_freq)
    weighted = ((contrast * noise_weight)[None] * images).astype(jnp.bfloat16)
    squared = (contrast * contrast * noise_weight).astype(jnp.bfloat16)
    cross = jnp.einsum("jbrc,tkjrc->btk", weighted, shifted, preferred_element_type=jnp.float32)
    quadratic = jnp.einsum("brc,krc->bk", squared, power, preferred_element_type=jnp.float32)
    partial_logits = cross - 0.5 * quadratic[:, None, :]
    orientation = jnp.arange(K, dtype=jnp.int32)
    pick = candidates[:, :, None] == orientation[None, None, :]
    chosen = jnp.sum(
        jnp.where(pick[:, None, :, :], partial_logits[:, :, None, :], 0.0), axis=3
    )
    logits = gather_all(scatter_sum(chosen, "vol", 0), "vol", 0)
    listed = posterior_of(logits, counts)
    weights = jnp.sum(
        jnp.where(pick[:, None, :, :], listed[:, :, :, None], jnp.zeros((), jnp.bfloat16)),
        axis=2,
    )
    y_part = jnp.einsum("btk,jbrc->tkrjc", weights, weighted, preferred_element_type=jnp.float32)
    d_part = jnp.einsum("btk,brc->tkrc", weights, squared, preferred_element_type=jnp.float32)
    num_re = jnp.sum(
        cosine[:, None] * y_part[:, :, :, 0] + sine[:, None] * y_part[:, :, :, 1], axis=0
    )
    num_im = jnp.sum(
        cosine[:, None] * y_part[:, :, :, 1] - sine[:, None] * y_part[:, :, :, 0], axis=0
    )
    partial_value = scatter_sum(
        jnp.stack([num_re, num_im, jnp.sum(d_part, axis=0)], axis=2), "img", 0
    )
    piece = gather_all(partial_value.astype(jnp.bfloat16), "vol", 1)
    inserted = insert_rows(
        piece.reshape(share * ROWS, 3 * COLS), start.reshape(-1), weight_share.reshape(-1), planes_here
    )
    slab = inserted.reshape(planes_here, ROWS, 3, COLS)
    summed = scatter_sum(slab, "img", 1)
    denom = summed[:, :, 2] + regularizer
    return jnp.stack([summed[:, :, 0] / denom, summed[:, :, 1] / denom], axis=0)


def solution(mesh):
    return jax.shard_map(
        body,
        mesh=mesh,
        in_specs=(
            P(None, "img", "vol", None),
            P("img"),
            P("img", None),
            P("img"),
            P("vol", None),
            P(None, "vol", None, None),
            P(),
            P(),
            P(),
            P("vol", "img", None),
        ),
        out_specs=P(None, "vol", "img", None),
        check_vma=False,
    )
```

```python
import math

import jax
import jax.numpy as jnp
from jax import lax
from jax.experimental import pallas as pl
from jax.experimental.pallas import tpu as pltpu
from jax.sharding import PartitionSpec as P

ROWS = 256
COLS = 128
K = 64
TRANS = 4


AMPLITUDE = 0.1


def contrast_of(defocus, row_freq, col_freq):
    radius_sq = row_freq[:, None] * row_freq[:, None] + col_freq[None, :] * col_freq[None, :]
    angle = defocus[:, None, None] * radius_sq[None]
    return -(math.sqrt(1.0 - AMPLITUDE * AMPLITUDE) * jnp.sin(angle) + AMPLITUDE * jnp.cos(angle))


def shift_phases(row_freq, col_freq, number):
    shift_ids = jnp.arange(number)
    shift_x = (shift_ids % 2).astype(jnp.float32) - 0.5
    shift_y = (shift_ids // 2).astype(jnp.float32) - 0.5
    angle = (
        -2.0
        * math.pi
        * (
            shift_x[:, None, None] * col_freq[None, None, :]
            + shift_y[:, None, None] * row_freq[None, :, None]
        )
    )
    return (jnp.cos(angle), jnp.sin(angle))


def make_references(slices, cosine, sine):
    real_part = slices[0].astype(jnp.float32)
    imag_part = slices[1].astype(jnp.float32)
    shift_re = cosine[:, None] * real_part[None] - sine[:, None] * imag_part[None]
    shift_im = sine[:, None] * real_part[None] + cosine[:, None] * imag_part[None]
    shifted = jnp.stack([shift_re, shift_im], axis=2).astype(jnp.bfloat16)
    power = (real_part * real_part + imag_part * imag_part).astype(jnp.bfloat16)
    return (shifted, power)


def posterior_of(logits, counts):
    allowed = (jnp.arange(logits.shape[2])[None, :] < counts[:, None])[:, None, :]
    masked = jnp.where(allowed, logits, -1e30)
    highest = jnp.max(masked, axis=(1, 2), keepdims=True)
    exponent = jnp.where(allowed, jnp.exp(masked - highest), 0.0)
    return (exponent / jnp.sum(exponent, axis=(1, 2), keepdims=True)).astype(jnp.bfloat16)


def extract_rows(volume, plane_part, line_part, weight_part, slab_id):
    planes_here = volume.shape[1]
    flat = volume.reshape(2, planes_here * ROWS, COLS)
    local_plane = plane_part - slab_id * planes_here
    owned = (local_plane >= 0) & (local_plane < planes_here)
    line_index = jnp.clip(local_plane, 0, planes_here - 1) * ROWS + line_part
    lower = jnp.take(flat, line_index, axis=1)
    upper = jnp.take(flat, line_index + 1, axis=1)
    weight = weight_part[None, :, :, None]
    values = weight * lower + (1.0 - weight) * upper
    rounded = jnp.where(owned[None, :, :, None], values, 0.0).astype(jnp.bfloat16)
    return lax.optimization_barrier(rounded).astype(jnp.float32)


def insert_into(
    carry, piece, planes_all, lines_all, weights_all, slab_id, planes_here, line_first, line_count
):
    orient_count = piece.shape[0]
    number = piece.shape[1]
    local_plane = planes_all - slab_id * planes_here
    local_line = lines_all - line_first
    in_slab = (local_plane >= 0) & (local_plane < planes_here)
    lower_ok = in_slab & (local_line >= 0) & (local_line < line_count)
    upper_ok = in_slab & (local_line + 1 >= 0) & (local_line + 1 < line_count)
    dump_row = planes_here * line_count
    lower_index = jnp.where(lower_ok, local_plane * line_count + local_line, dump_row).reshape(-1)
    upper_index = jnp.where(upper_ok, local_plane * line_count + local_line + 1, dump_row).reshape(
        -1
    )
    values = piece.reshape(orient_count * number, 3 * COLS)
    weight = weights_all.reshape(-1, 1)
    carry = carry.at[lower_index].add(weight * values)
    return carry.at[upper_index].add((1.0 - weight) * values)


def scatter_sum(x, axis_name, dim):
    count = lax.axis_size(axis_name)
    shape = x.shape
    split = x.reshape(shape[:dim] + (count, shape[dim] // count) + shape[dim + 1 :])
    received = lax.all_to_all(split, axis_name, dim, dim, tiled=True)
    return jnp.sum(received, axis=dim)


def gather_all(x, axis_name, dim):
    count = lax.axis_size(axis_name)
    copies = jnp.broadcast_to(x[None], (count,) + x.shape)
    received = jnp.moveaxis(lax.all_to_all(copies, axis_name, 0, 0, tiled=True), 0, dim)
    return received.reshape(x.shape[:dim] + (count * x.shape[dim],) + x.shape[dim + 1 :])


def insert_kernel(start_ref, weight_ref, value_ref, out_ref):
    lines = out_ref.shape[0]
    rows = value_ref.shape[0]
    chunk = 512
    first_slot = pl.program_id(0) * lines
    slot = first_slot + lax.broadcasted_iota(jnp.int32, (lines, chunk), 0)
    total = jnp.zeros(out_ref.shape, jnp.float32)
    for part in range(rows // chunk):
        cols = pl.ds(part * chunk, chunk)
        start = start_ref[:, cols]
        weight = weight_ref[:, cols]
        spread = jnp.where(slot == start, weight, jnp.where(slot == start + 1, 1.0 - weight, 0.0))
        high = spread.astype(jnp.bfloat16)
        low = (spread - high.astype(jnp.float32)).astype(jnp.bfloat16)
        block = value_ref[cols, :]
        total += jnp.dot(high, block, preferred_element_type=jnp.float32)
        total += jnp.dot(low, block, preferred_element_type=jnp.float32)
    out_ref[...] = total


def insert_rows(values, start, weight, planes_here):
    rows, width = values.shape
    return pl.pallas_call(
        insert_kernel,
        grid=(planes_here,),
        in_specs=[
            pl.BlockSpec((1, rows), lambda q: (0, 0)),
            pl.BlockSpec((1, rows), lambda q: (0, 0)),
            pl.BlockSpec((rows, width), lambda q: (0, 0)),
        ],
        out_specs=pl.BlockSpec((ROWS, width), lambda q: (q, 0)),
        out_shape=jax.ShapeDtypeStruct((planes_here * ROWS, width), jnp.float32),
        compiler_params=pltpu.CompilerParams(vmem_limit_bytes=48 * 1024 * 1024),
        cost_estimate=pl.CostEstimate(
            flops=4 * planes_here * ROWS * rows * width,
            bytes_accessed=rows * width * 2 + planes_here * ROWS * width * 4,
            transcendentals=0,
        ),
    )(start.reshape(1, rows), weight.reshape(1, rows), values)


def extract_kernel(start_ref, weight_ref, high_ref, middle_ref, low_ref, out_ref):
    rows = out_ref.shape[1]
    slots = high_ref.shape[0]
    chunk = 512
    start = start_ref[...]
    total = jnp.zeros((rows, high_ref.shape[1]), jnp.float32)
    for part in range(slots // chunk):
        slot = part * chunk + lax.broadcasted_iota(jnp.int32, (rows, chunk), 1)
        pick = (slot == start).astype(jnp.bfloat16)
        cols = pl.ds(part * chunk, chunk)
        for piece_ref in (high_ref, middle_ref, low_ref):
            total += jnp.dot(pick, piece_ref[cols, :], preferred_element_type=jnp.float32)
    weight = weight_ref[...]
    for j in range(2):
        lower = total[:, j * COLS : (j + 1) * COLS]
        upper = total[:, (2 + j) * COLS : (3 + j) * COLS]
        out_ref[j] = (weight * lower + (1.0 - weight) * upper).astype(out_ref.dtype)


def extract_share(volume, start, weight):
    slots = volume.shape[1] * ROWS
    flat = volume.reshape(2, slots, COLS)
    following = jnp.concatenate([flat[:, 1:], jnp.zeros_like(flat[:, :1])], axis=1)
    pairs = jnp.concatenate([flat, following], axis=0).transpose(1, 0, 2).reshape(slots, 4 * COLS)
    high = lax.reduce_precision(pairs, exponent_bits=8, mantissa_bits=7)
    rest = pairs - high
    middle = lax.reduce_precision(rest, exponent_bits=8, mantissa_bits=7)
    low = rest - middle
    high, middle, low = (x.astype(jnp.bfloat16) for x in (high, middle, low))
    rows = start.size
    return pl.pallas_call(
        extract_kernel,
        grid=(rows // ROWS,),
        in_specs=[
            pl.BlockSpec((ROWS, 1), lambda q: (q, 0)),
            pl.BlockSpec((ROWS, 1), lambda q: (q, 0)),
            pl.BlockSpec((slots, 4 * COLS), lambda q: (0, 0)),
            pl.BlockSpec((slots, 4 * COLS), lambda q: (0, 0)),
            pl.BlockSpec((slots, 4 * COLS), lambda q: (0, 0)),
        ],
        out_specs=pl.BlockSpec((2, ROWS, COLS), lambda q: (0, q, 0)),
        out_shape=jax.ShapeDtypeStruct((2, rows, COLS), jnp.bfloat16),
        compiler_params=pltpu.CompilerParams(vmem_limit_bytes=48 * 1024 * 1024),
        cost_estimate=pl.CostEstimate(
            flops=24 * rows * slots * COLS,
            bytes_accessed=3 * slots * 4 * COLS * 2 + 2 * rows * COLS * 2,
            transcendentals=0,
        ),
    )(start.reshape(rows, 1), weight.reshape(rows, 1), high, middle, low)


def body(
    images,
    defocus,
    candidates,
    counts,
    noise_weight,
    volume,
    row_plane,
    row_line,
    row_weight,
    regularizer,
):
    local_rows = noise_weight.shape[0]
    slab_id = lax.axis_index("vol")
    global_rows = slab_id * local_rows + jnp.arange(local_rows)
    row_freq = (global_rows.astype(jnp.float32) - ROWS // 2) / ROWS
    col_freq = jnp.arange(COLS).astype(jnp.float32) / (2 * COLS)
    img_count = lax.axis_size("img")
    group_id = lax.axis_index("img")
    share = K // img_count
    first = group_id * share
    plane_share = lax.dynamic_slice_in_dim(row_plane, first, share, 0)
    line_share = lax.dynamic_slice_in_dim(row_line, first, share, 0)
    weight_share = lax.dynamic_slice_in_dim(row_weight, first, share, 0)
    planes_here = volume.shape[1]
    local_plane = plane_share - slab_id * planes_here
    in_slab = (local_plane >= 0) & (local_plane < planes_here)
    start = jnp.where(in_slab, local_plane * ROWS + line_share, -2)
    masked = extract_share(volume, start.reshape(-1), weight_share.reshape(-1))
    own_rows = scatter_sum(masked.reshape(2, share, ROWS, COLS), "vol", 2)
    slices = gather_all(own_rows, "img", 1)
    cosine, sine = shift_phases(row_freq, col_freq, TRANS)
    shifted, power = make_references(slices, cosine, sine)
    contrast = contrast_of(defocus, row_freq, col_freq)
    weighted = ((contrast * noise_weight)[None] * images).astype(jnp.bfloat16)
    squared = (contrast * contrast * noise_weight).astype(jnp.bfloat16)
    cross = jnp.einsum("jbrc,tkjrc->btk", weighted, shifted, preferred_element_type=jnp.float32)
    quadratic = jnp.einsum("brc,krc->bk", squared, power, preferred_element_type=jnp.float32)
    partial_logits = cross - 0.5 * quadratic[:, None, :]
    orientation = jnp.arange(K, dtype=jnp.int32)
    pick = candidates[:, :, None] == orientation[None, None, :]
    chosen = jnp.sum(
        jnp.where(pick[:, None, :, :], partial_logits[:, :, None, :], 0.0), axis=3
    )
    logits = gather_all(scatter_sum(chosen, "vol", 0), "vol", 0)
    listed = posterior_of(logits, counts)
    weights = jnp.sum(
        jnp.where(pick[:, None, :, :], listed[:, :, :, None], jnp.zeros((), jnp.bfloat16)),
        axis=2,
    )
    y_part = jnp.einsum("btk,jbrc->tkrjc", weights, weighted, preferred_element_type=jnp.float32)
    d_part = jnp.einsum("btk,brc->tkrc", weights, squared, preferred_element_type=jnp.float32)
    num_re = jnp.sum(
        cosine[:, None] * y_part[:, :, :, 0] + sine[:, None] * y_part[:, :, :, 1], axis=0
    )
    num_im = jnp.sum(
        cosine[:, None] * y_part[:, :, :, 1] - sine[:, None] * y_part[:, :, :, 0], axis=0
    )
    partial_value = scatter_sum(
        jnp.stack([num_re, num_im, jnp.sum(d_part, axis=0)], axis=2), "img", 0
    )
    piece = gather_all(partial_value.astype(jnp.bfloat16), "vol", 1)
    inserted = insert_rows(
        piece.reshape(share * ROWS, 3 * COLS), start.reshape(-1), weight_share.reshape(-1), planes_here
    )
    slab = inserted.reshape(planes_here, ROWS, 3, COLS)
    summed = scatter_sum(slab, "img", 1)
    denom = summed[:, :, 2] + regularizer
    return jnp.stack([summed[:, :, 0] / denom, summed[:, :, 1] / denom], axis=0)


def solution(mesh):
    return jax.shard_map(
        body,
        mesh=mesh,
        in_specs=(
            P(None, "img", "vol", None),
            P("img"),
            P("img", None),
            P("img"),
            P("vol", None),
            P(None, "vol", None, None),
            P(),
            P(),
            P(),
            P("vol", "img", None),
        ),
        out_specs=P(None, "vol", "img", None),
        check_vma=False,
    )
```

```python
import math

import jax
import jax.numpy as jnp
from jax import lax
from jax.experimental import pallas as pl
from jax.experimental.pallas import tpu as pltpu
from jax.sharding import Mesh, PartitionSpec as P

ROWS = 256
COLS = 128
K = 64
TRANS = 4


AMPLITUDE = 0.1


def contrast_of(defocus, row_freq, col_freq):
    radius_sq = row_freq[:, None] * row_freq[:, None] + col_freq[None, :] * col_freq[None, :]
    angle = defocus[:, None, None] * radius_sq[None]
    return -(math.sqrt(1.0 - AMPLITUDE * AMPLITUDE) * jnp.sin(angle) + AMPLITUDE * jnp.cos(angle))


def shift_phases(row_freq, col_freq, number):
    shift_ids = jnp.arange(number)
    shift_x = (shift_ids % 2).astype(jnp.float32) - 0.5
    shift_y = (shift_ids // 2).astype(jnp.float32) - 0.5
    angle = (
        -2.0
        * math.pi
        * (
            shift_x[:, None, None] * col_freq[None, None, :]
            + shift_y[:, None, None] * row_freq[None, :, None]
        )
    )
    return (jnp.cos(angle), jnp.sin(angle))


def make_references(slices, cosine, sine):
    real_part = slices[0].astype(jnp.float32)
    imag_part = slices[1].astype(jnp.float32)
    shift_re = cosine[:, None] * real_part[None] - sine[:, None] * imag_part[None]
    shift_im = sine[:, None] * real_part[None] + cosine[:, None] * imag_part[None]
    shifted = jnp.stack([shift_re, shift_im], axis=2).astype(jnp.bfloat16)
    power = (real_part * real_part + imag_part * imag_part).astype(jnp.bfloat16)
    return (shifted, power)


def posterior_of(logits, counts):
    allowed = (jnp.arange(logits.shape[2])[None, :] < counts[:, None])[:, None, :]
    masked = jnp.where(allowed, logits, -1e30)
    highest = jnp.max(masked, axis=(1, 2), keepdims=True)
    exponent = jnp.where(allowed, jnp.exp(masked - highest), 0.0)
    return (exponent / jnp.sum(exponent, axis=(1, 2), keepdims=True)).astype(jnp.bfloat16)


def extract_rows(volume, plane_part, line_part, weight_part, slab_id):
    planes_here = volume.shape[1]
    flat = volume.reshape(2, planes_here * ROWS, COLS)
    local_plane = plane_part - slab_id * planes_here
    owned = (local_plane >= 0) & (local_plane < planes_here)
    line_index = jnp.clip(local_plane, 0, planes_here - 1) * ROWS + line_part
    lower = jnp.take(flat, line_index, axis=1)
    upper = jnp.take(flat, line_index + 1, axis=1)
    weight = weight_part[None, :, :, None]
    values = weight * lower + (1.0 - weight) * upper
    rounded = jnp.where(owned[None, :, :, None], values, 0.0).astype(jnp.bfloat16)
    return lax.optimization_barrier(rounded).astype(jnp.float32)


def insert_into(
    carry, piece, planes_all, lines_all, weights_all, slab_id, planes_here, line_first, line_count
):
    orient_count = piece.shape[0]
    number = piece.shape[1]
    local_plane = planes_all - slab_id * planes_here
    local_line = lines_all - line_first
    in_slab = (local_plane >= 0) & (local_plane < planes_here)
    lower_ok = in_slab & (local_line >= 0) & (local_line < line_count)
    upper_ok = in_slab & (local_line + 1 >= 0) & (local_line + 1 < line_count)
    dump_row = planes_here * line_count
    lower_index = jnp.where(lower_ok, local_plane * line_count + local_line, dump_row).reshape(-1)
    upper_index = jnp.where(upper_ok, local_plane * line_count + local_line + 1, dump_row).reshape(
        -1
    )
    values = piece.reshape(orient_count * number, 3 * COLS)
    weight = weights_all.reshape(-1, 1)
    carry = carry.at[lower_index].add(weight * values)
    return carry.at[upper_index].add((1.0 - weight) * values)


def scatter_sum(x, axis_name, dim):
    count = lax.axis_size(axis_name)
    shape = x.shape
    split = x.reshape(shape[:dim] + (count, shape[dim] // count) + shape[dim + 1 :])
    received = lax.all_to_all(split, axis_name, dim, dim, tiled=True)
    return jnp.sum(received, axis=dim)


def gather_all(x, axis_name, dim):
    count = lax.axis_size(axis_name)
    copies = jnp.broadcast_to(x[None], (count,) + x.shape)
    received = jnp.moveaxis(lax.all_to_all(copies, axis_name, 0, 0, tiled=True), 0, dim)
    return received.reshape(x.shape[:dim] + (count * x.shape[dim],) + x.shape[dim + 1 :])


def insert_kernel(start_ref, weight_ref, value_ref, out_ref):
    lines = out_ref.shape[0]
    rows = value_ref.shape[0]
    chunk = 512
    first_slot = pl.program_id(0) * lines
    slot = first_slot + lax.broadcasted_iota(jnp.int32, (lines, chunk), 0)
    total = jnp.zeros(out_ref.shape, jnp.float32)
    for part in range(rows // chunk):
        cols = pl.ds(part * chunk, chunk)
        start = start_ref[:, cols]
        weight = weight_ref[:, cols]
        spread = jnp.where(slot == start, weight, jnp.where(slot == start + 1, 1.0 - weight, 0.0))
        high = spread.astype(jnp.bfloat16)
        low = (spread - high.astype(jnp.float32)).astype(jnp.bfloat16)
        block = value_ref[cols, :]
        total += jnp.dot(high, block, preferred_element_type=jnp.float32)
        total += jnp.dot(low, block, preferred_element_type=jnp.float32)
    out_ref[...] = total


def insert_rows(values, start, weight, planes_here):
    rows, width = values.shape
    return pl.pallas_call(
        insert_kernel,
        grid=(planes_here,),
        in_specs=[
            pl.BlockSpec((1, rows), lambda q: (0, 0)),
            pl.BlockSpec((1, rows), lambda q: (0, 0)),
            pl.BlockSpec((rows, width), lambda q: (0, 0)),
        ],
        out_specs=pl.BlockSpec((ROWS, width), lambda q: (q, 0)),
        out_shape=jax.ShapeDtypeStruct((planes_here * ROWS, width), jnp.float32),
        compiler_params=pltpu.CompilerParams(vmem_limit_bytes=48 * 1024 * 1024),
        cost_estimate=pl.CostEstimate(
            flops=4 * planes_here * ROWS * rows * width,
            bytes_accessed=rows * width * 2 + planes_here * ROWS * width * 4,
            transcendentals=0,
        ),
    )(start.reshape(1, rows), weight.reshape(1, rows), values)


def extract_kernel(start_ref, weight_ref, high_ref, middle_ref, low_ref, out_ref):
    rows = out_ref.shape[1]
    slots = high_ref.shape[0]
    chunk = 512
    start = start_ref[...]
    total = jnp.zeros((rows, high_ref.shape[1]), jnp.float32)
    for part in range(slots // chunk):
        slot = part * chunk + lax.broadcasted_iota(jnp.int32, (rows, chunk), 1)
        pick = (slot == start).astype(jnp.bfloat16)
        cols = pl.ds(part * chunk, chunk)
        for piece_ref in (high_ref, middle_ref, low_ref):
            total += jnp.dot(pick, piece_ref[cols, :], preferred_element_type=jnp.float32)
    weight = weight_ref[...]
    for j in range(2):
        lower = total[:, j * COLS : (j + 1) * COLS]
        upper = total[:, (2 + j) * COLS : (3 + j) * COLS]
        out_ref[j] = (weight * lower + (1.0 - weight) * upper).astype(out_ref.dtype)


def extract_share(volume, start, weight):
    slots = volume.shape[1] * ROWS
    flat = volume.reshape(2, slots, COLS)
    following = jnp.concatenate([flat[:, 1:], jnp.zeros_like(flat[:, :1])], axis=1)
    pairs = jnp.concatenate([flat, following], axis=0).transpose(1, 0, 2).reshape(slots, 4 * COLS)
    high = lax.reduce_precision(pairs, exponent_bits=8, mantissa_bits=7)
    rest = pairs - high
    middle = lax.reduce_precision(rest, exponent_bits=8, mantissa_bits=7)
    low = rest - middle
    high, middle, low = (x.astype(jnp.bfloat16) for x in (high, middle, low))
    rows = start.size
    return pl.pallas_call(
        extract_kernel,
        grid=(rows // ROWS,),
        in_specs=[
            pl.BlockSpec((ROWS, 1), lambda q: (q, 0)),
            pl.BlockSpec((ROWS, 1), lambda q: (q, 0)),
            pl.BlockSpec((slots, 4 * COLS), lambda q: (0, 0)),
            pl.BlockSpec((slots, 4 * COLS), lambda q: (0, 0)),
            pl.BlockSpec((slots, 4 * COLS), lambda q: (0, 0)),
        ],
        out_specs=pl.BlockSpec((2, ROWS, COLS), lambda q: (0, q, 0)),
        out_shape=jax.ShapeDtypeStruct((2, rows, COLS), jnp.bfloat16),
        compiler_params=pltpu.CompilerParams(vmem_limit_bytes=48 * 1024 * 1024),
        cost_estimate=pl.CostEstimate(
            flops=24 * rows * slots * COLS,
            bytes_accessed=3 * slots * 4 * COLS * 2 + 2 * rows * COLS * 2,
            transcendentals=0,
        ),
    )(start.reshape(rows, 1), weight.reshape(rows, 1), high, middle, low)


def two_stage_sum(x, dim):
    chips = lax.axis_size("ix")
    cores = lax.axis_size("ic")
    shape = x.shape
    split = x.reshape(shape[:dim] + (chips, cores, shape[dim] // (chips * cores)) + shape[dim + 1 :])
    within = scatter_sum(split, "ic", dim + 1)
    across = scatter_sum(within, "ix", dim)
    return across.reshape(shape[:dim] + (shape[dim] // (chips * cores),) + shape[dim + 1 :])


def body(
    images,
    defocus,
    candidates,
    counts,
    noise_weight,
    volume,
    row_plane,
    row_line,
    row_weight,
    regularizer,
):
    local_rows = noise_weight.shape[0]
    slab_id = lax.axis_index("vol")
    global_rows = slab_id * local_rows + jnp.arange(local_rows)
    row_freq = (global_rows.astype(jnp.float32) - ROWS // 2) / ROWS
    col_freq = jnp.arange(COLS).astype(jnp.float32) / (2 * COLS)
    img_count = lax.axis_size("ix") * lax.axis_size("ic")
    group_id = lax.axis_index("ix") * lax.axis_size("ic") + lax.axis_index("ic")
    share = K // img_count
    first = group_id * share
    plane_share = lax.dynamic_slice_in_dim(row_plane, first, share, 0)
    line_share = lax.dynamic_slice_in_dim(row_line, first, share, 0)
    weight_share = lax.dynamic_slice_in_dim(row_weight, first, share, 0)
    planes_here = volume.shape[1]
    local_plane = plane_share - slab_id * planes_here
    in_slab = (local_plane >= 0) & (local_plane < planes_here)
    start = jnp.where(in_slab, local_plane * ROWS + line_share, -2)
    masked = extract_share(volume, start.reshape(-1), weight_share.reshape(-1))
    own_rows = scatter_sum(masked.reshape(2, share, ROWS, COLS), "vol", 2)
    slices = gather_all(own_rows, ("ix", "ic"), 1)
    cosine, sine = shift_phases(row_freq, col_freq, TRANS)
    shifted, power = make_references(slices, cosine, sine)
    contrast = contrast_of(defocus, row_freq, col_freq)
    weighted = ((contrast * noise_weight)[None] * images).astype(jnp.bfloat16)
    squared = (contrast * contrast * noise_weight).astype(jnp.bfloat16)
    cross = jnp.einsum("jbrc,tkjrc->btk", weighted, shifted, preferred_element_type=jnp.float32)
    quadratic = jnp.einsum("brc,krc->bk", squared, power, preferred_element_type=jnp.float32)
    partial_logits = cross - 0.5 * quadratic[:, None, :]
    orientation = jnp.arange(K, dtype=jnp.int32)
    pick = candidates[:, :, None] == orientation[None, None, :]
    chosen = jnp.sum(
        jnp.where(pick[:, None, :, :], partial_logits[:, :, None, :], 0.0), axis=3
    )
    logits = gather_all(scatter_sum(chosen, "vol", 0), "vol", 0)
    listed = posterior_of(logits, counts)
    weights = jnp.sum(
        jnp.where(pick[:, None, :, :], listed[:, :, :, None], jnp.zeros((), jnp.bfloat16)),
        axis=2,
    )
    y_part = jnp.einsum("btk,jbrc->tkrjc", weights, weighted, preferred_element_type=jnp.float32)
    d_part = jnp.einsum("btk,brc->tkrc", weights, squared, preferred_element_type=jnp.float32)
    num_re = jnp.sum(
        cosine[:, None] * y_part[:, :, :, 0] + sine[:, None] * y_part[:, :, :, 1], axis=0
    )
    num_im = jnp.sum(
        cosine[:, None] * y_part[:, :, :, 1] - sine[:, None] * y_part[:, :, :, 0], axis=0
    )
    stacked = jnp.stack([num_re, num_im, jnp.sum(d_part, axis=0)], axis=2)
    partial_value = two_stage_sum(stacked, 0)
    piece = gather_all(partial_value.astype(jnp.bfloat16), "vol", 1)
    inserted = insert_rows(
        piece.reshape(share * ROWS, 3 * COLS), start.reshape(-1), weight_share.reshape(-1), planes_here
    )
    slab = inserted.reshape(planes_here, ROWS, 3, COLS)
    summed = two_stage_sum(slab, 1)
    denom = summed[:, :, 2] + regularizer
    return jnp.stack([summed[:, :, 0] / denom, summed[:, :, 1] / denom], axis=0)


def solution(mesh):
    chips = dict(zip(mesh.axis_names, mesh.devices.shape))["img"] // 2
    return jax.shard_map(
        body,
        mesh=Mesh(mesh.devices.reshape(chips, -1, mesh.devices.shape[1]), ("ix", "ic", "vol")),
        in_specs=(
            P(None, ("ix", "ic"), "vol", None),
            P(("ix", "ic")),
            P(("ix", "ic"), None),
            P(("ix", "ic")),
            P("vol", None),
            P(None, "vol", None, None),
            P(),
            P(),
            P(),
            P("vol", ("ix", "ic"), None),
        ),
        out_specs=P(None, "vol", ("ix", "ic"), None),
        check_vma=False,
    )
```

```python
import math

import jax
import jax.numpy as jnp
from jax import lax
from jax.experimental import pallas as pl
from jax.experimental.pallas import tpu as pltpu
from jax.sharding import Mesh, PartitionSpec as P

ROWS = 256
COLS = 128
K = 64
TRANS = 4


AMPLITUDE = 0.1


def contrast_of(defocus, row_freq, col_freq):
    radius_sq = row_freq[:, None] * row_freq[:, None] + col_freq[None, :] * col_freq[None, :]
    angle = defocus[:, None, None] * radius_sq[None]
    return -(math.sqrt(1.0 - AMPLITUDE * AMPLITUDE) * jnp.sin(angle) + AMPLITUDE * jnp.cos(angle))


def shift_phases(row_freq, col_freq, number):
    shift_ids = jnp.arange(number)
    shift_x = (shift_ids % 2).astype(jnp.float32) - 0.5
    shift_y = (shift_ids // 2).astype(jnp.float32) - 0.5
    angle = (
        -2.0
        * math.pi
        * (
            shift_x[:, None, None] * col_freq[None, None, :]
            + shift_y[:, None, None] * row_freq[None, :, None]
        )
    )
    return (jnp.cos(angle), jnp.sin(angle))


def make_references(slices, cosine, sine):
    real_part = slices[0].astype(jnp.float32)
    imag_part = slices[1].astype(jnp.float32)
    shift_re = cosine[:, None] * real_part[None] - sine[:, None] * imag_part[None]
    shift_im = sine[:, None] * real_part[None] + cosine[:, None] * imag_part[None]
    shifted = jnp.stack([shift_re, shift_im], axis=2).astype(jnp.bfloat16)
    power = (real_part * real_part + imag_part * imag_part).astype(jnp.bfloat16)
    return (shifted, power)


def posterior_of(logits, counts):
    allowed = (jnp.arange(logits.shape[2])[None, :] < counts[:, None])[:, None, :]
    masked = jnp.where(allowed, logits, -1e30)
    highest = jnp.max(masked, axis=(1, 2), keepdims=True)
    exponent = jnp.where(allowed, jnp.exp(masked - highest), 0.0)
    return (exponent / jnp.sum(exponent, axis=(1, 2), keepdims=True)).astype(jnp.bfloat16)


def extract_rows(volume, plane_part, line_part, weight_part, slab_id):
    planes_here = volume.shape[1]
    flat = volume.reshape(2, planes_here * ROWS, COLS)
    local_plane = plane_part - slab_id * planes_here
    owned = (local_plane >= 0) & (local_plane < planes_here)
    line_index = jnp.clip(local_plane, 0, planes_here - 1) * ROWS + line_part
    lower = jnp.take(flat, line_index, axis=1)
    upper = jnp.take(flat, line_index + 1, axis=1)
    weight = weight_part[None, :, :, None]
    values = weight * lower + (1.0 - weight) * upper
    rounded = jnp.where(owned[None, :, :, None], values, 0.0).astype(jnp.bfloat16)
    return lax.optimization_barrier(rounded).astype(jnp.float32)


def insert_into(
    carry, piece, planes_all, lines_all, weights_all, slab_id, planes_here, line_first, line_count
):
    orient_count = piece.shape[0]
    number = piece.shape[1]
    local_plane = planes_all - slab_id * planes_here
    local_line = lines_all - line_first
    in_slab = (local_plane >= 0) & (local_plane < planes_here)
    lower_ok = in_slab & (local_line >= 0) & (local_line < line_count)
    upper_ok = in_slab & (local_line + 1 >= 0) & (local_line + 1 < line_count)
    dump_row = planes_here * line_count
    lower_index = jnp.where(lower_ok, local_plane * line_count + local_line, dump_row).reshape(-1)
    upper_index = jnp.where(upper_ok, local_plane * line_count + local_line + 1, dump_row).reshape(
        -1
    )
    values = piece.reshape(orient_count * number, 3 * COLS)
    weight = weights_all.reshape(-1, 1)
    carry = carry.at[lower_index].add(weight * values)
    return carry.at[upper_index].add((1.0 - weight) * values)


def scatter_sum(x, axis_name, dim):
    count = lax.axis_size(axis_name)
    shape = x.shape
    split = x.reshape(shape[:dim] + (count, shape[dim] // count) + shape[dim + 1 :])
    received = lax.all_to_all(split, axis_name, dim, dim, tiled=True)
    return jnp.sum(received, axis=dim)


def gather_all(x, axis_name, dim):
    count = lax.axis_size(axis_name)
    copies = jnp.broadcast_to(x[None], (count,) + x.shape)
    received = jnp.moveaxis(lax.all_to_all(copies, axis_name, 0, 0, tiled=True), 0, dim)
    return received.reshape(x.shape[:dim] + (count * x.shape[dim],) + x.shape[dim + 1 :])


def insert_kernel(start_ref, weight_ref, value_ref, out_ref):
    lines = out_ref.shape[0]
    rows = value_ref.shape[0]
    chunk = 512
    first_slot = pl.program_id(0) * lines
    slot = first_slot + lax.broadcasted_iota(jnp.int32, (lines, chunk), 0)
    total = jnp.zeros(out_ref.shape, jnp.float32)
    for part in range(rows // chunk):
        cols = pl.ds(part * chunk, chunk)
        start = start_ref[:, cols]
        weight = weight_ref[:, cols]
        spread = jnp.where(slot == start, weight, jnp.where(slot == start + 1, 1.0 - weight, 0.0))
        high = spread.astype(jnp.bfloat16)
        low = (spread - high.astype(jnp.float32)).astype(jnp.bfloat16)
        block = value_ref[cols, :]
        total += jnp.dot(high, block, preferred_element_type=jnp.float32)
        total += jnp.dot(low, block, preferred_element_type=jnp.float32)
    out_ref[...] = total


def insert_rows(values, start, weight, planes_here):
    rows, width = values.shape
    return pl.pallas_call(
        insert_kernel,
        grid=(planes_here,),
        in_specs=[
            pl.BlockSpec((1, rows), lambda q: (0, 0)),
            pl.BlockSpec((1, rows), lambda q: (0, 0)),
            pl.BlockSpec((rows, width), lambda q: (0, 0)),
        ],
        out_specs=pl.BlockSpec((ROWS, width), lambda q: (q, 0)),
        out_shape=jax.ShapeDtypeStruct((planes_here * ROWS, width), jnp.float32),
        compiler_params=pltpu.CompilerParams(vmem_limit_bytes=48 * 1024 * 1024),
        cost_estimate=pl.CostEstimate(
            flops=4 * planes_here * ROWS * rows * width,
            bytes_accessed=rows * width * 2 + planes_here * ROWS * width * 4,
            transcendentals=0,
        ),
    )(start.reshape(1, rows), weight.reshape(1, rows), values)


def extract_kernel(start_ref, weight_ref, high_ref, middle_ref, low_ref, out_ref):
    rows = out_ref.shape[1]
    slots = high_ref.shape[0]
    chunk = 512
    start = start_ref[...]
    total = jnp.zeros((rows, high_ref.shape[1]), jnp.float32)
    for part in range(slots // chunk):
        slot = part * chunk + lax.broadcasted_iota(jnp.int32, (rows, chunk), 1)
        pick = (slot == start).astype(jnp.bfloat16)
        cols = pl.ds(part * chunk, chunk)
        for piece_ref in (high_ref, middle_ref, low_ref):
            total += jnp.dot(pick, piece_ref[cols, :], preferred_element_type=jnp.float32)
    weight = weight_ref[...]
    for j in range(2):
        lower = total[:, j * COLS : (j + 1) * COLS]
        upper = total[:, (2 + j) * COLS : (3 + j) * COLS]
        out_ref[j] = (weight * lower + (1.0 - weight) * upper).astype(out_ref.dtype)


def extract_share(volume, start, weight):
    slots = volume.shape[1] * ROWS
    flat = volume.reshape(2, slots, COLS)
    following = jnp.concatenate([flat[:, 1:], jnp.zeros_like(flat[:, :1])], axis=1)
    pairs = jnp.concatenate([flat, following], axis=0).transpose(1, 0, 2).reshape(slots, 4 * COLS)
    high = lax.reduce_precision(pairs, exponent_bits=8, mantissa_bits=7)
    rest = pairs - high
    middle = lax.reduce_precision(rest, exponent_bits=8, mantissa_bits=7)
    low = rest - middle
    high, middle, low = (x.astype(jnp.bfloat16) for x in (high, middle, low))
    rows = start.size
    return pl.pallas_call(
        extract_kernel,
        grid=(rows // ROWS,),
        in_specs=[
            pl.BlockSpec((ROWS, 1), lambda q: (q, 0)),
            pl.BlockSpec((ROWS, 1), lambda q: (q, 0)),
            pl.BlockSpec((slots, 4 * COLS), lambda q: (0, 0)),
            pl.BlockSpec((slots, 4 * COLS), lambda q: (0, 0)),
            pl.BlockSpec((slots, 4 * COLS), lambda q: (0, 0)),
        ],
        out_specs=pl.BlockSpec((2, ROWS, COLS), lambda q: (0, q, 0)),
        out_shape=jax.ShapeDtypeStruct((2, rows, COLS), jnp.bfloat16),
        compiler_params=pltpu.CompilerParams(vmem_limit_bytes=48 * 1024 * 1024),
        cost_estimate=pl.CostEstimate(
            flops=24 * rows * slots * COLS,
            bytes_accessed=3 * slots * 4 * COLS * 2 + 2 * rows * COLS * 2,
            transcendentals=0,
        ),
    )(start.reshape(rows, 1), weight.reshape(rows, 1), high, middle, low)


def staged_sum(x, dim, outer, inner, outer_first):
    outer_count = lax.axis_size(outer)
    inner_count = lax.axis_size(inner)
    shape = x.shape
    block = shape[dim] // (outer_count * inner_count)
    split = x.reshape(shape[:dim] + (outer_count, inner_count, block) + shape[dim + 1 :])
    if outer_first:
        split = scatter_sum(scatter_sum(split, outer, dim), inner, dim + 1)
    else:
        split = scatter_sum(scatter_sum(split, inner, dim + 1), outer, dim)
    return split.reshape(shape[:dim] + (block,) + shape[dim + 1 :])


def body(
    images,
    defocus,
    candidates,
    counts,
    noise_weight,
    volume,
    row_plane,
    row_line,
    row_weight,
    regularizer,
):
    local_rows = noise_weight.shape[0]
    slab_id = lax.axis_index("vy") * lax.axis_size("vz") + lax.axis_index("vz")
    global_rows = slab_id * local_rows + jnp.arange(local_rows)
    row_freq = (global_rows.astype(jnp.float32) - ROWS // 2) / ROWS
    col_freq = jnp.arange(COLS).astype(jnp.float32) / (2 * COLS)
    img_count = lax.axis_size("ix") * lax.axis_size("ic")
    group_id = lax.axis_index("ix") * lax.axis_size("ic") + lax.axis_index("ic")
    share = K // img_count
    first = group_id * share
    plane_share = lax.dynamic_slice_in_dim(row_plane, first, share, 0)
    line_share = lax.dynamic_slice_in_dim(row_line, first, share, 0)
    weight_share = lax.dynamic_slice_in_dim(row_weight, first, share, 0)
    planes_here = volume.shape[1]
    local_plane = plane_share - slab_id * planes_here
    in_slab = (local_plane >= 0) & (local_plane < planes_here)
    start = jnp.where(in_slab, local_plane * ROWS + line_share, -2)
    masked = extract_share(volume, start.reshape(-1), weight_share.reshape(-1))
    own_rows = staged_sum(masked.reshape(2, share, ROWS, COLS), 2, "vy", "vz", True)
    slices = gather_all(own_rows, ("ix", "ic"), 1)
    cosine, sine = shift_phases(row_freq, col_freq, TRANS)
    shifted, power = make_references(slices, cosine, sine)
    contrast = contrast_of(defocus, row_freq, col_freq)
    weighted = ((contrast * noise_weight)[None] * images).astype(jnp.bfloat16)
    squared = (contrast * contrast * noise_weight).astype(jnp.bfloat16)
    cross = jnp.einsum("jbrc,tkjrc->btk", weighted, shifted, preferred_element_type=jnp.float32)
    quadratic = jnp.einsum("brc,krc->bk", squared, power, preferred_element_type=jnp.float32)
    partial_logits = cross - 0.5 * quadratic[:, None, :]
    orientation = jnp.arange(K, dtype=jnp.int32)
    pick = candidates[:, :, None] == orientation[None, None, :]
    chosen = jnp.sum(
        jnp.where(pick[:, None, :, :], partial_logits[:, :, None, :], 0.0), axis=3
    )
    logits = gather_all(scatter_sum(chosen, ("vy", "vz"), 0), ("vy", "vz"), 0)
    listed = posterior_of(logits, counts)
    weights = jnp.sum(
        jnp.where(pick[:, None, :, :], listed[:, :, :, None], jnp.zeros((), jnp.bfloat16)),
        axis=2,
    )
    y_part = jnp.einsum("btk,jbrc->tkrjc", weights, weighted, preferred_element_type=jnp.float32)
    d_part = jnp.einsum("btk,brc->tkrc", weights, squared, preferred_element_type=jnp.float32)
    num_re = jnp.sum(
        cosine[:, None] * y_part[:, :, :, 0] + sine[:, None] * y_part[:, :, :, 1], axis=0
    )
    num_im = jnp.sum(
        cosine[:, None] * y_part[:, :, :, 1] - sine[:, None] * y_part[:, :, :, 0], axis=0
    )
    stacked = jnp.stack([num_re, num_im, jnp.sum(d_part, axis=0)], axis=2)
    partial_value = staged_sum(stacked, 0, "ix", "ic", False)
    piece = gather_all(gather_all(partial_value.astype(jnp.bfloat16), "vz", 1), "vy", 1)
    inserted = insert_rows(
        piece.reshape(share * ROWS, 3 * COLS), start.reshape(-1), weight_share.reshape(-1), planes_here
    )
    slab = inserted.reshape(planes_here, ROWS, 3, COLS)
    summed = staged_sum(slab, 1, "ix", "ic", False)
    denom = summed[:, :, 2] + regularizer
    return jnp.stack([summed[:, :, 0] / denom, summed[:, :, 1] / denom], axis=0)


def solution(mesh):
    chips = dict(zip(mesh.axis_names, mesh.devices.shape))["img"] // 2
    rings = mesh.devices.shape[1] // 8
    return jax.shard_map(
        body,
        mesh=Mesh(mesh.devices.reshape(chips, -1, rings, mesh.devices.shape[1] // rings), ("ix", "ic", "vy", "vz")),
        in_specs=(
            P(None, ("ix", "ic"), ("vy", "vz"), None),
            P(("ix", "ic")),
            P(("ix", "ic"), None),
            P(("ix", "ic")),
            P(("vy", "vz"), None),
            P(None, ("vy", "vz"), None, None),
            P(),
            P(),
            P(),
            P(("vy", "vz"), ("ix", "ic"), None),
        ),
        out_specs=P(None, ("vy", "vz"), ("ix", "ic"), None),
        check_vma=False,
    )
```

```python
import math

import jax
import jax.numpy as jnp
from jax import lax
from jax.experimental import pallas as pl
from jax.experimental.pallas import tpu as pltpu
from jax.sharding import Mesh, PartitionSpec as P

ROWS = 256
COLS = 128
K = 64
TRANS = 4


AMPLITUDE = 0.1


def contrast_of(defocus, row_freq, col_freq):
    radius_sq = row_freq[:, None] * row_freq[:, None] + col_freq[None, :] * col_freq[None, :]
    angle = defocus[:, None, None] * radius_sq[None]
    return -(math.sqrt(1.0 - AMPLITUDE * AMPLITUDE) * jnp.sin(angle) + AMPLITUDE * jnp.cos(angle))


def shift_phases(row_freq, col_freq, number):
    shift_ids = jnp.arange(number)
    shift_x = (shift_ids % 2).astype(jnp.float32) - 0.5
    shift_y = (shift_ids // 2).astype(jnp.float32) - 0.5
    angle = (
        -2.0
        * math.pi
        * (
            shift_x[:, None, None] * col_freq[None, None, :]
            + shift_y[:, None, None] * row_freq[None, :, None]
        )
    )
    return (jnp.cos(angle), jnp.sin(angle))


def make_references(slices, cosine, sine):
    real_part = slices[0].astype(jnp.float32)
    imag_part = slices[1].astype(jnp.float32)
    shift_re = cosine[:, None] * real_part[None] - sine[:, None] * imag_part[None]
    shift_im = sine[:, None] * real_part[None] + cosine[:, None] * imag_part[None]
    shifted = jnp.stack([shift_re, shift_im], axis=2).astype(jnp.bfloat16)
    power = (real_part * real_part + imag_part * imag_part).astype(jnp.bfloat16)
    return (shifted, power)


def posterior_of(logits, counts):
    allowed = (jnp.arange(logits.shape[2])[None, :] < counts[:, None])[:, None, :]
    masked = jnp.where(allowed, logits, -1e30)
    highest = jnp.max(masked, axis=(1, 2), keepdims=True)
    exponent = jnp.where(allowed, jnp.exp(masked - highest), 0.0)
    return (exponent / jnp.sum(exponent, axis=(1, 2), keepdims=True)).astype(jnp.bfloat16)


def extract_rows(volume, plane_part, line_part, weight_part, slab_id):
    planes_here = volume.shape[1]
    flat = volume.reshape(2, planes_here * ROWS, COLS)
    local_plane = plane_part - slab_id * planes_here
    owned = (local_plane >= 0) & (local_plane < planes_here)
    line_index = jnp.clip(local_plane, 0, planes_here - 1) * ROWS + line_part
    lower = jnp.take(flat, line_index, axis=1)
    upper = jnp.take(flat, line_index + 1, axis=1)
    weight = weight_part[None, :, :, None]
    values = weight * lower + (1.0 - weight) * upper
    rounded = jnp.where(owned[None, :, :, None], values, 0.0).astype(jnp.bfloat16)
    return lax.optimization_barrier(rounded).astype(jnp.float32)


def insert_into(
    carry, piece, planes_all, lines_all, weights_all, slab_id, planes_here, line_first, line_count
):
    orient_count = piece.shape[0]
    number = piece.shape[1]
    local_plane = planes_all - slab_id * planes_here
    local_line = lines_all - line_first
    in_slab = (local_plane >= 0) & (local_plane < planes_here)
    lower_ok = in_slab & (local_line >= 0) & (local_line < line_count)
    upper_ok = in_slab & (local_line + 1 >= 0) & (local_line + 1 < line_count)
    dump_row = planes_here * line_count
    lower_index = jnp.where(lower_ok, local_plane * line_count + local_line, dump_row).reshape(-1)
    upper_index = jnp.where(upper_ok, local_plane * line_count + local_line + 1, dump_row).reshape(
        -1
    )
    values = piece.reshape(orient_count * number, 3 * COLS)
    weight = weights_all.reshape(-1, 1)
    carry = carry.at[lower_index].add(weight * values)
    return carry.at[upper_index].add((1.0 - weight) * values)


def scatter_sum(x, axis_name, dim):
    count = lax.axis_size(axis_name)
    shape = x.shape
    split = x.reshape(shape[:dim] + (count, shape[dim] // count) + shape[dim + 1 :])
    received = lax.all_to_all(split, axis_name, dim, dim, tiled=True)
    return jnp.sum(received, axis=dim)


def gather_all(x, axis_name, dim):
    count = lax.axis_size(axis_name)
    copies = jnp.broadcast_to(x[None], (count,) + x.shape)
    received = jnp.moveaxis(lax.all_to_all(copies, axis_name, 0, 0, tiled=True), 0, dim)
    return received.reshape(x.shape[:dim] + (count * x.shape[dim],) + x.shape[dim + 1 :])


def insert_kernel(start_ref, weight_ref, value_ref, out_ref):
    lines = out_ref.shape[0]
    rows = value_ref.shape[0]
    chunk = 512
    first_slot = pl.program_id(0) * lines
    slot = first_slot + lax.broadcasted_iota(jnp.int32, (lines, chunk), 0)
    total = jnp.zeros(out_ref.shape, jnp.float32)
    for part in range(rows // chunk):
        cols = pl.ds(part * chunk, chunk)
        start = start_ref[:, cols]
        weight = weight_ref[:, cols]
        spread = jnp.where(slot == start, weight, jnp.where(slot == start + 1, 1.0 - weight, 0.0))
        high = spread.astype(jnp.bfloat16)
        low = (spread - high.astype(jnp.float32)).astype(jnp.bfloat16)
        block = value_ref[cols, :]
        total += jnp.dot(high, block, preferred_element_type=jnp.float32)
        total += jnp.dot(low, block, preferred_element_type=jnp.float32)
    out_ref[...] = total


def insert_rows(values, start, weight, planes_here):
    rows, width = values.shape
    return pl.pallas_call(
        insert_kernel,
        grid=(planes_here,),
        in_specs=[
            pl.BlockSpec((1, rows), lambda q: (0, 0)),
            pl.BlockSpec((1, rows), lambda q: (0, 0)),
            pl.BlockSpec((rows, width), lambda q: (0, 0)),
        ],
        out_specs=pl.BlockSpec((ROWS, width), lambda q: (q, 0)),
        out_shape=jax.ShapeDtypeStruct((planes_here * ROWS, width), jnp.float32),
        compiler_params=pltpu.CompilerParams(vmem_limit_bytes=48 * 1024 * 1024),
        cost_estimate=pl.CostEstimate(
            flops=4 * planes_here * ROWS * rows * width,
            bytes_accessed=rows * width * 2 + planes_here * ROWS * width * 4,
            transcendentals=0,
        ),
    )(start.reshape(1, rows), weight.reshape(1, rows), values)


def extract_kernel(start_ref, weight_ref, high_ref, middle_ref, low_ref, out_ref):
    rows = out_ref.shape[1]
    slots = high_ref.shape[0]
    chunk = 512
    start = start_ref[...]
    total = jnp.zeros((rows, high_ref.shape[1]), jnp.float32)
    for part in range(slots // chunk):
        slot = part * chunk + lax.broadcasted_iota(jnp.int32, (rows, chunk), 1)
        pick = (slot == start).astype(jnp.bfloat16)
        cols = pl.ds(part * chunk, chunk)
        for piece_ref in (high_ref, middle_ref, low_ref):
            total += jnp.dot(pick, piece_ref[cols, :], preferred_element_type=jnp.float32)
    weight = weight_ref[...]
    for j in range(2):
        lower = total[:, j * COLS : (j + 1) * COLS]
        upper = total[:, (2 + j) * COLS : (3 + j) * COLS]
        out_ref[j] = (weight * lower + (1.0 - weight) * upper).astype(out_ref.dtype)


def extract_share(volume, start, weight):
    slots = volume.shape[1] * ROWS
    flat = volume.reshape(2, slots, COLS)
    following = jnp.concatenate([flat[:, 1:], jnp.zeros_like(flat[:, :1])], axis=1)
    pairs = jnp.concatenate([flat, following], axis=0).transpose(1, 0, 2).reshape(slots, 4 * COLS)
    high = lax.reduce_precision(pairs, exponent_bits=8, mantissa_bits=7)
    rest = pairs - high
    middle = lax.reduce_precision(rest, exponent_bits=8, mantissa_bits=7)
    low = rest - middle
    high, middle, low = (x.astype(jnp.bfloat16) for x in (high, middle, low))
    rows = start.size
    return pl.pallas_call(
        extract_kernel,
        grid=(rows // ROWS,),
        in_specs=[
            pl.BlockSpec((ROWS, 1), lambda q: (q, 0)),
            pl.BlockSpec((ROWS, 1), lambda q: (q, 0)),
            pl.BlockSpec((slots, 4 * COLS), lambda q: (0, 0)),
            pl.BlockSpec((slots, 4 * COLS), lambda q: (0, 0)),
            pl.BlockSpec((slots, 4 * COLS), lambda q: (0, 0)),
        ],
        out_specs=pl.BlockSpec((2, ROWS, COLS), lambda q: (0, q, 0)),
        out_shape=jax.ShapeDtypeStruct((2, rows, COLS), jnp.bfloat16),
        compiler_params=pltpu.CompilerParams(vmem_limit_bytes=48 * 1024 * 1024),
        cost_estimate=pl.CostEstimate(
            flops=24 * rows * slots * COLS,
            bytes_accessed=3 * slots * 4 * COLS * 2 + 2 * rows * COLS * 2,
            transcendentals=0,
        ),
    )(start.reshape(rows, 1), weight.reshape(rows, 1), high, middle, low)


def staged_sum(x, dim, outer, inner, outer_first):
    outer_count = lax.axis_size(outer)
    inner_count = lax.axis_size(inner)
    shape = x.shape
    block = shape[dim] // (outer_count * inner_count)
    split = x.reshape(shape[:dim] + (outer_count, inner_count, block) + shape[dim + 1 :])
    if outer_first:
        split = scatter_sum(scatter_sum(split, outer, dim), inner, dim + 1)
    else:
        split = scatter_sum(scatter_sum(split, inner, dim + 1), outer, dim)
    return split.reshape(shape[:dim] + (block,) + shape[dim + 1 :])


def body(
    images,
    defocus,
    candidates,
    counts,
    noise_weight,
    volume,
    row_plane,
    row_line,
    row_weight,
    regularizer,
):
    local_rows = noise_weight.shape[0]
    slab_id = lax.axis_index("vy") * lax.axis_size("vz") + lax.axis_index("vz")
    global_rows = slab_id * local_rows + jnp.arange(local_rows)
    row_freq = (global_rows.astype(jnp.float32) - ROWS // 2) / ROWS
    col_freq = jnp.arange(COLS).astype(jnp.float32) / (2 * COLS)
    img_count = lax.axis_size("ix") * lax.axis_size("ic")
    group_id = lax.axis_index("ix") * lax.axis_size("ic") + lax.axis_index("ic")
    share = K // img_count
    first = group_id * share
    plane_share = lax.dynamic_slice_in_dim(row_plane, first, share, 0)
    line_share = lax.dynamic_slice_in_dim(row_line, first, share, 0)
    weight_share = lax.dynamic_slice_in_dim(row_weight, first, share, 0)
    planes_here = volume.shape[1]
    local_plane = plane_share - slab_id * planes_here
    in_slab = (local_plane >= 0) & (local_plane < planes_here)
    start = jnp.where(in_slab, local_plane * ROWS + line_share, -2)
    masked = extract_share(volume, start.reshape(-1), weight_share.reshape(-1))
    own_rows = staged_sum(masked.reshape(2, share, ROWS, COLS), 2, "vy", "vz", True)
    slices = gather_all(own_rows, ("ix", "ic"), 1)
    cosine, sine = shift_phases(row_freq, col_freq, TRANS)
    shifted, power = make_references(slices, cosine, sine)
    contrast = contrast_of(defocus, row_freq, col_freq)
    weighted = ((contrast * noise_weight)[None] * images).astype(jnp.bfloat16)
    squared = (contrast * contrast * noise_weight).astype(jnp.bfloat16)
    cross = jnp.einsum("jbrc,tkjrc->btk", weighted, shifted, preferred_element_type=jnp.float32)
    quadratic = jnp.einsum("brc,krc->bk", squared, power, preferred_element_type=jnp.float32)
    partial_logits = cross - 0.5 * quadratic[:, None, :]
    orientation = jnp.arange(K, dtype=jnp.int32)
    pick = candidates[:, :, None] == orientation[None, None, :]
    chosen = jnp.sum(
        jnp.where(pick[:, None, :, :], partial_logits[:, :, None, :], 0.0), axis=3
    )
    logits = gather_all(scatter_sum(chosen, ("vy", "vz"), 0), ("vy", "vz"), 0)
    listed = posterior_of(logits, counts)
    weights = jnp.sum(
        jnp.where(pick[:, None, :, :], listed[:, :, :, None], jnp.zeros((), jnp.bfloat16)),
        axis=2,
    )
    y_part = jnp.einsum("btk,jbrc->tkrjc", weights, weighted, preferred_element_type=jnp.float32)
    d_part = jnp.einsum("btk,brc->tkrc", weights, squared, preferred_element_type=jnp.float32)
    num_re = jnp.sum(
        cosine[:, None] * y_part[:, :, :, 0] + sine[:, None] * y_part[:, :, :, 1], axis=0
    )
    num_im = jnp.sum(
        cosine[:, None] * y_part[:, :, :, 1] - sine[:, None] * y_part[:, :, :, 0], axis=0
    )
    stacked = jnp.stack([num_re, num_im, jnp.sum(d_part, axis=0)], axis=2)
    partial_value = staged_sum(stacked, 0, "ix", "ic", False)
    piece = gather_all(gather_all(partial_value.astype(jnp.bfloat16), "vz", 1), "vy", 1)
    inserted = insert_rows(
        piece.reshape(share * ROWS, 3 * COLS), start.reshape(-1), weight_share.reshape(-1), planes_here
    )
    slab = inserted.reshape(planes_here, ROWS, 3, COLS)
    chips = lax.axis_size("ix")
    cores = lax.axis_size("ic")
    split = slab.reshape(planes_here, chips, cores, ROWS // (chips * cores), 3, COLS)
    within = scatter_sum(split, "ic", 2).astype(jnp.bfloat16)
    received = lax.all_to_all(within, "ix", 1, 1, tiled=True)
    summed = jnp.sum(received.astype(jnp.float32), axis=1).reshape(
        planes_here, ROWS // (chips * cores), 3, COLS
    )
    denom = summed[:, :, 2] + regularizer
    return jnp.stack([summed[:, :, 0] / denom, summed[:, :, 1] / denom], axis=0)


def solution(mesh):
    chips = dict(zip(mesh.axis_names, mesh.devices.shape))["img"] // 2
    rings = mesh.devices.shape[1] // 8
    return jax.shard_map(
        body,
        mesh=Mesh(mesh.devices.reshape(chips, -1, rings, mesh.devices.shape[1] // rings), ("ix", "ic", "vy", "vz")),
        in_specs=(
            P(None, ("ix", "ic"), ("vy", "vz"), None),
            P(("ix", "ic")),
            P(("ix", "ic"), None),
            P(("ix", "ic")),
            P(("vy", "vz"), None),
            P(None, ("vy", "vz"), None, None),
            P(),
            P(),
            P(),
            P(("vy", "vz"), ("ix", "ic"), None),
        ),
        out_specs=P(None, ("vy", "vz"), ("ix", "ic"), None),
        check_vma=False,
    )
```

```python
import math

import jax
import jax.numpy as jnp
from jax import lax
from jax.experimental import pallas as pl
from jax.experimental.pallas import tpu as pltpu
from jax.sharding import Mesh, PartitionSpec as P

ROWS = 256
COLS = 128
K = 64
TRANS = 4


AMPLITUDE = 0.1


def contrast_of(defocus, row_freq, col_freq):
    radius_sq = row_freq[:, None] * row_freq[:, None] + col_freq[None, :] * col_freq[None, :]
    angle = defocus[:, None, None] * radius_sq[None]
    return -(math.sqrt(1.0 - AMPLITUDE * AMPLITUDE) * jnp.sin(angle) + AMPLITUDE * jnp.cos(angle))


def shift_phases(row_freq, col_freq, number):
    shift_ids = jnp.arange(number)
    shift_x = (shift_ids % 2).astype(jnp.float32) - 0.5
    shift_y = (shift_ids // 2).astype(jnp.float32) - 0.5
    angle = (
        -2.0
        * math.pi
        * (
            shift_x[:, None, None] * col_freq[None, None, :]
            + shift_y[:, None, None] * row_freq[None, :, None]
        )
    )
    return (jnp.cos(angle), jnp.sin(angle))


def make_references(slices, cosine, sine):
    real_part = slices[0].astype(jnp.float32)
    imag_part = slices[1].astype(jnp.float32)
    shift_re = cosine[:, None] * real_part[None] - sine[:, None] * imag_part[None]
    shift_im = sine[:, None] * real_part[None] + cosine[:, None] * imag_part[None]
    shifted = jnp.stack([shift_re, shift_im], axis=2).astype(jnp.bfloat16)
    power = (real_part * real_part + imag_part * imag_part).astype(jnp.bfloat16)
    return (shifted, power)


def posterior_of(logits, counts):
    allowed = (jnp.arange(logits.shape[2])[None, :] < counts[:, None])[:, None, :]
    masked = jnp.where(allowed, logits, -1e30)
    highest = jnp.max(masked, axis=(1, 2), keepdims=True)
    exponent = jnp.where(allowed, jnp.exp(masked - highest), 0.0)
    return (exponent / jnp.sum(exponent, axis=(1, 2), keepdims=True)).astype(jnp.bfloat16)


def extract_rows(volume, plane_part, line_part, weight_part, slab_id):
    planes_here = volume.shape[1]
    flat = volume.reshape(2, planes_here * ROWS, COLS)
    local_plane = plane_part - slab_id * planes_here
    owned = (local_plane >= 0) & (local_plane < planes_here)
    line_index = jnp.clip(local_plane, 0, planes_here - 1) * ROWS + line_part
    lower = jnp.take(flat, line_index, axis=1)
    upper = jnp.take(flat, line_index + 1, axis=1)
    weight = weight_part[None, :, :, None]
    values = weight * lower + (1.0 - weight) * upper
    rounded = jnp.where(owned[None, :, :, None], values, 0.0).astype(jnp.bfloat16)
    return lax.optimization_barrier(rounded).astype(jnp.float32)


def insert_into(
    carry, piece, planes_all, lines_all, weights_all, slab_id, planes_here, line_first, line_count
):
    orient_count = piece.shape[0]
    number = piece.shape[1]
    local_plane = planes_all - slab_id * planes_here
    local_line = lines_all - line_first
    in_slab = (local_plane >= 0) & (local_plane < planes_here)
    lower_ok = in_slab & (local_line >= 0) & (local_line < line_count)
    upper_ok = in_slab & (local_line + 1 >= 0) & (local_line + 1 < line_count)
    dump_row = planes_here * line_count
    lower_index = jnp.where(lower_ok, local_plane * line_count + local_line, dump_row).reshape(-1)
    upper_index = jnp.where(upper_ok, local_plane * line_count + local_line + 1, dump_row).reshape(
        -1
    )
    values = piece.reshape(orient_count * number, 3 * COLS)
    weight = weights_all.reshape(-1, 1)
    carry = carry.at[lower_index].add(weight * values)
    return carry.at[upper_index].add((1.0 - weight) * values)


def scatter_sum(x, axis_name, dim):
    count = lax.axis_size(axis_name)
    shape = x.shape
    split = x.reshape(shape[:dim] + (count, shape[dim] // count) + shape[dim + 1 :])
    received = lax.all_to_all(split, axis_name, dim, dim, tiled=True)
    return jnp.sum(received, axis=dim)


def gather_all(x, axis_name, dim):
    count = lax.axis_size(axis_name)
    copies = jnp.broadcast_to(x[None], (count,) + x.shape)
    received = jnp.moveaxis(lax.all_to_all(copies, axis_name, 0, 0, tiled=True), 0, dim)
    return received.reshape(x.shape[:dim] + (count * x.shape[dim],) + x.shape[dim + 1 :])


def insert_kernel(start_ref, weight_ref, value_ref, out_ref):
    lines = out_ref.shape[0]
    rows = value_ref.shape[0]
    chunk = 512
    first_slot = pl.program_id(0) * lines
    slot = first_slot + lax.broadcasted_iota(jnp.int32, (lines, chunk), 0)
    total = jnp.zeros(out_ref.shape, jnp.float32)
    for part in range(rows // chunk):
        cols = pl.ds(part * chunk, chunk)
        start = start_ref[:, cols]
        weight = weight_ref[:, cols]
        spread = jnp.where(slot == start, weight, jnp.where(slot == start + 1, 1.0 - weight, 0.0))
        high = spread.astype(jnp.bfloat16)
        low = (spread - high.astype(jnp.float32)).astype(jnp.bfloat16)
        block = value_ref[cols, :]
        total += jnp.dot(high, block, preferred_element_type=jnp.float32)
        total += jnp.dot(low, block, preferred_element_type=jnp.float32)
    out_ref[...] = total


def insert_rows(values, start, weight, planes_here):
    rows, width = values.shape
    return pl.pallas_call(
        insert_kernel,
        grid=(planes_here,),
        in_specs=[
            pl.BlockSpec((1, rows), lambda q: (0, 0)),
            pl.BlockSpec((1, rows), lambda q: (0, 0)),
            pl.BlockSpec((rows, width), lambda q: (0, 0)),
        ],
        out_specs=pl.BlockSpec((ROWS, width), lambda q: (q, 0)),
        out_shape=jax.ShapeDtypeStruct((planes_here * ROWS, width), jnp.float32),
        compiler_params=pltpu.CompilerParams(vmem_limit_bytes=48 * 1024 * 1024),
        cost_estimate=pl.CostEstimate(
            flops=4 * planes_here * ROWS * rows * width,
            bytes_accessed=rows * width * 2 + planes_here * ROWS * width * 4,
            transcendentals=0,
        ),
    )(start.reshape(1, rows), weight.reshape(1, rows), values)


def extract_kernel(start_ref, weight_ref, high_ref, middle_ref, low_ref, out_ref):
    rows = out_ref.shape[1]
    slots = high_ref.shape[0]
    chunk = 512
    start = start_ref[...]
    total = jnp.zeros((rows, high_ref.shape[1]), jnp.float32)
    for part in range(slots // chunk):
        slot = part * chunk + lax.broadcasted_iota(jnp.int32, (rows, chunk), 1)
        pick = (slot == start).astype(jnp.bfloat16)
        cols = pl.ds(part * chunk, chunk)
        for piece_ref in (high_ref, middle_ref, low_ref):
            total += jnp.dot(pick, piece_ref[cols, :], preferred_element_type=jnp.float32)
    weight = weight_ref[...]
    for j in range(2):
        lower = total[:, j * COLS : (j + 1) * COLS]
        upper = total[:, (2 + j) * COLS : (3 + j) * COLS]
        out_ref[j] = (weight * lower + (1.0 - weight) * upper).astype(out_ref.dtype)


def extract_share(volume, start, weight):
    slots = volume.shape[1] * ROWS
    flat = volume.reshape(2, slots, COLS)
    following = jnp.concatenate([flat[:, 1:], jnp.zeros_like(flat[:, :1])], axis=1)
    pairs = jnp.concatenate([flat, following], axis=0).transpose(1, 0, 2).reshape(slots, 4 * COLS)
    high = lax.reduce_precision(pairs, exponent_bits=8, mantissa_bits=7)
    rest = pairs - high
    middle = lax.reduce_precision(rest, exponent_bits=8, mantissa_bits=7)
    low = rest - middle
    high, middle, low = (x.astype(jnp.bfloat16) for x in (high, middle, low))
    rows = start.size
    return pl.pallas_call(
        extract_kernel,
        grid=(rows // ROWS,),
        in_specs=[
            pl.BlockSpec((ROWS, 1), lambda q: (q, 0)),
            pl.BlockSpec((ROWS, 1), lambda q: (q, 0)),
            pl.BlockSpec((slots, 4 * COLS), lambda q: (0, 0)),
            pl.BlockSpec((slots, 4 * COLS), lambda q: (0, 0)),
            pl.BlockSpec((slots, 4 * COLS), lambda q: (0, 0)),
        ],
        out_specs=pl.BlockSpec((2, ROWS, COLS), lambda q: (0, q, 0)),
        out_shape=jax.ShapeDtypeStruct((2, rows, COLS), jnp.bfloat16),
        compiler_params=pltpu.CompilerParams(vmem_limit_bytes=48 * 1024 * 1024),
        cost_estimate=pl.CostEstimate(
            flops=24 * rows * slots * COLS,
            bytes_accessed=3 * slots * 4 * COLS * 2 + 2 * rows * COLS * 2,
            transcendentals=0,
        ),
    )(start.reshape(rows, 1), weight.reshape(rows, 1), high, middle, low)


def staged_sum(x, dim, outer, inner, outer_first):
    outer_count = lax.axis_size(outer)
    inner_count = lax.axis_size(inner)
    shape = x.shape
    block = shape[dim] // (outer_count * inner_count)
    split = x.reshape(shape[:dim] + (outer_count, inner_count, block) + shape[dim + 1 :])
    if outer_first:
        split = scatter_sum(scatter_sum(split, outer, dim), inner, dim + 1)
    else:
        split = scatter_sum(scatter_sum(split, inner, dim + 1), outer, dim)
    return split.reshape(shape[:dim] + (block,) + shape[dim + 1 :])


def body(
    images,
    defocus,
    candidates,
    counts,
    noise_weight,
    volume,
    row_plane,
    row_line,
    row_weight,
    regularizer,
):
    local_rows = noise_weight.shape[0]
    slab_id = lax.axis_index("vy") * lax.axis_size("vz") + lax.axis_index("vz")
    global_rows = slab_id * local_rows + jnp.arange(local_rows)
    row_freq = (global_rows.astype(jnp.float32) - ROWS // 2) / ROWS
    col_freq = jnp.arange(COLS).astype(jnp.float32) / (2 * COLS)
    img_count = lax.axis_size("ix") * lax.axis_size("ic")
    group_id = lax.axis_index("ix") * lax.axis_size("ic") + lax.axis_index("ic")
    share = K // img_count
    first = group_id * share
    plane_share = lax.dynamic_slice_in_dim(row_plane, first, share, 0)
    line_share = lax.dynamic_slice_in_dim(row_line, first, share, 0)
    weight_share = lax.dynamic_slice_in_dim(row_weight, first, share, 0)
    planes_here = volume.shape[1]
    local_plane = plane_share - slab_id * planes_here
    in_slab = (local_plane >= 0) & (local_plane < planes_here)
    start = jnp.where(in_slab, local_plane * ROWS + line_share, -2)
    masked = extract_share(volume, start.reshape(-1), weight_share.reshape(-1))
    own_rows = staged_sum(masked.reshape(2, share, ROWS, COLS), 2, "vy", "vz", True)
    slices = gather_all(own_rows, ("ix", "ic"), 1)
    cosine, sine = shift_phases(row_freq, col_freq, TRANS)
    shifted, power = make_references(slices, cosine, sine)
    contrast = contrast_of(defocus, row_freq, col_freq)
    weighted = ((contrast * noise_weight)[None] * images).astype(jnp.bfloat16)
    squared = (contrast * contrast * noise_weight).astype(jnp.bfloat16)
    cross = jnp.einsum("jbrc,tkjrc->btk", weighted, shifted, preferred_element_type=jnp.float32)
    quadratic = jnp.einsum("brc,krc->bk", squared, power, preferred_element_type=jnp.float32)
    partial_logits = cross - 0.5 * quadratic[:, None, :]
    orientation = jnp.arange(K, dtype=jnp.int32)
    pick = candidates[:, :, None] == orientation[None, None, :]
    chosen = jnp.sum(
        jnp.where(pick[:, None, :, :], partial_logits[:, :, None, :], 0.0), axis=3
    )
    logits = scatter_sum(chosen, ("vy", "vz"), 0)
    held = logits.shape[0]
    counts_here = lax.dynamic_slice_in_dim(counts, slab_id * held, held, 0)
    listed = gather_all(posterior_of(logits, counts_here), ("vy", "vz"), 0)
    weights = jnp.sum(
        jnp.where(pick[:, None, :, :], listed[:, :, :, None], jnp.zeros((), jnp.bfloat16)),
        axis=2,
    )
    y_part = jnp.einsum("btk,jbrc->tkrjc", weights, weighted, preferred_element_type=jnp.float32)
    d_part = jnp.einsum("btk,brc->tkrc", weights, squared, preferred_element_type=jnp.float32)
    num_re = jnp.sum(
        cosine[:, None] * y_part[:, :, :, 0] + sine[:, None] * y_part[:, :, :, 1], axis=0
    )
    num_im = jnp.sum(
        cosine[:, None] * y_part[:, :, :, 1] - sine[:, None] * y_part[:, :, :, 0], axis=0
    )
    stacked = jnp.stack([num_re, num_im, jnp.sum(d_part, axis=0)], axis=2)
    partial_value = staged_sum(stacked, 0, "ix", "ic", False)
    piece = gather_all(gather_all(partial_value.astype(jnp.bfloat16), "vz", 1), "vy", 1)
    inserted = insert_rows(
        piece.reshape(share * ROWS, 3 * COLS), start.reshape(-1), weight_share.reshape(-1), planes_here
    )
    slab = inserted.reshape(planes_here, ROWS, 3, COLS)
    chips = lax.axis_size("ix")
    cores = lax.axis_size("ic")
    split = slab.reshape(planes_here, chips, cores, ROWS // (chips * cores), 3, COLS)
    within = scatter_sum(split, "ic", 2).astype(jnp.bfloat16)
    received = lax.all_to_all(within, "ix", 1, 1, tiled=True)
    summed = jnp.sum(received.astype(jnp.float32), axis=1).reshape(
        planes_here, ROWS // (chips * cores), 3, COLS
    )
    denom = summed[:, :, 2] + regularizer
    return jnp.stack([summed[:, :, 0] / denom, summed[:, :, 1] / denom], axis=0)


def solution(mesh):
    chips = dict(zip(mesh.axis_names, mesh.devices.shape))["img"] // 2
    rings = mesh.devices.shape[1] // 8
    return jax.shard_map(
        body,
        mesh=Mesh(mesh.devices.reshape(chips, -1, rings, mesh.devices.shape[1] // rings), ("ix", "ic", "vy", "vz")),
        in_specs=(
            P(None, ("ix", "ic"), ("vy", "vz"), None),
            P(("ix", "ic")),
            P(("ix", "ic"), None),
            P(("ix", "ic")),
            P(("vy", "vz"), None),
            P(None, ("vy", "vz"), None, None),
            P(),
            P(),
            P(),
            P(("vy", "vz"), ("ix", "ic"), None),
        ),
        out_specs=P(None, ("vy", "vz"), ("ix", "ic"), None),
        check_vma=False,
    )
```

```python
import math

import jax
import jax.numpy as jnp
from jax import lax
from jax.experimental import pallas as pl
from jax.experimental.pallas import tpu as pltpu
from jax.sharding import Mesh, PartitionSpec as P

ROWS = 256
COLS = 128
K = 64
TRANS = 4


AMPLITUDE = 0.1


def contrast_of(defocus, row_freq, col_freq):
    radius_sq = row_freq[:, None] * row_freq[:, None] + col_freq[None, :] * col_freq[None, :]
    angle = defocus[:, None, None] * radius_sq[None]
    return -(math.sqrt(1.0 - AMPLITUDE * AMPLITUDE) * jnp.sin(angle) + AMPLITUDE * jnp.cos(angle))


def shift_phases(row_freq, col_freq, number):
    shift_ids = jnp.arange(number)
    shift_x = (shift_ids % 2).astype(jnp.float32) - 0.5
    shift_y = (shift_ids // 2).astype(jnp.float32) - 0.5
    angle = (
        -2.0
        * math.pi
        * (
            shift_x[:, None, None] * col_freq[None, None, :]
            + shift_y[:, None, None] * row_freq[None, :, None]
        )
    )
    return (jnp.cos(angle), jnp.sin(angle))


def make_references(slices, cosine, sine):
    real_part = slices[0].astype(jnp.float32)
    imag_part = slices[1].astype(jnp.float32)
    shift_re = cosine[:, None] * real_part[None] - sine[:, None] * imag_part[None]
    shift_im = sine[:, None] * real_part[None] + cosine[:, None] * imag_part[None]
    shifted = jnp.stack([shift_re, shift_im], axis=2).astype(jnp.bfloat16)
    power = (real_part * real_part + imag_part * imag_part).astype(jnp.bfloat16)
    return (shifted, power)


def posterior_of(logits, counts):
    allowed = (jnp.arange(logits.shape[2])[None, :] < counts[:, None])[:, None, :]
    masked = jnp.where(allowed, logits, -1e30)
    highest = jnp.max(masked, axis=(1, 2), keepdims=True)
    exponent = jnp.where(allowed, jnp.exp(masked - highest), 0.0)
    return (exponent / jnp.sum(exponent, axis=(1, 2), keepdims=True)).astype(jnp.bfloat16)


def extract_rows(volume, plane_part, line_part, weight_part, slab_id):
    planes_here = volume.shape[1]
    flat = volume.reshape(2, planes_here * ROWS, COLS)
    local_plane = plane_part - slab_id * planes_here
    owned = (local_plane >= 0) & (local_plane < planes_here)
    line_index = jnp.clip(local_plane, 0, planes_here - 1) * ROWS + line_part
    lower = jnp.take(flat, line_index, axis=1)
    upper = jnp.take(flat, line_index + 1, axis=1)
    weight = weight_part[None, :, :, None]
    values = weight * lower + (1.0 - weight) * upper
    rounded = jnp.where(owned[None, :, :, None], values, 0.0).astype(jnp.bfloat16)
    return lax.optimization_barrier(rounded).astype(jnp.float32)


def insert_into(
    carry, piece, planes_all, lines_all, weights_all, slab_id, planes_here, line_first, line_count
):
    orient_count = piece.shape[0]
    number = piece.shape[1]
    local_plane = planes_all - slab_id * planes_here
    local_line = lines_all - line_first
    in_slab = (local_plane >= 0) & (local_plane < planes_here)
    lower_ok = in_slab & (local_line >= 0) & (local_line < line_count)
    upper_ok = in_slab & (local_line + 1 >= 0) & (local_line + 1 < line_count)
    dump_row = planes_here * line_count
    lower_index = jnp.where(lower_ok, local_plane * line_count + local_line, dump_row).reshape(-1)
    upper_index = jnp.where(upper_ok, local_plane * line_count + local_line + 1, dump_row).reshape(
        -1
    )
    values = piece.reshape(orient_count * number, 3 * COLS)
    weight = weights_all.reshape(-1, 1)
    carry = carry.at[lower_index].add(weight * values)
    return carry.at[upper_index].add((1.0 - weight) * values)


def scatter_sum(x, axis_name, dim):
    count = lax.axis_size(axis_name)
    shape = x.shape
    split = x.reshape(shape[:dim] + (count, shape[dim] // count) + shape[dim + 1 :])
    received = lax.all_to_all(split, axis_name, dim, dim, tiled=True)
    return jnp.sum(received, axis=dim)


def gather_all(x, axis_name, dim):
    count = lax.axis_size(axis_name)
    copies = jnp.broadcast_to(x[None], (count,) + x.shape)
    received = jnp.moveaxis(lax.all_to_all(copies, axis_name, 0, 0, tiled=True), 0, dim)
    return received.reshape(x.shape[:dim] + (count * x.shape[dim],) + x.shape[dim + 1 :])


def insert_kernel(start_ref, weight_ref, value_ref, out_ref):
    lines = out_ref.shape[0]
    rows = value_ref.shape[0]
    chunk = 512
    first_slot = pl.program_id(0) * lines
    slot = first_slot + lax.broadcasted_iota(jnp.int32, (lines, chunk), 0)
    total = jnp.zeros(out_ref.shape, jnp.float32)
    for part in range(rows // chunk):
        cols = pl.ds(part * chunk, chunk)
        start = start_ref[:, cols]
        weight = weight_ref[:, cols]
        spread = jnp.where(slot == start, weight, jnp.where(slot == start + 1, 1.0 - weight, 0.0))
        high = spread.astype(jnp.bfloat16)
        low = (spread - high.astype(jnp.float32)).astype(jnp.bfloat16)
        block = value_ref[cols, :]
        total += jnp.dot(high, block, preferred_element_type=jnp.float32)
        total += jnp.dot(low, block, preferred_element_type=jnp.float32)
    out_ref[...] = total


def insert_rows(values, start, weight, planes_here):
    rows, width = values.shape
    return pl.pallas_call(
        insert_kernel,
        grid=(planes_here,),
        in_specs=[
            pl.BlockSpec((1, rows), lambda q: (0, 0)),
            pl.BlockSpec((1, rows), lambda q: (0, 0)),
            pl.BlockSpec((rows, width), lambda q: (0, 0)),
        ],
        out_specs=pl.BlockSpec((ROWS, width), lambda q: (q, 0)),
        out_shape=jax.ShapeDtypeStruct((planes_here * ROWS, width), jnp.float32),
        compiler_params=pltpu.CompilerParams(vmem_limit_bytes=48 * 1024 * 1024),
        cost_estimate=pl.CostEstimate(
            flops=4 * planes_here * ROWS * rows * width,
            bytes_accessed=rows * width * 2 + planes_here * ROWS * width * 4,
            transcendentals=0,
        ),
    )(start.reshape(1, rows), weight.reshape(1, rows), values)


def extract_kernel(start_ref, weight_ref, high_ref, middle_ref, low_ref, out_ref):
    rows = out_ref.shape[1]
    slots = high_ref.shape[1]
    chunk = 512
    start = start_ref[...]
    totals = [jnp.zeros((rows, COLS), jnp.float32) for _ in range(high_ref.shape[0])]
    for part in range(slots // chunk):
        slot = part * chunk + lax.broadcasted_iota(jnp.int32, (rows, chunk), 1)
        pick = (slot == start).astype(jnp.bfloat16)
        cols = pl.ds(part * chunk, chunk)
        for piece_ref in (high_ref, middle_ref, low_ref):
            for m in range(len(totals)):
                totals[m] += jnp.dot(pick, piece_ref[m, cols, :], preferred_element_type=jnp.float32)
    weight = weight_ref[...]
    for j in range(2):
        lower = totals[j]
        upper = totals[2 + j]
        out_ref[j] = (weight * lower + (1.0 - weight) * upper).astype(out_ref.dtype)


def extract_share(volume, start, weight):
    slots = volume.shape[1] * ROWS
    flat = volume.reshape(2, slots, COLS)
    following = jnp.concatenate([flat[:, 1:], jnp.zeros_like(flat[:, :1])], axis=1)
    pairs = jnp.concatenate([flat, following], axis=0)
    high = lax.reduce_precision(pairs, exponent_bits=8, mantissa_bits=7)
    rest = pairs - high
    middle = lax.reduce_precision(rest, exponent_bits=8, mantissa_bits=7)
    low = rest - middle
    high, middle, low = (x.astype(jnp.bfloat16) for x in (high, middle, low))
    rows = start.size
    return pl.pallas_call(
        extract_kernel,
        grid=(rows // ROWS,),
        in_specs=[
            pl.BlockSpec((ROWS, 1), lambda q: (q, 0)),
            pl.BlockSpec((ROWS, 1), lambda q: (q, 0)),
            pl.BlockSpec((4, slots, COLS), lambda q: (0, 0, 0)),
            pl.BlockSpec((4, slots, COLS), lambda q: (0, 0, 0)),
            pl.BlockSpec((4, slots, COLS), lambda q: (0, 0, 0)),
        ],
        out_specs=pl.BlockSpec((2, ROWS, COLS), lambda q: (0, q, 0)),
        out_shape=jax.ShapeDtypeStruct((2, rows, COLS), jnp.bfloat16),
        compiler_params=pltpu.CompilerParams(vmem_limit_bytes=48 * 1024 * 1024),
        cost_estimate=pl.CostEstimate(
            flops=24 * rows * slots * COLS,
            bytes_accessed=3 * slots * 4 * COLS * 2 + 2 * rows * COLS * 2,
            transcendentals=0,
        ),
    )(start.reshape(rows, 1), weight.reshape(rows, 1), high, middle, low)


def staged_sum(x, dim, outer, inner, outer_first):
    outer_count = lax.axis_size(outer)
    inner_count = lax.axis_size(inner)
    shape = x.shape
    block = shape[dim] // (outer_count * inner_count)
    split = x.reshape(shape[:dim] + (outer_count, inner_count, block) + shape[dim + 1 :])
    if outer_first:
        split = scatter_sum(scatter_sum(split, outer, dim), inner, dim + 1)
    else:
        split = scatter_sum(scatter_sum(split, inner, dim + 1), outer, dim)
    return split.reshape(shape[:dim] + (block,) + shape[dim + 1 :])


def body(
    images,
    defocus,
    candidates,
    counts,
    noise_weight,
    volume,
    row_plane,
    row_line,
    row_weight,
    regularizer,
):
    local_rows = noise_weight.shape[0]
    slab_id = lax.axis_index("vy") * lax.axis_size("vz") + lax.axis_index("vz")
    global_rows = slab_id * local_rows + jnp.arange(local_rows)
    row_freq = (global_rows.astype(jnp.float32) - ROWS // 2) / ROWS
    col_freq = jnp.arange(COLS).astype(jnp.float32) / (2 * COLS)
    img_count = lax.axis_size("ix") * lax.axis_size("ic")
    group_id = lax.axis_index("ix") * lax.axis_size("ic") + lax.axis_index("ic")
    share = K // img_count
    first = group_id * share
    plane_share = lax.dynamic_slice_in_dim(row_plane, first, share, 0)
    line_share = lax.dynamic_slice_in_dim(row_line, first, share, 0)
    weight_share = lax.dynamic_slice_in_dim(row_weight, first, share, 0)
    planes_here = volume.shape[1]
    local_plane = plane_share - slab_id * planes_here
    in_slab = (local_plane >= 0) & (local_plane < planes_here)
    start = jnp.where(in_slab, local_plane * ROWS + line_share, -2)
    masked = extract_share(volume, start.reshape(-1), weight_share.reshape(-1))
    own_rows = staged_sum(masked.reshape(2, share, ROWS, COLS), 2, "vy", "vz", True)
    slices = gather_all(own_rows, ("ix", "ic"), 1)
    cosine, sine = shift_phases(row_freq, col_freq, TRANS)
    shifted, power = make_references(slices, cosine, sine)
    contrast = contrast_of(defocus, row_freq, col_freq)
    weighted = ((contrast * noise_weight)[None] * images).astype(jnp.bfloat16)
    squared = (contrast * contrast * noise_weight).astype(jnp.bfloat16)
    cross = jnp.einsum("jbrc,tkjrc->btk", weighted, shifted, preferred_element_type=jnp.float32)
    quadratic = jnp.einsum("brc,krc->bk", squared, power, preferred_element_type=jnp.float32)
    partial_logits = cross - 0.5 * quadratic[:, None, :]
    orientation = jnp.arange(K, dtype=jnp.int32)
    pick = candidates[:, :, None] == orientation[None, None, :]
    chosen = jnp.sum(
        jnp.where(pick[:, None, :, :], partial_logits[:, :, None, :], 0.0), axis=3
    )
    logits = gather_all(scatter_sum(chosen, ("vy", "vz"), 0), ("vy", "vz"), 0)
    listed = posterior_of(logits, counts)
    weights = jnp.sum(
        jnp.where(pick[:, None, :, :], listed[:, :, :, None], jnp.zeros((), jnp.bfloat16)),
        axis=2,
    )
    y_part = jnp.einsum("btk,jbrc->tkrjc", weights, weighted, preferred_element_type=jnp.float32)
    d_part = jnp.einsum("btk,brc->tkrc", weights, squared, preferred_element_type=jnp.float32)
    num_re = jnp.sum(
        cosine[:, None] * y_part[:, :, :, 0] + sine[:, None] * y_part[:, :, :, 1], axis=0
    )
    num_im = jnp.sum(
        cosine[:, None] * y_part[:, :, :, 1] - sine[:, None] * y_part[:, :, :, 0], axis=0
    )
    stacked = jnp.stack([num_re, num_im, jnp.sum(d_part, axis=0)], axis=2)
    partial_value = staged_sum(stacked, 0, "ix", "ic", False)
    piece = gather_all(gather_all(partial_value.astype(jnp.bfloat16), "vz", 1), "vy", 1)
    inserted = insert_rows(
        piece.reshape(share * ROWS, 3 * COLS), start.reshape(-1), weight_share.reshape(-1), planes_here
    )
    slab = inserted.reshape(planes_here, ROWS, 3, COLS)
    chips = lax.axis_size("ix")
    cores = lax.axis_size("ic")
    split = slab.reshape(planes_here, chips, cores, ROWS // (chips * cores), 3, COLS)
    within = scatter_sum(split, "ic", 2).astype(jnp.bfloat16)
    received = lax.all_to_all(within, "ix", 1, 1, tiled=True)
    summed = jnp.sum(received.astype(jnp.float32), axis=1).reshape(
        planes_here, ROWS // (chips * cores), 3, COLS
    )
    denom = summed[:, :, 2] + regularizer
    return jnp.stack([summed[:, :, 0] / denom, summed[:, :, 1] / denom], axis=0)


def solution(mesh):
    chips = dict(zip(mesh.axis_names, mesh.devices.shape))["img"] // 2
    rings = mesh.devices.shape[1] // 8
    return jax.shard_map(
        body,
        mesh=Mesh(mesh.devices.reshape(chips, -1, rings, mesh.devices.shape[1] // rings), ("ix", "ic", "vy", "vz")),
        in_specs=(
            P(None, ("ix", "ic"), ("vy", "vz"), None),
            P(("ix", "ic")),
            P(("ix", "ic"), None),
            P(("ix", "ic")),
            P(("vy", "vz"), None),
            P(None, ("vy", "vz"), None, None),
            P(),
            P(),
            P(),
            P(("vy", "vz"), ("ix", "ic"), None),
        ),
        out_specs=P(None, ("vy", "vz"), ("ix", "ic"), None),
        check_vma=False,
    )
```

```python
import math

import jax
import jax.numpy as jnp
from jax import lax
from jax.experimental import pallas as pl
from jax.experimental.pallas import tpu as pltpu
from jax.sharding import Mesh, PartitionSpec as P

ROWS = 256
COLS = 128
K = 64
TRANS = 4


AMPLITUDE = 0.1


def contrast_of(defocus, row_freq, col_freq):
    radius_sq = row_freq[:, None] * row_freq[:, None] + col_freq[None, :] * col_freq[None, :]
    angle = defocus[:, None, None] * radius_sq[None]
    return -(math.sqrt(1.0 - AMPLITUDE * AMPLITUDE) * jnp.sin(angle) + AMPLITUDE * jnp.cos(angle))


def shift_phases(row_freq, col_freq, number):
    shift_ids = jnp.arange(number)
    shift_x = (shift_ids % 2).astype(jnp.float32) - 0.5
    shift_y = (shift_ids // 2).astype(jnp.float32) - 0.5
    angle = (
        -2.0
        * math.pi
        * (
            shift_x[:, None, None] * col_freq[None, None, :]
            + shift_y[:, None, None] * row_freq[None, :, None]
        )
    )
    return (jnp.cos(angle), jnp.sin(angle))


def make_references(slices, cosine, sine):
    real_part = slices[0].astype(jnp.float32)
    imag_part = slices[1].astype(jnp.float32)
    shift_re = cosine[:, None] * real_part[None] - sine[:, None] * imag_part[None]
    shift_im = sine[:, None] * real_part[None] + cosine[:, None] * imag_part[None]
    shifted = jnp.stack([shift_re, shift_im], axis=2).astype(jnp.bfloat16)
    power = (real_part * real_part + imag_part * imag_part).astype(jnp.bfloat16)
    return (shifted, power)


def posterior_of(logits, counts):
    allowed = (jnp.arange(logits.shape[2])[None, :] < counts[:, None])[:, None, :]
    masked = jnp.where(allowed, logits, -1e30)
    highest = jnp.max(masked, axis=(1, 2), keepdims=True)
    exponent = jnp.where(allowed, jnp.exp(masked - highest), 0.0)
    return (exponent / jnp.sum(exponent, axis=(1, 2), keepdims=True)).astype(jnp.bfloat16)


def extract_rows(volume, plane_part, line_part, weight_part, slab_id):
    planes_here = volume.shape[1]
    flat = volume.reshape(2, planes_here * ROWS, COLS)
    local_plane = plane_part - slab_id * planes_here
    owned = (local_plane >= 0) & (local_plane < planes_here)
    line_index = jnp.clip(local_plane, 0, planes_here - 1) * ROWS + line_part
    lower = jnp.take(flat, line_index, axis=1)
    upper = jnp.take(flat, line_index + 1, axis=1)
    weight = weight_part[None, :, :, None]
    values = weight * lower + (1.0 - weight) * upper
    rounded = jnp.where(owned[None, :, :, None], values, 0.0).astype(jnp.bfloat16)
    return lax.optimization_barrier(rounded).astype(jnp.float32)


def insert_into(
    carry, piece, planes_all, lines_all, weights_all, slab_id, planes_here, line_first, line_count
):
    orient_count = piece.shape[0]
    number = piece.shape[1]
    local_plane = planes_all - slab_id * planes_here
    local_line = lines_all - line_first
    in_slab = (local_plane >= 0) & (local_plane < planes_here)
    lower_ok = in_slab & (local_line >= 0) & (local_line < line_count)
    upper_ok = in_slab & (local_line + 1 >= 0) & (local_line + 1 < line_count)
    dump_row = planes_here * line_count
    lower_index = jnp.where(lower_ok, local_plane * line_count + local_line, dump_row).reshape(-1)
    upper_index = jnp.where(upper_ok, local_plane * line_count + local_line + 1, dump_row).reshape(
        -1
    )
    values = piece.reshape(orient_count * number, 3 * COLS)
    weight = weights_all.reshape(-1, 1)
    carry = carry.at[lower_index].add(weight * values)
    return carry.at[upper_index].add((1.0 - weight) * values)


def scatter_sum(x, axis_name, dim):
    count = lax.axis_size(axis_name)
    shape = x.shape
    split = x.reshape(shape[:dim] + (count, shape[dim] // count) + shape[dim + 1 :])
    received = lax.all_to_all(split, axis_name, dim, dim, tiled=True)
    return jnp.sum(received, axis=dim)


def gather_all(x, axis_name, dim):
    count = lax.axis_size(axis_name)
    copies = jnp.broadcast_to(x[None], (count,) + x.shape)
    received = jnp.moveaxis(lax.all_to_all(copies, axis_name, 0, 0, tiled=True), 0, dim)
    return received.reshape(x.shape[:dim] + (count * x.shape[dim],) + x.shape[dim + 1 :])


def insert_kernel(start_ref, weight_ref, value_ref, out_ref):
    lines = out_ref.shape[0]
    rows = value_ref.shape[0]
    chunk = 512
    first_slot = pl.program_id(0) * lines
    slot = first_slot + lax.broadcasted_iota(jnp.int32, (lines, chunk), 0)
    total = jnp.zeros(out_ref.shape, jnp.float32)
    for part in range(rows // chunk):
        cols = pl.ds(part * chunk, chunk)
        start = start_ref[:, cols]
        weight = weight_ref[:, cols]
        spread = jnp.where(slot == start, weight, jnp.where(slot == start + 1, 1.0 - weight, 0.0))
        high = spread.astype(jnp.bfloat16)
        low = (spread - high.astype(jnp.float32)).astype(jnp.bfloat16)
        block = value_ref[cols, :]
        total += jnp.dot(high, block, preferred_element_type=jnp.float32)
        total += jnp.dot(low, block, preferred_element_type=jnp.float32)
    out_ref[...] = total


def insert_rows(values, start, weight, planes_here):
    rows, width = values.shape
    return pl.pallas_call(
        insert_kernel,
        grid=(planes_here,),
        in_specs=[
            pl.BlockSpec((1, rows), lambda q: (0, 0)),
            pl.BlockSpec((1, rows), lambda q: (0, 0)),
            pl.BlockSpec((rows, width), lambda q: (0, 0)),
        ],
        out_specs=pl.BlockSpec((ROWS, width), lambda q: (q, 0)),
        out_shape=jax.ShapeDtypeStruct((planes_here * ROWS, width), jnp.float32),
        compiler_params=pltpu.CompilerParams(vmem_limit_bytes=48 * 1024 * 1024),
        cost_estimate=pl.CostEstimate(
            flops=4 * planes_here * ROWS * rows * width,
            bytes_accessed=rows * width * 2 + planes_here * ROWS * width * 4,
            transcendentals=0,
        ),
    )(start.reshape(1, rows), weight.reshape(1, rows), values)


def extract_kernel(start_ref, weight_ref, high_ref, middle_ref, low_ref, out_ref):
    rows = out_ref.shape[1]
    slots = high_ref.shape[0]
    chunk = 512
    start = start_ref[...]
    total = jnp.zeros((rows, high_ref.shape[1]), jnp.float32)
    for part in range(slots // chunk):
        slot = part * chunk + lax.broadcasted_iota(jnp.int32, (rows, chunk), 1)
        pick = (slot == start).astype(jnp.bfloat16)
        cols = pl.ds(part * chunk, chunk)
        for piece_ref in (high_ref, middle_ref, low_ref):
            total += jnp.dot(pick, piece_ref[cols, :], preferred_element_type=jnp.float32)
    weight = weight_ref[...]
    for j in range(2):
        lower = total[:, j * COLS : (j + 1) * COLS]
        upper = total[:, (2 + j) * COLS : (3 + j) * COLS]
        out_ref[j] = (weight * lower + (1.0 - weight) * upper).astype(out_ref.dtype)


def extract_share(volume, start, weight):
    slots = volume.shape[1] * ROWS
    flat = volume.reshape(2, slots, COLS)
    following = jnp.concatenate([flat[:, 1:], jnp.zeros_like(flat[:, :1])], axis=1)
    pairs = jnp.concatenate([flat, following], axis=0).transpose(1, 0, 2).reshape(slots, 4 * COLS)
    high = lax.reduce_precision(pairs, exponent_bits=8, mantissa_bits=7)
    rest = pairs - high
    middle = lax.reduce_precision(rest, exponent_bits=8, mantissa_bits=7)
    low = rest - middle
    high, middle, low = (x.astype(jnp.bfloat16) for x in (high, middle, low))
    rows = start.size
    return pl.pallas_call(
        extract_kernel,
        grid=(rows // ROWS,),
        in_specs=[
            pl.BlockSpec((ROWS, 1), lambda q: (q, 0)),
            pl.BlockSpec((ROWS, 1), lambda q: (q, 0)),
            pl.BlockSpec((slots, 4 * COLS), lambda q: (0, 0)),
            pl.BlockSpec((slots, 4 * COLS), lambda q: (0, 0)),
            pl.BlockSpec((slots, 4 * COLS), lambda q: (0, 0)),
        ],
        out_specs=pl.BlockSpec((2, ROWS, COLS), lambda q: (0, q, 0)),
        out_shape=jax.ShapeDtypeStruct((2, rows, COLS), jnp.bfloat16),
        compiler_params=pltpu.CompilerParams(vmem_limit_bytes=48 * 1024 * 1024),
        cost_estimate=pl.CostEstimate(
            flops=24 * rows * slots * COLS,
            bytes_accessed=3 * slots * 4 * COLS * 2 + 2 * rows * COLS * 2,
            transcendentals=0,
        ),
    )(start.reshape(rows, 1), weight.reshape(rows, 1), high, middle, low)


def staged_sum(x, dim, outer, inner, outer_first):
    outer_count = lax.axis_size(outer)
    inner_count = lax.axis_size(inner)
    shape = x.shape
    block = shape[dim] // (outer_count * inner_count)
    split = x.reshape(shape[:dim] + (outer_count, inner_count, block) + shape[dim + 1 :])
    if outer_first:
        split = scatter_sum(scatter_sum(split, outer, dim), inner, dim + 1)
    else:
        split = scatter_sum(scatter_sum(split, inner, dim + 1), outer, dim)
    return split.reshape(shape[:dim] + (block,) + shape[dim + 1 :])


def body(
    images,
    defocus,
    candidates,
    counts,
    noise_weight,
    volume,
    row_plane,
    row_line,
    row_weight,
    regularizer,
):
    local_rows = noise_weight.shape[0]
    slab_id = lax.axis_index("vy") * lax.axis_size("vz") + lax.axis_index("vz")
    global_rows = slab_id * local_rows + jnp.arange(local_rows)
    row_freq = (global_rows.astype(jnp.float32) - ROWS // 2) / ROWS
    col_freq = jnp.arange(COLS).astype(jnp.float32) / (2 * COLS)
    img_count = lax.axis_size("ix") * lax.axis_size("ic")
    group_id = lax.axis_index("ix") * lax.axis_size("ic") + lax.axis_index("ic")
    share = K // img_count
    first = group_id * share
    plane_share = lax.dynamic_slice_in_dim(row_plane, first, share, 0)
    line_share = lax.dynamic_slice_in_dim(row_line, first, share, 0)
    weight_share = lax.dynamic_slice_in_dim(row_weight, first, share, 0)
    planes_here = volume.shape[1]
    local_plane = plane_share - slab_id * planes_here
    in_slab = (local_plane >= 0) & (local_plane < planes_here)
    start = jnp.where(in_slab, local_plane * ROWS + line_share, -2)
    masked = extract_share(volume, start.reshape(-1), weight_share.reshape(-1))
    own_rows = staged_sum(masked.reshape(2, share, ROWS, COLS), 2, "vy", "vz", True)
    slices = gather_all(own_rows, ("ix", "ic"), 1)
    cosine, sine = shift_phases(row_freq, col_freq, TRANS)
    shifted, power = make_references(slices, cosine, sine)
    contrast = contrast_of(defocus, row_freq, col_freq)
    weighted = ((contrast * noise_weight)[None] * images).astype(jnp.bfloat16)
    squared = (contrast * contrast * noise_weight).astype(jnp.bfloat16)
    cross = jnp.einsum("jbrc,tkjrc->btk", weighted, shifted, preferred_element_type=jnp.float32)
    quadratic = jnp.einsum("brc,krc->bk", squared, power, preferred_element_type=jnp.float32)
    partial_logits = cross - 0.5 * quadratic[:, None, :]
    orientation = jnp.arange(K, dtype=jnp.int32)
    pick = candidates[:, :, None] == orientation[None, None, :]
    chosen = jnp.sum(
        jnp.where(pick[:, None, :, :], partial_logits[:, :, None, :], 0.0), axis=3
    )
    logits = gather_all(scatter_sum(chosen, ("vy", "vz"), 0), ("vy", "vz"), 0)
    listed = posterior_of(logits, counts)
    weights = jnp.sum(
        jnp.where(pick[:, None, :, :], listed[:, :, :, None], jnp.zeros((), jnp.bfloat16)),
        axis=2,
    )
    y_part = jnp.einsum("btk,jbrc->tkrjc", weights, weighted, preferred_element_type=jnp.float32)
    d_part = jnp.einsum("btk,brc->tkrc", weights, squared, preferred_element_type=jnp.float32)
    num_re = jnp.sum(
        cosine[:, None] * y_part[:, :, :, 0] + sine[:, None] * y_part[:, :, :, 1], axis=0
    )
    num_im = jnp.sum(
        cosine[:, None] * y_part[:, :, :, 1] - sine[:, None] * y_part[:, :, :, 0], axis=0
    )
    stacked = jnp.stack([num_re, num_im, jnp.sum(d_part, axis=0)], axis=2)
    chips = lax.axis_size("ix")
    cores = lax.axis_size("ic")
    split = stacked.reshape((chips, cores, K // (chips * cores)) + stacked.shape[1:])
    within = scatter_sum(split, "ic", 1).astype(jnp.bfloat16)
    received = lax.all_to_all(within, "ix", 0, 0, tiled=True)
    partial_value = jnp.sum(received.astype(jnp.float32), axis=0).reshape(
        (K // (chips * cores),) + stacked.shape[1:]
    )
    piece = gather_all(gather_all(partial_value.astype(jnp.bfloat16), "vz", 1), "vy", 1)
    inserted = insert_rows(
        piece.reshape(share * ROWS, 3 * COLS), start.reshape(-1), weight_share.reshape(-1), planes_here
    )
    slab = inserted.reshape(planes_here, ROWS, 3, COLS)
    split = slab.reshape(planes_here, chips, cores, ROWS // (chips * cores), 3, COLS)
    within = scatter_sum(split, "ic", 2).astype(jnp.bfloat16)
    received = lax.all_to_all(within, "ix", 1, 1, tiled=True)
    summed = jnp.sum(received.astype(jnp.float32), axis=1).reshape(
        planes_here, ROWS // (chips * cores), 3, COLS
    )
    denom = summed[:, :, 2] + regularizer
    return jnp.stack([summed[:, :, 0] / denom, summed[:, :, 1] / denom], axis=0)


def solution(mesh):
    chips = dict(zip(mesh.axis_names, mesh.devices.shape))["img"] // 2
    rings = mesh.devices.shape[1] // 8
    return jax.shard_map(
        body,
        mesh=Mesh(mesh.devices.reshape(chips, -1, rings, mesh.devices.shape[1] // rings), ("ix", "ic", "vy", "vz")),
        in_specs=(
            P(None, ("ix", "ic"), ("vy", "vz"), None),
            P(("ix", "ic")),
            P(("ix", "ic"), None),
            P(("ix", "ic")),
            P(("vy", "vz"), None),
            P(None, ("vy", "vz"), None, None),
            P(),
            P(),
            P(),
            P(("vy", "vz"), ("ix", "ic"), None),
        ),
        out_specs=P(None, ("vy", "vz"), ("ix", "ic"), None),
        check_vma=False,
    )
```

```python
import math

import jax
import jax.numpy as jnp
from jax import lax
from jax.experimental import pallas as pl
from jax.experimental.pallas import tpu as pltpu
from jax.sharding import Mesh, PartitionSpec as P

ROWS = 256
COLS = 128
K = 64
TRANS = 4


AMPLITUDE = 0.1


def contrast_of(defocus, row_freq, col_freq):
    radius_sq = row_freq[:, None] * row_freq[:, None] + col_freq[None, :] * col_freq[None, :]
    angle = defocus[:, None, None] * radius_sq[None]
    return -(math.sqrt(1.0 - AMPLITUDE * AMPLITUDE) * jnp.sin(angle) + AMPLITUDE * jnp.cos(angle))


def shift_phases(row_freq, col_freq, number):
    shift_ids = jnp.arange(number)
    shift_x = (shift_ids % 2).astype(jnp.float32) - 0.5
    shift_y = (shift_ids // 2).astype(jnp.float32) - 0.5
    angle = (
        -2.0
        * math.pi
        * (
            shift_x[:, None, None] * col_freq[None, None, :]
            + shift_y[:, None, None] * row_freq[None, :, None]
        )
    )
    return (jnp.cos(angle), jnp.sin(angle))


def make_references(slices, cosine, sine):
    real_part = slices[0].astype(jnp.float32)
    imag_part = slices[1].astype(jnp.float32)
    shift_re = cosine[:, None] * real_part[None] - sine[:, None] * imag_part[None]
    shift_im = sine[:, None] * real_part[None] + cosine[:, None] * imag_part[None]
    shifted = jnp.stack([shift_re, shift_im], axis=2).astype(jnp.bfloat16)
    power = (real_part * real_part + imag_part * imag_part).astype(jnp.bfloat16)
    return (shifted, power)


def posterior_of(logits, counts):
    allowed = (jnp.arange(logits.shape[2])[None, :] < counts[:, None])[:, None, :]
    masked = jnp.where(allowed, logits, -1e30)
    highest = jnp.max(masked, axis=(1, 2), keepdims=True)
    exponent = jnp.where(allowed, jnp.exp(masked - highest), 0.0)
    return (exponent / jnp.sum(exponent, axis=(1, 2), keepdims=True)).astype(jnp.bfloat16)


def extract_rows(volume, plane_part, line_part, weight_part, slab_id):
    planes_here = volume.shape[1]
    flat = volume.reshape(2, planes_here * ROWS, COLS)
    local_plane = plane_part - slab_id * planes_here
    owned = (local_plane >= 0) & (local_plane < planes_here)
    line_index = jnp.clip(local_plane, 0, planes_here - 1) * ROWS + line_part
    lower = jnp.take(flat, line_index, axis=1)
    upper = jnp.take(flat, line_index + 1, axis=1)
    weight = weight_part[None, :, :, None]
    values = weight * lower + (1.0 - weight) * upper
    rounded = jnp.where(owned[None, :, :, None], values, 0.0).astype(jnp.bfloat16)
    return lax.optimization_barrier(rounded).astype(jnp.float32)


def insert_into(
    carry, piece, planes_all, lines_all, weights_all, slab_id, planes_here, line_first, line_count
):
    orient_count = piece.shape[0]
    number = piece.shape[1]
    local_plane = planes_all - slab_id * planes_here
    local_line = lines_all - line_first
    in_slab = (local_plane >= 0) & (local_plane < planes_here)
    lower_ok = in_slab & (local_line >= 0) & (local_line < line_count)
    upper_ok = in_slab & (local_line + 1 >= 0) & (local_line + 1 < line_count)
    dump_row = planes_here * line_count
    lower_index = jnp.where(lower_ok, local_plane * line_count + local_line, dump_row).reshape(-1)
    upper_index = jnp.where(upper_ok, local_plane * line_count + local_line + 1, dump_row).reshape(
        -1
    )
    values = piece.reshape(orient_count * number, 3 * COLS)
    weight = weights_all.reshape(-1, 1)
    carry = carry.at[lower_index].add(weight * values)
    return carry.at[upper_index].add((1.0 - weight) * values)


def scatter_sum(x, axis_name, dim):
    count = lax.axis_size(axis_name)
    shape = x.shape
    split = x.reshape(shape[:dim] + (count, shape[dim] // count) + shape[dim + 1 :])
    received = lax.all_to_all(split, axis_name, dim, dim, tiled=True)
    return jnp.sum(received, axis=dim)


def gather_all(x, axis_name, dim):
    count = lax.axis_size(axis_name)
    copies = jnp.broadcast_to(x[None], (count,) + x.shape)
    received = jnp.moveaxis(lax.all_to_all(copies, axis_name, 0, 0, tiled=True), 0, dim)
    return received.reshape(x.shape[:dim] + (count * x.shape[dim],) + x.shape[dim + 1 :])


def insert_kernel(start_ref, weight_ref, value_ref, out_ref):
    lines = out_ref.shape[0]
    rows = value_ref.shape[0]
    chunk = 512
    first_slot = pl.program_id(0) * lines
    slot = first_slot + lax.broadcasted_iota(jnp.int32, (lines, chunk), 0)
    total = jnp.zeros(out_ref.shape, jnp.float32)
    for part in range(rows // chunk):
        cols = pl.ds(part * chunk, chunk)
        start = start_ref[:, cols]
        weight = weight_ref[:, cols]
        spread = jnp.where(slot == start, weight, jnp.where(slot == start + 1, 1.0 - weight, 0.0))
        high = spread.astype(jnp.bfloat16)
        low = (spread - high.astype(jnp.float32)).astype(jnp.bfloat16)
        block = value_ref[cols, :]
        total += jnp.dot(high, block, preferred_element_type=jnp.float32)
        total += jnp.dot(low, block, preferred_element_type=jnp.float32)
    out_ref[...] = total


def insert_rows(values, start, weight, planes_here):
    rows, width = values.shape
    return pl.pallas_call(
        insert_kernel,
        grid=(planes_here,),
        in_specs=[
            pl.BlockSpec((1, rows), lambda q: (0, 0)),
            pl.BlockSpec((1, rows), lambda q: (0, 0)),
            pl.BlockSpec((rows, width), lambda q: (0, 0)),
        ],
        out_specs=pl.BlockSpec((ROWS, width), lambda q: (q, 0)),
        out_shape=jax.ShapeDtypeStruct((planes_here * ROWS, width), jnp.float32),
        compiler_params=pltpu.CompilerParams(vmem_limit_bytes=48 * 1024 * 1024),
        cost_estimate=pl.CostEstimate(
            flops=4 * planes_here * ROWS * rows * width,
            bytes_accessed=rows * width * 2 + planes_here * ROWS * width * 4,
            transcendentals=0,
        ),
    )(start.reshape(1, rows), weight.reshape(1, rows), values)


def extract_kernel(start_ref, weight_ref, high_ref, middle_ref, low_ref, out_ref):
    rows = out_ref.shape[1]
    slots = high_ref.shape[0]
    chunk = 1024
    start = start_ref[...]
    total = jnp.zeros((rows, high_ref.shape[1]), jnp.float32)
    for part in range(slots // chunk):
        slot = part * chunk + lax.broadcasted_iota(jnp.int32, (rows, chunk), 1)
        pick = (slot == start).astype(jnp.bfloat16)
        cols = pl.ds(part * chunk, chunk)
        for piece_ref in (high_ref, middle_ref, low_ref):
            total += jnp.dot(pick, piece_ref[cols, :], preferred_element_type=jnp.float32)
    weight = weight_ref[...]
    for j in range(2):
        lower = total[:, j * COLS : (j + 1) * COLS]
        upper = total[:, (2 + j) * COLS : (3 + j) * COLS]
        out_ref[j] = (weight * lower + (1.0 - weight) * upper).astype(out_ref.dtype)


def extract_share(volume, start, weight):
    slots = volume.shape[1] * ROWS
    flat = volume.reshape(2, slots, COLS)
    following = jnp.concatenate([flat[:, 1:], jnp.zeros_like(flat[:, :1])], axis=1)
    pairs = jnp.concatenate([flat, following], axis=0).transpose(1, 0, 2).reshape(slots, 4 * COLS)
    high = lax.reduce_precision(pairs, exponent_bits=8, mantissa_bits=7)
    rest = pairs - high
    middle = lax.reduce_precision(rest, exponent_bits=8, mantissa_bits=7)
    low = rest - middle
    high, middle, low = (x.astype(jnp.bfloat16) for x in (high, middle, low))
    rows = start.size
    return pl.pallas_call(
        extract_kernel,
        grid=(rows // ROWS,),
        in_specs=[
            pl.BlockSpec((ROWS, 1), lambda q: (q, 0)),
            pl.BlockSpec((ROWS, 1), lambda q: (q, 0)),
            pl.BlockSpec((slots, 4 * COLS), lambda q: (0, 0)),
            pl.BlockSpec((slots, 4 * COLS), lambda q: (0, 0)),
            pl.BlockSpec((slots, 4 * COLS), lambda q: (0, 0)),
        ],
        out_specs=pl.BlockSpec((2, ROWS, COLS), lambda q: (0, q, 0)),
        out_shape=jax.ShapeDtypeStruct((2, rows, COLS), jnp.bfloat16),
        compiler_params=pltpu.CompilerParams(vmem_limit_bytes=48 * 1024 * 1024),
        cost_estimate=pl.CostEstimate(
            flops=24 * rows * slots * COLS,
            bytes_accessed=3 * slots * 4 * COLS * 2 + 2 * rows * COLS * 2,
            transcendentals=0,
        ),
    )(start.reshape(rows, 1), weight.reshape(rows, 1), high, middle, low)


def staged_sum(x, dim, outer, inner, outer_first):
    outer_count = lax.axis_size(outer)
    inner_count = lax.axis_size(inner)
    shape = x.shape
    block = shape[dim] // (outer_count * inner_count)
    split = x.reshape(shape[:dim] + (outer_count, inner_count, block) + shape[dim + 1 :])
    if outer_first:
        split = scatter_sum(scatter_sum(split, outer, dim), inner, dim + 1)
    else:
        split = scatter_sum(scatter_sum(split, inner, dim + 1), outer, dim)
    return split.reshape(shape[:dim] + (block,) + shape[dim + 1 :])


def body(
    images,
    defocus,
    candidates,
    counts,
    noise_weight,
    volume,
    row_plane,
    row_line,
    row_weight,
    regularizer,
):
    local_rows = noise_weight.shape[0]
    slab_id = lax.axis_index("vy") * lax.axis_size("vz") + lax.axis_index("vz")
    global_rows = slab_id * local_rows + jnp.arange(local_rows)
    row_freq = (global_rows.astype(jnp.float32) - ROWS // 2) / ROWS
    col_freq = jnp.arange(COLS).astype(jnp.float32) / (2 * COLS)
    img_count = lax.axis_size("ix") * lax.axis_size("ic")
    group_id = lax.axis_index("ix") * lax.axis_size("ic") + lax.axis_index("ic")
    share = K // img_count
    first = group_id * share
    plane_share = lax.dynamic_slice_in_dim(row_plane, first, share, 0)
    line_share = lax.dynamic_slice_in_dim(row_line, first, share, 0)
    weight_share = lax.dynamic_slice_in_dim(row_weight, first, share, 0)
    planes_here = volume.shape[1]
    local_plane = plane_share - slab_id * planes_here
    in_slab = (local_plane >= 0) & (local_plane < planes_here)
    start = jnp.where(in_slab, local_plane * ROWS + line_share, -2)
    masked = extract_share(volume, start.reshape(-1), weight_share.reshape(-1))
    own_rows = staged_sum(masked.reshape(2, share, ROWS, COLS), 2, "vy", "vz", True)
    slices = gather_all(own_rows, ("ix", "ic"), 1)
    cosine, sine = shift_phases(row_freq, col_freq, TRANS)
    shifted, power = make_references(slices, cosine, sine)
    contrast = contrast_of(defocus, row_freq, col_freq)
    weighted = ((contrast * noise_weight)[None] * images).astype(jnp.bfloat16)
    squared = (contrast * contrast * noise_weight).astype(jnp.bfloat16)
    cross = jnp.einsum("jbrc,tkjrc->btk", weighted, shifted, preferred_element_type=jnp.float32)
    quadratic = jnp.einsum("brc,krc->bk", squared, power, preferred_element_type=jnp.float32)
    partial_logits = cross - 0.5 * quadratic[:, None, :]
    orientation = jnp.arange(K, dtype=jnp.int32)
    pick = candidates[:, :, None] == orientation[None, None, :]
    chosen = jnp.sum(
        jnp.where(pick[:, None, :, :], partial_logits[:, :, None, :], 0.0), axis=3
    )
    logits = gather_all(scatter_sum(chosen, ("vy", "vz"), 0), ("vy", "vz"), 0)
    listed = posterior_of(logits, counts)
    weights = jnp.sum(
        jnp.where(pick[:, None, :, :], listed[:, :, :, None], jnp.zeros((), jnp.bfloat16)),
        axis=2,
    )
    y_part = jnp.einsum("btk,jbrc->tkrjc", weights, weighted, preferred_element_type=jnp.float32)
    d_part = jnp.einsum("btk,brc->tkrc", weights, squared, preferred_element_type=jnp.float32)
    num_re = jnp.sum(
        cosine[:, None] * y_part[:, :, :, 0] + sine[:, None] * y_part[:, :, :, 1], axis=0
    )
    num_im = jnp.sum(
        cosine[:, None] * y_part[:, :, :, 1] - sine[:, None] * y_part[:, :, :, 0], axis=0
    )
    stacked = jnp.stack([num_re, num_im, jnp.sum(d_part, axis=0)], axis=2)
    chips = lax.axis_size("ix")
    cores = lax.axis_size("ic")
    split = stacked.reshape((chips, cores, K // (chips * cores)) + stacked.shape[1:])
    within = scatter_sum(split, "ic", 1).astype(jnp.bfloat16)
    received = lax.all_to_all(within, "ix", 0, 0, tiled=True)
    partial_value = jnp.sum(received.astype(jnp.float32), axis=0).reshape(
        (K // (chips * cores),) + stacked.shape[1:]
    )
    piece = gather_all(gather_all(partial_value.astype(jnp.bfloat16), "vz", 1), "vy", 1)
    inserted = insert_rows(
        piece.reshape(share * ROWS, 3 * COLS), start.reshape(-1), weight_share.reshape(-1), planes_here
    )
    slab = inserted.reshape(planes_here, ROWS, 3, COLS)
    split = slab.reshape(planes_here, chips, cores, ROWS // (chips * cores), 3, COLS)
    within = scatter_sum(split, "ic", 2).astype(jnp.bfloat16)
    received = lax.all_to_all(within, "ix", 1, 1, tiled=True)
    summed = jnp.sum(received.astype(jnp.float32), axis=1).reshape(
        planes_here, ROWS // (chips * cores), 3, COLS
    )
    denom = summed[:, :, 2] + regularizer
    return jnp.stack([summed[:, :, 0] / denom, summed[:, :, 1] / denom], axis=0)


def solution(mesh):
    chips = dict(zip(mesh.axis_names, mesh.devices.shape))["img"] // 2
    rings = mesh.devices.shape[1] // 8
    return jax.shard_map(
        body,
        mesh=Mesh(mesh.devices.reshape(chips, -1, rings, mesh.devices.shape[1] // rings), ("ix", "ic", "vy", "vz")),
        in_specs=(
            P(None, ("ix", "ic"), ("vy", "vz"), None),
            P(("ix", "ic")),
            P(("ix", "ic"), None),
            P(("ix", "ic")),
            P(("vy", "vz"), None),
            P(None, ("vy", "vz"), None, None),
            P(),
            P(),
            P(),
            P(("vy", "vz"), ("ix", "ic"), None),
        ),
        out_specs=P(None, ("vy", "vz"), ("ix", "ic"), None),
        check_vma=False,
    )
```

```python
import math

import jax
import jax.numpy as jnp
from jax import lax
from jax.experimental import pallas as pl
from jax.experimental.pallas import tpu as pltpu
from jax.sharding import Mesh, PartitionSpec as P

ROWS = 256
COLS = 128
K = 64
TRANS = 4


AMPLITUDE = 0.1


def contrast_of(defocus, row_freq, col_freq):
    radius_sq = row_freq[:, None] * row_freq[:, None] + col_freq[None, :] * col_freq[None, :]
    angle = defocus[:, None, None] * radius_sq[None]
    return -(math.sqrt(1.0 - AMPLITUDE * AMPLITUDE) * jnp.sin(angle) + AMPLITUDE * jnp.cos(angle))


def shift_phases(row_freq, col_freq, number):
    shift_ids = jnp.arange(number)
    shift_x = (shift_ids % 2).astype(jnp.float32) - 0.5
    shift_y = (shift_ids // 2).astype(jnp.float32) - 0.5
    angle = (
        -2.0
        * math.pi
        * (
            shift_x[:, None, None] * col_freq[None, None, :]
            + shift_y[:, None, None] * row_freq[None, :, None]
        )
    )
    return (jnp.cos(angle), jnp.sin(angle))


def make_references(slices, cosine, sine):
    real_part = slices[0].astype(jnp.float32)
    imag_part = slices[1].astype(jnp.float32)
    shift_re = cosine[:, None] * real_part[None] - sine[:, None] * imag_part[None]
    shift_im = sine[:, None] * real_part[None] + cosine[:, None] * imag_part[None]
    shifted = jnp.stack([shift_re, shift_im], axis=2).astype(jnp.bfloat16)
    power = (real_part * real_part + imag_part * imag_part).astype(jnp.bfloat16)
    return (shifted, power)


def posterior_of(logits, counts):
    allowed = (jnp.arange(logits.shape[2])[None, :] < counts[:, None])[:, None, :]
    masked = jnp.where(allowed, logits, -1e30)
    highest = jnp.max(masked, axis=(1, 2), keepdims=True)
    exponent = jnp.where(allowed, jnp.exp(masked - highest), 0.0)
    return (exponent / jnp.sum(exponent, axis=(1, 2), keepdims=True)).astype(jnp.bfloat16)


def extract_rows(volume, plane_part, line_part, weight_part, slab_id):
    planes_here = volume.shape[1]
    flat = volume.reshape(2, planes_here * ROWS, COLS)
    local_plane = plane_part - slab_id * planes_here
    owned = (local_plane >= 0) & (local_plane < planes_here)
    line_index = jnp.clip(local_plane, 0, planes_here - 1) * ROWS + line_part
    lower = jnp.take(flat, line_index, axis=1)
    upper = jnp.take(flat, line_index + 1, axis=1)
    weight = weight_part[None, :, :, None]
    values = weight * lower + (1.0 - weight) * upper
    rounded = jnp.where(owned[None, :, :, None], values, 0.0).astype(jnp.bfloat16)
    return lax.optimization_barrier(rounded).astype(jnp.float32)


def insert_into(
    carry, piece, planes_all, lines_all, weights_all, slab_id, planes_here, line_first, line_count
):
    orient_count = piece.shape[0]
    number = piece.shape[1]
    local_plane = planes_all - slab_id * planes_here
    local_line = lines_all - line_first
    in_slab = (local_plane >= 0) & (local_plane < planes_here)
    lower_ok = in_slab & (local_line >= 0) & (local_line < line_count)
    upper_ok = in_slab & (local_line + 1 >= 0) & (local_line + 1 < line_count)
    dump_row = planes_here * line_count
    lower_index = jnp.where(lower_ok, local_plane * line_count + local_line, dump_row).reshape(-1)
    upper_index = jnp.where(upper_ok, local_plane * line_count + local_line + 1, dump_row).reshape(
        -1
    )
    values = piece.reshape(orient_count * number, 3 * COLS)
    weight = weights_all.reshape(-1, 1)
    carry = carry.at[lower_index].add(weight * values)
    return carry.at[upper_index].add((1.0 - weight) * values)


def scatter_sum(x, axis_name, dim):
    count = lax.axis_size(axis_name)
    shape = x.shape
    split = x.reshape(shape[:dim] + (count, shape[dim] // count) + shape[dim + 1 :])
    received = lax.all_to_all(split, axis_name, dim, dim, tiled=True)
    return jnp.sum(received, axis=dim)


def gather_all(x, axis_name, dim):
    count = lax.axis_size(axis_name)
    copies = jnp.broadcast_to(x[None], (count,) + x.shape)
    received = jnp.moveaxis(lax.all_to_all(copies, axis_name, 0, 0, tiled=True), 0, dim)
    return received.reshape(x.shape[:dim] + (count * x.shape[dim],) + x.shape[dim + 1 :])


def insert_kernel(start_ref, weight_ref, value_ref, out_ref):
    lines = ROWS
    rows = value_ref.shape[0]
    chunk = 512
    first_slot = pl.program_id(0) * lines
    slot = first_slot + lax.broadcasted_iota(jnp.int32, (lines, chunk), 0)
    total = jnp.zeros((lines, value_ref.shape[1]), jnp.float32)
    for part in range(rows // chunk):
        cols = pl.ds(part * chunk, chunk)
        start = start_ref[:, cols]
        weight = weight_ref[:, cols]
        spread = jnp.where(slot == start, weight, jnp.where(slot == start + 1, 1.0 - weight, 0.0))
        high = spread.astype(jnp.bfloat16)
        low = (spread - high.astype(jnp.float32)).astype(jnp.bfloat16)
        block = value_ref[cols, :]
        total += jnp.dot(high, block, preferred_element_type=jnp.float32)
        total += jnp.dot(low, block, preferred_element_type=jnp.float32)
    out_ref[...] = total.reshape(out_ref.shape)


def insert_rows(values, start, weight, planes_here, chips, cores):
    rows, width = values.shape
    block = ROWS // (chips * cores)
    return pl.pallas_call(
        insert_kernel,
        grid=(planes_here,),
        in_specs=[
            pl.BlockSpec((1, rows), lambda q: (0, 0)),
            pl.BlockSpec((1, rows), lambda q: (0, 0)),
            pl.BlockSpec((rows, width), lambda q: (0, 0)),
        ],
        out_specs=pl.BlockSpec((chips, cores, 1, block, width), lambda q: (0, 0, q, 0, 0)),
        out_shape=jax.ShapeDtypeStruct((chips, cores, planes_here, block, width), jnp.float32),
        compiler_params=pltpu.CompilerParams(vmem_limit_bytes=48 * 1024 * 1024),
        cost_estimate=pl.CostEstimate(
            flops=4 * planes_here * ROWS * rows * width,
            bytes_accessed=rows * width * 2 + planes_here * ROWS * width * 4,
            transcendentals=0,
        ),
    )(start.reshape(1, rows), weight.reshape(1, rows), values)


def extract_kernel(start_ref, weight_ref, high_ref, middle_ref, low_ref, out_ref):
    rows = out_ref.shape[1]
    slots = high_ref.shape[0]
    chunk = 512
    start = start_ref[...]
    total = jnp.zeros((rows, high_ref.shape[1]), jnp.float32)
    for part in range(slots // chunk):
        slot = part * chunk + lax.broadcasted_iota(jnp.int32, (rows, chunk), 1)
        pick = (slot == start).astype(jnp.bfloat16)
        cols = pl.ds(part * chunk, chunk)
        for piece_ref in (high_ref, middle_ref, low_ref):
            total += jnp.dot(pick, piece_ref[cols, :], preferred_element_type=jnp.float32)
    weight = weight_ref[...]
    for j in range(2):
        lower = total[:, j * COLS : (j + 1) * COLS]
        upper = total[:, (2 + j) * COLS : (3 + j) * COLS]
        out_ref[j] = (weight * lower + (1.0 - weight) * upper).astype(out_ref.dtype)


def extract_share(volume, start, weight):
    slots = volume.shape[1] * ROWS
    flat = volume.reshape(2, slots, COLS)
    following = jnp.concatenate([flat[:, 1:], jnp.zeros_like(flat[:, :1])], axis=1)
    pairs = jnp.concatenate([flat, following], axis=0).transpose(1, 0, 2).reshape(slots, 4 * COLS)
    high = lax.reduce_precision(pairs, exponent_bits=8, mantissa_bits=7)
    rest = pairs - high
    middle = lax.reduce_precision(rest, exponent_bits=8, mantissa_bits=7)
    low = rest - middle
    high, middle, low = (x.astype(jnp.bfloat16) for x in (high, middle, low))
    rows = start.size
    return pl.pallas_call(
        extract_kernel,
        grid=(rows // ROWS,),
        in_specs=[
            pl.BlockSpec((ROWS, 1), lambda q: (q, 0)),
            pl.BlockSpec((ROWS, 1), lambda q: (q, 0)),
            pl.BlockSpec((slots, 4 * COLS), lambda q: (0, 0)),
            pl.BlockSpec((slots, 4 * COLS), lambda q: (0, 0)),
            pl.BlockSpec((slots, 4 * COLS), lambda q: (0, 0)),
        ],
        out_specs=pl.BlockSpec((2, ROWS, COLS), lambda q: (0, q, 0)),
        out_shape=jax.ShapeDtypeStruct((2, rows, COLS), jnp.bfloat16),
        compiler_params=pltpu.CompilerParams(vmem_limit_bytes=48 * 1024 * 1024),
        cost_estimate=pl.CostEstimate(
            flops=24 * rows * slots * COLS,
            bytes_accessed=3 * slots * 4 * COLS * 2 + 2 * rows * COLS * 2,
            transcendentals=0,
        ),
    )(start.reshape(rows, 1), weight.reshape(rows, 1), high, middle, low)


def staged_sum(x, dim, outer, inner, outer_first):
    outer_count = lax.axis_size(outer)
    inner_count = lax.axis_size(inner)
    shape = x.shape
    block = shape[dim] // (outer_count * inner_count)
    split = x.reshape(shape[:dim] + (outer_count, inner_count, block) + shape[dim + 1 :])
    if outer_first:
        split = scatter_sum(scatter_sum(split, outer, dim), inner, dim + 1)
    else:
        split = scatter_sum(scatter_sum(split, inner, dim + 1), outer, dim)
    return split.reshape(shape[:dim] + (block,) + shape[dim + 1 :])


def body(
    images,
    defocus,
    candidates,
    counts,
    noise_weight,
    volume,
    row_plane,
    row_line,
    row_weight,
    regularizer,
):
    local_rows = noise_weight.shape[0]
    slab_id = lax.axis_index("vy") * lax.axis_size("vz") + lax.axis_index("vz")
    global_rows = slab_id * local_rows + jnp.arange(local_rows)
    row_freq = (global_rows.astype(jnp.float32) - ROWS // 2) / ROWS
    col_freq = jnp.arange(COLS).astype(jnp.float32) / (2 * COLS)
    img_count = lax.axis_size("ix") * lax.axis_size("ic")
    group_id = lax.axis_index("ix") * lax.axis_size("ic") + lax.axis_index("ic")
    share = K // img_count
    first = group_id * share
    plane_share = lax.dynamic_slice_in_dim(row_plane, first, share, 0)
    line_share = lax.dynamic_slice_in_dim(row_line, first, share, 0)
    weight_share = lax.dynamic_slice_in_dim(row_weight, first, share, 0)
    planes_here = volume.shape[1]
    local_plane = plane_share - slab_id * planes_here
    in_slab = (local_plane >= 0) & (local_plane < planes_here)
    start = jnp.where(in_slab, local_plane * ROWS + line_share, -2)
    masked = extract_share(volume, start.reshape(-1), weight_share.reshape(-1))
    own_rows = staged_sum(masked.reshape(2, share, ROWS, COLS), 2, "vy", "vz", True)
    slices = gather_all(own_rows, ("ix", "ic"), 1)
    cosine, sine = shift_phases(row_freq, col_freq, TRANS)
    shifted, power = make_references(slices, cosine, sine)
    contrast = contrast_of(defocus, row_freq, col_freq)
    weighted = ((contrast * noise_weight)[None] * images).astype(jnp.bfloat16)
    squared = (contrast * contrast * noise_weight).astype(jnp.bfloat16)
    cross = jnp.einsum("jbrc,tkjrc->btk", weighted, shifted, preferred_element_type=jnp.float32)
    quadratic = jnp.einsum("brc,krc->bk", squared, power, preferred_element_type=jnp.float32)
    partial_logits = cross - 0.5 * quadratic[:, None, :]
    orientation = jnp.arange(K, dtype=jnp.int32)
    pick = candidates[:, :, None] == orientation[None, None, :]
    chosen = jnp.sum(
        jnp.where(pick[:, None, :, :], partial_logits[:, :, None, :], 0.0), axis=3
    )
    logits = gather_all(scatter_sum(chosen, ("vy", "vz"), 0), ("vy", "vz"), 0)
    listed = posterior_of(logits, counts)
    weights = jnp.sum(
        jnp.where(pick[:, None, :, :], listed[:, :, :, None], jnp.zeros((), jnp.bfloat16)),
        axis=2,
    )
    y_part = jnp.einsum("btk,jbrc->tkrjc", weights, weighted, preferred_element_type=jnp.float32)
    d_part = jnp.einsum("btk,brc->tkrc", weights, squared, preferred_element_type=jnp.float32)
    num_re = jnp.sum(
        cosine[:, None] * y_part[:, :, :, 0] + sine[:, None] * y_part[:, :, :, 1], axis=0
    )
    num_im = jnp.sum(
        cosine[:, None] * y_part[:, :, :, 1] - sine[:, None] * y_part[:, :, :, 0], axis=0
    )
    stacked = jnp.stack([num_re, num_im, jnp.sum(d_part, axis=0)], axis=2)
    chips = lax.axis_size("ix")
    cores = lax.axis_size("ic")
    split = stacked.reshape((chips, cores, K // (chips * cores)) + stacked.shape[1:])
    within = scatter_sum(split, "ic", 1).astype(jnp.bfloat16)
    received = lax.all_to_all(within, "ix", 0, 0, tiled=True)
    partial_value = jnp.sum(received.astype(jnp.float32), axis=0).reshape(
        (K // (chips * cores),) + stacked.shape[1:]
    )
    piece = gather_all(gather_all(partial_value.astype(jnp.bfloat16), "vz", 1), "vy", 1)
    inserted = insert_rows(
        piece.reshape(share * ROWS, 3 * COLS),
        start.reshape(-1),
        weight_share.reshape(-1),
        planes_here,
        chips,
        cores,
    )
    within = scatter_sum(inserted, "ic", 1).astype(jnp.bfloat16)
    received = lax.all_to_all(within, "ix", 0, 0, tiled=True)
    summed = jnp.sum(received.astype(jnp.float32), axis=0).reshape(
        planes_here, ROWS // (chips * cores), 3, COLS
    )
    denom = summed[:, :, 2] + regularizer
    return jnp.stack([summed[:, :, 0] / denom, summed[:, :, 1] / denom], axis=0)


def solution(mesh):
    chips = dict(zip(mesh.axis_names, mesh.devices.shape))["img"] // 2
    rings = mesh.devices.shape[1] // 8
    return jax.shard_map(
        body,
        mesh=Mesh(mesh.devices.reshape(chips, -1, rings, mesh.devices.shape[1] // rings), ("ix", "ic", "vy", "vz")),
        in_specs=(
            P(None, ("ix", "ic"), ("vy", "vz"), None),
            P(("ix", "ic")),
            P(("ix", "ic"), None),
            P(("ix", "ic")),
            P(("vy", "vz"), None),
            P(None, ("vy", "vz"), None, None),
            P(),
            P(),
            P(),
            P(("vy", "vz"), ("ix", "ic"), None),
        ),
        out_specs=P(None, ("vy", "vz"), ("ix", "ic"), None),
        check_vma=False,
    )
```

```python
import math

import jax
import jax.numpy as jnp
from jax import lax
from jax.experimental import pallas as pl
from jax.experimental.pallas import tpu as pltpu
from jax.sharding import Mesh, PartitionSpec as P

ROWS = 256
COLS = 128
K = 64
TRANS = 4


AMPLITUDE = 0.1


def contrast_of(defocus, row_freq, col_freq):
    radius_sq = row_freq[:, None] * row_freq[:, None] + col_freq[None, :] * col_freq[None, :]
    angle = defocus[:, None, None] * radius_sq[None]
    return -(math.sqrt(1.0 - AMPLITUDE * AMPLITUDE) * jnp.sin(angle) + AMPLITUDE * jnp.cos(angle))


def shift_phases(row_freq, col_freq, number):
    shift_ids = jnp.arange(number)
    shift_x = (shift_ids % 2).astype(jnp.float32) - 0.5
    shift_y = (shift_ids // 2).astype(jnp.float32) - 0.5
    angle = (
        -2.0
        * math.pi
        * (
            shift_x[:, None, None] * col_freq[None, None, :]
            + shift_y[:, None, None] * row_freq[None, :, None]
        )
    )
    return (jnp.cos(angle), jnp.sin(angle))


def make_references(slices, cosine, sine):
    real_part = slices[0].astype(jnp.float32)
    imag_part = slices[1].astype(jnp.float32)
    shift_re = cosine[:, None] * real_part[None] - sine[:, None] * imag_part[None]
    shift_im = sine[:, None] * real_part[None] + cosine[:, None] * imag_part[None]
    shifted = jnp.stack([shift_re, shift_im], axis=2).astype(jnp.bfloat16)
    power = (real_part * real_part + imag_part * imag_part).astype(jnp.bfloat16)
    return (shifted, power)


def posterior_of(logits, counts):
    allowed = (jnp.arange(logits.shape[2])[None, :] < counts[:, None])[:, None, :]
    masked = jnp.where(allowed, logits, -1e30)
    highest = jnp.max(masked, axis=(1, 2), keepdims=True)
    exponent = jnp.where(allowed, jnp.exp(masked - highest), 0.0)
    return (exponent / jnp.sum(exponent, axis=(1, 2), keepdims=True)).astype(jnp.bfloat16)


def extract_rows(volume, plane_part, line_part, weight_part, slab_id):
    planes_here = volume.shape[1]
    flat = volume.reshape(2, planes_here * ROWS, COLS)
    local_plane = plane_part - slab_id * planes_here
    owned = (local_plane >= 0) & (local_plane < planes_here)
    line_index = jnp.clip(local_plane, 0, planes_here - 1) * ROWS + line_part
    lower = jnp.take(flat, line_index, axis=1)
    upper = jnp.take(flat, line_index + 1, axis=1)
    weight = weight_part[None, :, :, None]
    values = weight * lower + (1.0 - weight) * upper
    rounded = jnp.where(owned[None, :, :, None], values, 0.0).astype(jnp.bfloat16)
    return lax.optimization_barrier(rounded).astype(jnp.float32)


def insert_into(
    carry, piece, planes_all, lines_all, weights_all, slab_id, planes_here, line_first, line_count
):
    orient_count = piece.shape[0]
    number = piece.shape[1]
    local_plane = planes_all - slab_id * planes_here
    local_line = lines_all - line_first
    in_slab = (local_plane >= 0) & (local_plane < planes_here)
    lower_ok = in_slab & (local_line >= 0) & (local_line < line_count)
    upper_ok = in_slab & (local_line + 1 >= 0) & (local_line + 1 < line_count)
    dump_row = planes_here * line_count
    lower_index = jnp.where(lower_ok, local_plane * line_count + local_line, dump_row).reshape(-1)
    upper_index = jnp.where(upper_ok, local_plane * line_count + local_line + 1, dump_row).reshape(
        -1
    )
    values = piece.reshape(orient_count * number, 3 * COLS)
    weight = weights_all.reshape(-1, 1)
    carry = carry.at[lower_index].add(weight * values)
    return carry.at[upper_index].add((1.0 - weight) * values)


def scatter_sum(x, axis_name, dim):
    count = lax.axis_size(axis_name)
    shape = x.shape
    split = x.reshape(shape[:dim] + (count, shape[dim] // count) + shape[dim + 1 :])
    received = lax.all_to_all(split, axis_name, dim, dim, tiled=True)
    return jnp.sum(received, axis=dim)


def gather_all(x, axis_name, dim):
    count = lax.axis_size(axis_name)
    copies = jnp.broadcast_to(x[None], (count,) + x.shape)
    received = jnp.moveaxis(lax.all_to_all(copies, axis_name, 0, 0, tiled=True), 0, dim)
    return received.reshape(x.shape[:dim] + (count * x.shape[dim],) + x.shape[dim + 1 :])


def insert_kernel(start_ref, weight_ref, value_ref, out_ref):
    lines = ROWS
    rows = value_ref.shape[0]
    chunk = 512
    first_slot = pl.program_id(0) * lines
    slot = first_slot + lax.broadcasted_iota(jnp.int32, (lines, chunk), 0)
    total = jnp.zeros((lines, value_ref.shape[1]), jnp.float32)
    for part in range(rows // chunk):
        cols = pl.ds(part * chunk, chunk)
        start = start_ref[:, cols]
        weight = weight_ref[:, cols]
        spread = jnp.where(slot == start, weight, jnp.where(slot == start + 1, 1.0 - weight, 0.0))
        high = spread.astype(jnp.bfloat16)
        low = (spread - high.astype(jnp.float32)).astype(jnp.bfloat16)
        block = value_ref[cols, :]
        total += jnp.dot(high, block, preferred_element_type=jnp.float32)
        total += jnp.dot(low, block, preferred_element_type=jnp.float32)
    out_ref[...] = total.reshape(out_ref.shape)


def insert_rows(values, start, weight, planes_here, chips, cores):
    rows, width = values.shape
    block = ROWS // (chips * cores)
    return pl.pallas_call(
        insert_kernel,
        grid=(planes_here,),
        in_specs=[
            pl.BlockSpec((1, rows), lambda q: (0, 0)),
            pl.BlockSpec((1, rows), lambda q: (0, 0)),
            pl.BlockSpec((rows, width), lambda q: (0, 0)),
        ],
        out_specs=pl.BlockSpec((chips, cores, 1, block, width), lambda q: (0, 0, q, 0, 0)),
        out_shape=jax.ShapeDtypeStruct((chips, cores, planes_here, block, width), jnp.float32),
        compiler_params=pltpu.CompilerParams(vmem_limit_bytes=48 * 1024 * 1024),
        cost_estimate=pl.CostEstimate(
            flops=4 * planes_here * ROWS * rows * width,
            bytes_accessed=rows * width * 2 + planes_here * ROWS * width * 4,
            transcendentals=0,
        ),
    )(start.reshape(1, rows), weight.reshape(1, rows), values)


def extract_kernel(start_ref, weight_ref, high_ref, middle_ref, low_ref, out_ref):
    rows = out_ref.shape[1]
    slots = high_ref.shape[0]
    chunk = 512
    start = start_ref[...]
    total = jnp.zeros((rows, high_ref.shape[1]), jnp.float32)
    for part in range(slots // chunk):
        slot = part * chunk + lax.broadcasted_iota(jnp.int32, (rows, chunk), 1)
        pick = (slot == start).astype(jnp.bfloat16)
        cols = pl.ds(part * chunk, chunk)
        for piece_ref in (high_ref, middle_ref, low_ref):
            total += jnp.dot(pick, piece_ref[cols, :], preferred_element_type=jnp.float32)
    weight = weight_ref[...]
    for j in range(2):
        lower = total[:, j * COLS : (j + 1) * COLS]
        upper = total[:, (2 + j) * COLS : (3 + j) * COLS]
        out_ref[j] = (weight * lower + (1.0 - weight) * upper).astype(out_ref.dtype)


def extract_share(volume, start, weight):
    slots = volume.shape[1] * ROWS
    flat = volume.reshape(2, slots, COLS)
    following = jnp.concatenate([flat[:, 1:], jnp.zeros_like(flat[:, :1])], axis=1)
    pairs = jnp.concatenate([flat, following], axis=0).transpose(1, 0, 2).reshape(slots, 4 * COLS)
    high = lax.reduce_precision(pairs, exponent_bits=8, mantissa_bits=7)
    rest = pairs - high
    middle = lax.reduce_precision(rest, exponent_bits=8, mantissa_bits=7)
    low = rest - middle
    high, middle, low = (x.astype(jnp.bfloat16) for x in (high, middle, low))
    rows = start.size
    return pl.pallas_call(
        extract_kernel,
        grid=(rows // (2 * ROWS),),
        in_specs=[
            pl.BlockSpec((2 * ROWS, 1), lambda q: (q, 0)),
            pl.BlockSpec((2 * ROWS, 1), lambda q: (q, 0)),
            pl.BlockSpec((slots, 4 * COLS), lambda q: (0, 0)),
            pl.BlockSpec((slots, 4 * COLS), lambda q: (0, 0)),
            pl.BlockSpec((slots, 4 * COLS), lambda q: (0, 0)),
        ],
        out_specs=pl.BlockSpec((2, 2 * ROWS, COLS), lambda q: (0, q, 0)),
        out_shape=jax.ShapeDtypeStruct((2, rows, COLS), jnp.bfloat16),
        compiler_params=pltpu.CompilerParams(vmem_limit_bytes=48 * 1024 * 1024),
        cost_estimate=pl.CostEstimate(
            flops=24 * rows * slots * COLS,
            bytes_accessed=3 * slots * 4 * COLS * 2 + 2 * rows * COLS * 2,
            transcendentals=0,
        ),
    )(start.reshape(rows, 1), weight.reshape(rows, 1), high, middle, low)


def staged_sum(x, dim, outer, inner, outer_first):
    outer_count = lax.axis_size(outer)
    inner_count = lax.axis_size(inner)
    shape = x.shape
    block = shape[dim] // (outer_count * inner_count)
    split = x.reshape(shape[:dim] + (outer_count, inner_count, block) + shape[dim + 1 :])
    if outer_first:
        split = scatter_sum(scatter_sum(split, outer, dim), inner, dim + 1)
    else:
        split = scatter_sum(scatter_sum(split, inner, dim + 1), outer, dim)
    return split.reshape(shape[:dim] + (block,) + shape[dim + 1 :])


def body(
    images,
    defocus,
    candidates,
    counts,
    noise_weight,
    volume,
    row_plane,
    row_line,
    row_weight,
    regularizer,
):
    local_rows = noise_weight.shape[0]
    slab_id = lax.axis_index("vy") * lax.axis_size("vz") + lax.axis_index("vz")
    global_rows = slab_id * local_rows + jnp.arange(local_rows)
    row_freq = (global_rows.astype(jnp.float32) - ROWS // 2) / ROWS
    col_freq = jnp.arange(COLS).astype(jnp.float32) / (2 * COLS)
    img_count = lax.axis_size("ix") * lax.axis_size("ic")
    group_id = lax.axis_index("ix") * lax.axis_size("ic") + lax.axis_index("ic")
    share = K // img_count
    first = group_id * share
    plane_share = lax.dynamic_slice_in_dim(row_plane, first, share, 0)
    line_share = lax.dynamic_slice_in_dim(row_line, first, share, 0)
    weight_share = lax.dynamic_slice_in_dim(row_weight, first, share, 0)
    planes_here = volume.shape[1]
    local_plane = plane_share - slab_id * planes_here
    in_slab = (local_plane >= 0) & (local_plane < planes_here)
    start = jnp.where(in_slab, local_plane * ROWS + line_share, -2)
    masked = extract_share(volume, start.reshape(-1), weight_share.reshape(-1))
    own_rows = staged_sum(masked.reshape(2, share, ROWS, COLS), 2, "vy", "vz", True)
    slices = gather_all(own_rows, ("ix", "ic"), 1)
    cosine, sine = shift_phases(row_freq, col_freq, TRANS)
    shifted, power = make_references(slices, cosine, sine)
    contrast = contrast_of(defocus, row_freq, col_freq)
    weighted = ((contrast * noise_weight)[None] * images).astype(jnp.bfloat16)
    squared = (contrast * contrast * noise_weight).astype(jnp.bfloat16)
    cross = jnp.einsum("jbrc,tkjrc->btk", weighted, shifted, preferred_element_type=jnp.float32)
    quadratic = jnp.einsum("brc,krc->bk", squared, power, preferred_element_type=jnp.float32)
    partial_logits = cross - 0.5 * quadratic[:, None, :]
    orientation = jnp.arange(K, dtype=jnp.int32)
    pick = candidates[:, :, None] == orientation[None, None, :]
    chosen = jnp.sum(
        jnp.where(pick[:, None, :, :], partial_logits[:, :, None, :], 0.0), axis=3
    )
    logits = gather_all(scatter_sum(chosen, ("vy", "vz"), 0), ("vy", "vz"), 0)
    listed = posterior_of(logits, counts)
    weights = jnp.sum(
        jnp.where(pick[:, None, :, :], listed[:, :, :, None], jnp.zeros((), jnp.bfloat16)),
        axis=2,
    )
    y_part = jnp.einsum("btk,jbrc->tkrjc", weights, weighted, preferred_element_type=jnp.float32)
    d_part = jnp.einsum("btk,brc->tkrc", weights, squared, preferred_element_type=jnp.float32)
    num_re = jnp.sum(
        cosine[:, None] * y_part[:, :, :, 0] + sine[:, None] * y_part[:, :, :, 1], axis=0
    )
    num_im = jnp.sum(
        cosine[:, None] * y_part[:, :, :, 1] - sine[:, None] * y_part[:, :, :, 0], axis=0
    )
    stacked = jnp.stack([num_re, num_im, jnp.sum(d_part, axis=0)], axis=2)
    chips = lax.axis_size("ix")
    cores = lax.axis_size("ic")
    split = stacked.reshape((chips, cores, K // (chips * cores)) + stacked.shape[1:])
    within = scatter_sum(split, "ic", 1).astype(jnp.bfloat16)
    received = lax.all_to_all(within, "ix", 0, 0, tiled=True)
    partial_value = jnp.sum(received.astype(jnp.float32), axis=0).reshape(
        (K // (chips * cores),) + stacked.shape[1:]
    )
    piece = gather_all(gather_all(partial_value.astype(jnp.bfloat16), "vz", 1), "vy", 1)
    inserted = insert_rows(
        piece.reshape(share * ROWS, 3 * COLS),
        start.reshape(-1),
        weight_share.reshape(-1),
        planes_here,
        chips,
        cores,
    )
    within = scatter_sum(inserted, "ic", 1).astype(jnp.bfloat16)
    received = lax.all_to_all(within, "ix", 0, 0, tiled=True)
    summed = jnp.sum(received.astype(jnp.float32), axis=0).reshape(
        planes_here, ROWS // (chips * cores), 3, COLS
    )
    denom = summed[:, :, 2] + regularizer
    return jnp.stack([summed[:, :, 0] / denom, summed[:, :, 1] / denom], axis=0)


def solution(mesh):
    chips = dict(zip(mesh.axis_names, mesh.devices.shape))["img"] // 2
    rings = mesh.devices.shape[1] // 8
    return jax.shard_map(
        body,
        mesh=Mesh(mesh.devices.reshape(chips, -1, rings, mesh.devices.shape[1] // rings), ("ix", "ic", "vy", "vz")),
        in_specs=(
            P(None, ("ix", "ic"), ("vy", "vz"), None),
            P(("ix", "ic")),
            P(("ix", "ic"), None),
            P(("ix", "ic")),
            P(("vy", "vz"), None),
            P(None, ("vy", "vz"), None, None),
            P(),
            P(),
            P(),
            P(("vy", "vz"), ("ix", "ic"), None),
        ),
        out_specs=P(None, ("vy", "vz"), ("ix", "ic"), None),
        check_vma=False,
    )
```

```python
import math

import jax
import jax.numpy as jnp
from jax import lax
from jax.experimental import pallas as pl
from jax.experimental.pallas import tpu as pltpu
from jax.sharding import Mesh, PartitionSpec as P

ROWS = 256
COLS = 128
K = 64
TRANS = 4


AMPLITUDE = 0.1


def contrast_of(defocus, row_freq, col_freq):
    radius_sq = row_freq[:, None] * row_freq[:, None] + col_freq[None, :] * col_freq[None, :]
    angle = defocus[:, None, None] * radius_sq[None]
    return -(math.sqrt(1.0 - AMPLITUDE * AMPLITUDE) * jnp.sin(angle) + AMPLITUDE * jnp.cos(angle))


def shift_phases(row_freq, col_freq, number):
    shift_ids = jnp.arange(number)
    shift_x = (shift_ids % 2).astype(jnp.float32) - 0.5
    shift_y = (shift_ids // 2).astype(jnp.float32) - 0.5
    angle = (
        -2.0
        * math.pi
        * (
            shift_x[:, None, None] * col_freq[None, None, :]
            + shift_y[:, None, None] * row_freq[None, :, None]
        )
    )
    return (jnp.cos(angle), jnp.sin(angle))


def make_references(slices, cosine, sine):
    real_part = slices[0].astype(jnp.float32)
    imag_part = slices[1].astype(jnp.float32)
    shift_re = cosine[:, None] * real_part[None] - sine[:, None] * imag_part[None]
    shift_im = sine[:, None] * real_part[None] + cosine[:, None] * imag_part[None]
    shifted = jnp.stack([shift_re, shift_im], axis=2).astype(jnp.bfloat16)
    power = (real_part * real_part + imag_part * imag_part).astype(jnp.bfloat16)
    return (shifted, power)


def posterior_of(logits, counts):
    allowed = (jnp.arange(logits.shape[2])[None, :] < counts[:, None])[:, None, :]
    masked = jnp.where(allowed, logits, -1e30)
    highest = jnp.max(masked, axis=(1, 2), keepdims=True)
    exponent = jnp.where(allowed, jnp.exp(masked - highest), 0.0)
    return (exponent / jnp.sum(exponent, axis=(1, 2), keepdims=True)).astype(jnp.bfloat16)


def extract_rows(volume, plane_part, line_part, weight_part, slab_id):
    planes_here = volume.shape[1]
    flat = volume.reshape(2, planes_here * ROWS, COLS)
    local_plane = plane_part - slab_id * planes_here
    owned = (local_plane >= 0) & (local_plane < planes_here)
    line_index = jnp.clip(local_plane, 0, planes_here - 1) * ROWS + line_part
    lower = jnp.take(flat, line_index, axis=1)
    upper = jnp.take(flat, line_index + 1, axis=1)
    weight = weight_part[None, :, :, None]
    values = weight * lower + (1.0 - weight) * upper
    rounded = jnp.where(owned[None, :, :, None], values, 0.0).astype(jnp.bfloat16)
    return lax.optimization_barrier(rounded).astype(jnp.float32)


def insert_into(
    carry, piece, planes_all, lines_all, weights_all, slab_id, planes_here, line_first, line_count
):
    orient_count = piece.shape[0]
    number = piece.shape[1]
    local_plane = planes_all - slab_id * planes_here
    local_line = lines_all - line_first
    in_slab = (local_plane >= 0) & (local_plane < planes_here)
    lower_ok = in_slab & (local_line >= 0) & (local_line < line_count)
    upper_ok = in_slab & (local_line + 1 >= 0) & (local_line + 1 < line_count)
    dump_row = planes_here * line_count
    lower_index = jnp.where(lower_ok, local_plane * line_count + local_line, dump_row).reshape(-1)
    upper_index = jnp.where(upper_ok, local_plane * line_count + local_line + 1, dump_row).reshape(
        -1
    )
    values = piece.reshape(orient_count * number, 3 * COLS)
    weight = weights_all.reshape(-1, 1)
    carry = carry.at[lower_index].add(weight * values)
    return carry.at[upper_index].add((1.0 - weight) * values)


def scatter_sum(x, axis_name, dim):
    count = lax.axis_size(axis_name)
    shape = x.shape
    split = x.reshape(shape[:dim] + (count, shape[dim] // count) + shape[dim + 1 :])
    received = lax.all_to_all(split, axis_name, dim, dim, tiled=True)
    return jnp.sum(received, axis=dim)


def gather_all(x, axis_name, dim):
    count = lax.axis_size(axis_name)
    copies = jnp.broadcast_to(x[None], (count,) + x.shape)
    received = jnp.moveaxis(lax.all_to_all(copies, axis_name, 0, 0, tiled=True), 0, dim)
    return received.reshape(x.shape[:dim] + (count * x.shape[dim],) + x.shape[dim + 1 :])


def insert_kernel(start_ref, weight_ref, value_ref, out_ref):
    lines = ROWS
    rows = value_ref.shape[0]
    chunk = 512
    first_slot = pl.program_id(0) * lines
    slot = first_slot + lax.broadcasted_iota(jnp.int32, (lines, chunk), 0)
    total = jnp.zeros((lines, value_ref.shape[1]), jnp.float32)
    for part in range(rows // chunk):
        cols = pl.ds(part * chunk, chunk)
        start = start_ref[:, cols]
        weight = weight_ref[:, cols]
        spread = jnp.where(slot == start, weight, jnp.where(slot == start + 1, 1.0 - weight, 0.0))
        high = spread.astype(jnp.bfloat16)
        low = (spread - high.astype(jnp.float32)).astype(jnp.bfloat16)
        block = value_ref[cols, :]
        total += jnp.dot(high, block, preferred_element_type=jnp.float32)
        total += jnp.dot(low, block, preferred_element_type=jnp.float32)
    out_ref[...] = total.reshape(out_ref.shape)


def insert_rows(values, start, weight, planes_here, chips, cores):
    rows, width = values.shape
    block = ROWS // (chips * cores)
    return pl.pallas_call(
        insert_kernel,
        grid=(planes_here,),
        in_specs=[
            pl.BlockSpec((1, rows), lambda q: (0, 0)),
            pl.BlockSpec((1, rows), lambda q: (0, 0)),
            pl.BlockSpec((rows, width), lambda q: (0, 0)),
        ],
        out_specs=pl.BlockSpec((chips, cores, 1, block, width), lambda q: (0, 0, q, 0, 0)),
        out_shape=jax.ShapeDtypeStruct((chips, cores, planes_here, block, width), jnp.float32),
        compiler_params=pltpu.CompilerParams(vmem_limit_bytes=48 * 1024 * 1024),
        cost_estimate=pl.CostEstimate(
            flops=4 * planes_here * ROWS * rows * width,
            bytes_accessed=rows * width * 2 + planes_here * ROWS * width * 4,
            transcendentals=0,
        ),
    )(start.reshape(1, rows), weight.reshape(1, rows), values)


def extract_kernel(start_ref, weight_ref, high_ref, middle_ref, low_ref, out_ref):
    rows = out_ref.shape[1]
    slots = high_ref.shape[0]
    chunk = 512
    start = start_ref[...]
    width = high_ref.shape[1]
    below = jnp.zeros((rows, width), jnp.float32)
    above = jnp.zeros((rows, width), jnp.float32)
    for part in range(slots // chunk):
        slot = part * chunk + lax.broadcasted_iota(jnp.int32, (rows, chunk), 1)
        pick_below = (slot == start).astype(jnp.bfloat16)
        pick_above = (slot == start + 1).astype(jnp.bfloat16)
        cols = pl.ds(part * chunk, chunk)
        for piece_ref in (high_ref, middle_ref, low_ref):
            piece = piece_ref[cols, :]
            below += jnp.dot(pick_below, piece, preferred_element_type=jnp.float32)
            above += jnp.dot(pick_above, piece, preferred_element_type=jnp.float32)
    weight = weight_ref[...]
    for j in range(2):
        lower = below[:, j * COLS : (j + 1) * COLS]
        upper = above[:, j * COLS : (j + 1) * COLS]
        out_ref[j] = (weight * lower + (1.0 - weight) * upper).astype(out_ref.dtype)


def extract_share(volume, start, weight):
    slots = volume.shape[1] * ROWS
    flat = volume.reshape(2, slots, COLS)
    pairs = flat.transpose(1, 0, 2).reshape(slots, 2 * COLS)
    high = lax.reduce_precision(pairs, exponent_bits=8, mantissa_bits=7)
    rest = pairs - high
    middle = lax.reduce_precision(rest, exponent_bits=8, mantissa_bits=7)
    low = rest - middle
    high, middle, low = (x.astype(jnp.bfloat16) for x in (high, middle, low))
    rows = start.size
    return pl.pallas_call(
        extract_kernel,
        grid=(rows // (2 * ROWS),),
        in_specs=[
            pl.BlockSpec((2 * ROWS, 1), lambda q: (q, 0)),
            pl.BlockSpec((2 * ROWS, 1), lambda q: (q, 0)),
            pl.BlockSpec((slots, 2 * COLS), lambda q: (0, 0)),
            pl.BlockSpec((slots, 2 * COLS), lambda q: (0, 0)),
            pl.BlockSpec((slots, 2 * COLS), lambda q: (0, 0)),
        ],
        out_specs=pl.BlockSpec((2, 2 * ROWS, COLS), lambda q: (0, q, 0)),
        out_shape=jax.ShapeDtypeStruct((2, rows, COLS), jnp.bfloat16),
        compiler_params=pltpu.CompilerParams(vmem_limit_bytes=48 * 1024 * 1024),
        cost_estimate=pl.CostEstimate(
            flops=24 * rows * slots * COLS,
            bytes_accessed=3 * slots * 2 * COLS * 2 + 2 * rows * COLS * 2,
            transcendentals=0,
        ),
    )(start.reshape(rows, 1), weight.reshape(rows, 1), high, middle, low)


def staged_sum(x, dim, outer, inner, outer_first):
    outer_count = lax.axis_size(outer)
    inner_count = lax.axis_size(inner)
    shape = x.shape
    block = shape[dim] // (outer_count * inner_count)
    split = x.reshape(shape[:dim] + (outer_count, inner_count, block) + shape[dim + 1 :])
    if outer_first:
        split = scatter_sum(scatter_sum(split, outer, dim), inner, dim + 1)
    else:
        split = scatter_sum(scatter_sum(split, inner, dim + 1), outer, dim)
    return split.reshape(shape[:dim] + (block,) + shape[dim + 1 :])


def body(
    images,
    defocus,
    candidates,
    counts,
    noise_weight,
    volume,
    row_plane,
    row_line,
    row_weight,
    regularizer,
):
    local_rows = noise_weight.shape[0]
    slab_id = lax.axis_index("vy") * lax.axis_size("vz") + lax.axis_index("vz")
    global_rows = slab_id * local_rows + jnp.arange(local_rows)
    row_freq = (global_rows.astype(jnp.float32) - ROWS // 2) / ROWS
    col_freq = jnp.arange(COLS).astype(jnp.float32) / (2 * COLS)
    img_count = lax.axis_size("ix") * lax.axis_size("ic")
    group_id = lax.axis_index("ix") * lax.axis_size("ic") + lax.axis_index("ic")
    share = K // img_count
    first = group_id * share
    plane_share = lax.dynamic_slice_in_dim(row_plane, first, share, 0)
    line_share = lax.dynamic_slice_in_dim(row_line, first, share, 0)
    weight_share = lax.dynamic_slice_in_dim(row_weight, first, share, 0)
    planes_here = volume.shape[1]
    local_plane = plane_share - slab_id * planes_here
    in_slab = (local_plane >= 0) & (local_plane < planes_here)
    start = jnp.where(in_slab, local_plane * ROWS + line_share, -2)
    masked = extract_share(volume, start.reshape(-1), weight_share.reshape(-1))
    own_rows = staged_sum(masked.reshape(2, share, ROWS, COLS), 2, "vy", "vz", True)
    slices = gather_all(own_rows, ("ix", "ic"), 1)
    cosine, sine = shift_phases(row_freq, col_freq, TRANS)
    shifted, power = make_references(slices, cosine, sine)
    contrast = contrast_of(defocus, row_freq, col_freq)
    weighted = ((contrast * noise_weight)[None] * images).astype(jnp.bfloat16)
    squared = (contrast * contrast * noise_weight).astype(jnp.bfloat16)
    cross = jnp.einsum("jbrc,tkjrc->btk", weighted, shifted, preferred_element_type=jnp.float32)
    quadratic = jnp.einsum("brc,krc->bk", squared, power, preferred_element_type=jnp.float32)
    partial_logits = cross - 0.5 * quadratic[:, None, :]
    orientation = jnp.arange(K, dtype=jnp.int32)
    pick = candidates[:, :, None] == orientation[None, None, :]
    chosen = jnp.sum(
        jnp.where(pick[:, None, :, :], partial_logits[:, :, None, :], 0.0), axis=3
    )
    logits = gather_all(scatter_sum(chosen, ("vy", "vz"), 0), ("vy", "vz"), 0)
    listed = posterior_of(logits, counts)
    weights = jnp.sum(
        jnp.where(pick[:, None, :, :], listed[:, :, :, None], jnp.zeros((), jnp.bfloat16)),
        axis=2,
    )
    y_part = jnp.einsum("btk,jbrc->tkrjc", weights, weighted, preferred_element_type=jnp.float32)
    d_part = jnp.einsum("btk,brc->tkrc", weights, squared, preferred_element_type=jnp.float32)
    num_re = jnp.sum(
        cosine[:, None] * y_part[:, :, :, 0] + sine[:, None] * y_part[:, :, :, 1], axis=0
    )
    num_im = jnp.sum(
        cosine[:, None] * y_part[:, :, :, 1] - sine[:, None] * y_part[:, :, :, 0], axis=0
    )
    stacked = jnp.stack([num_re, num_im, jnp.sum(d_part, axis=0)], axis=2)
    chips = lax.axis_size("ix")
    cores = lax.axis_size("ic")
    split = stacked.reshape((chips, cores, K // (chips * cores)) + stacked.shape[1:])
    within = scatter_sum(split, "ic", 1).astype(jnp.bfloat16)
    received = lax.all_to_all(within, "ix", 0, 0, tiled=True)
    partial_value = jnp.sum(received.astype(jnp.float32), axis=0).reshape(
        (K // (chips * cores),) + stacked.shape[1:]
    )
    piece = gather_all(gather_all(partial_value.astype(jnp.bfloat16), "vz", 1), "vy", 1)
    inserted = insert_rows(
        piece.reshape(share * ROWS, 3 * COLS),
        start.reshape(-1),
        weight_share.reshape(-1),
        planes_here,
        chips,
        cores,
    )
    within = scatter_sum(inserted, "ic", 1).astype(jnp.bfloat16)
    received = lax.all_to_all(within, "ix", 0, 0, tiled=True)
    summed = jnp.sum(received.astype(jnp.float32), axis=0).reshape(
        planes_here, ROWS // (chips * cores), 3, COLS
    )
    denom = summed[:, :, 2] + regularizer
    return jnp.stack([summed[:, :, 0] / denom, summed[:, :, 1] / denom], axis=0)


def solution(mesh):
    chips = dict(zip(mesh.axis_names, mesh.devices.shape))["img"] // 2
    rings = mesh.devices.shape[1] // 8
    return jax.shard_map(
        body,
        mesh=Mesh(mesh.devices.reshape(chips, -1, rings, mesh.devices.shape[1] // rings), ("ix", "ic", "vy", "vz")),
        in_specs=(
            P(None, ("ix", "ic"), ("vy", "vz"), None),
            P(("ix", "ic")),
            P(("ix", "ic"), None),
            P(("ix", "ic")),
            P(("vy", "vz"), None),
            P(None, ("vy", "vz"), None, None),
            P(),
            P(),
            P(),
            P(("vy", "vz"), ("ix", "ic"), None),
        ),
        out_specs=P(None, ("vy", "vz"), ("ix", "ic"), None),
        check_vma=False,
    )
```

```python
import math

import jax
import jax.numpy as jnp
from jax import lax
from jax.experimental import pallas as pl
from jax.experimental.pallas import tpu as pltpu
from jax.sharding import Mesh, PartitionSpec as P

ROWS = 256
COLS = 128
K = 64
TRANS = 4


AMPLITUDE = 0.1


def contrast_of(defocus, row_freq, col_freq):
    radius_sq = row_freq[:, None] * row_freq[:, None] + col_freq[None, :] * col_freq[None, :]
    angle = defocus[:, None, None] * radius_sq[None]
    return -(math.sqrt(1.0 - AMPLITUDE * AMPLITUDE) * jnp.sin(angle) + AMPLITUDE * jnp.cos(angle))


def shift_phases(row_freq, col_freq, number):
    shift_ids = jnp.arange(number)
    shift_x = (shift_ids % 2).astype(jnp.float32) - 0.5
    shift_y = (shift_ids // 2).astype(jnp.float32) - 0.5
    angle = (
        -2.0
        * math.pi
        * (
            shift_x[:, None, None] * col_freq[None, None, :]
            + shift_y[:, None, None] * row_freq[None, :, None]
        )
    )
    return (jnp.cos(angle), jnp.sin(angle))


def make_references(slices, cosine, sine):
    real_part = slices[0].astype(jnp.float32)
    imag_part = slices[1].astype(jnp.float32)
    shift_re = cosine[:, None] * real_part[None] - sine[:, None] * imag_part[None]
    shift_im = sine[:, None] * real_part[None] + cosine[:, None] * imag_part[None]
    shifted = jnp.stack([shift_re, shift_im], axis=2).astype(jnp.bfloat16)
    power = (real_part * real_part + imag_part * imag_part).astype(jnp.bfloat16)
    return (shifted, power)


def posterior_of(logits, counts):
    allowed = (jnp.arange(logits.shape[2])[None, :] < counts[:, None])[:, None, :]
    masked = jnp.where(allowed, logits, -1e30)
    highest = jnp.max(masked, axis=(1, 2), keepdims=True)
    exponent = jnp.where(allowed, jnp.exp(masked - highest), 0.0)
    return (exponent / jnp.sum(exponent, axis=(1, 2), keepdims=True)).astype(jnp.bfloat16)


def extract_rows(volume, plane_part, line_part, weight_part, slab_id):
    planes_here = volume.shape[1]
    flat = volume.reshape(2, planes_here * ROWS, COLS)
    local_plane = plane_part - slab_id * planes_here
    owned = (local_plane >= 0) & (local_plane < planes_here)
    line_index = jnp.clip(local_plane, 0, planes_here - 1) * ROWS + line_part
    lower = jnp.take(flat, line_index, axis=1)
    upper = jnp.take(flat, line_index + 1, axis=1)
    weight = weight_part[None, :, :, None]
    values = weight * lower + (1.0 - weight) * upper
    rounded = jnp.where(owned[None, :, :, None], values, 0.0).astype(jnp.bfloat16)
    return lax.optimization_barrier(rounded).astype(jnp.float32)


def insert_into(
    carry, piece, planes_all, lines_all, weights_all, slab_id, planes_here, line_first, line_count
):
    orient_count = piece.shape[0]
    number = piece.shape[1]
    local_plane = planes_all - slab_id * planes_here
    local_line = lines_all - line_first
    in_slab = (local_plane >= 0) & (local_plane < planes_here)
    lower_ok = in_slab & (local_line >= 0) & (local_line < line_count)
    upper_ok = in_slab & (local_line + 1 >= 0) & (local_line + 1 < line_count)
    dump_row = planes_here * line_count
    lower_index = jnp.where(lower_ok, local_plane * line_count + local_line, dump_row).reshape(-1)
    upper_index = jnp.where(upper_ok, local_plane * line_count + local_line + 1, dump_row).reshape(
        -1
    )
    values = piece.reshape(orient_count * number, 3 * COLS)
    weight = weights_all.reshape(-1, 1)
    carry = carry.at[lower_index].add(weight * values)
    return carry.at[upper_index].add((1.0 - weight) * values)


def scatter_sum(x, axis_name, dim):
    count = lax.axis_size(axis_name)
    shape = x.shape
    split = x.reshape(shape[:dim] + (count, shape[dim] // count) + shape[dim + 1 :])
    received = lax.all_to_all(split, axis_name, dim, dim, tiled=True)
    return jnp.sum(received, axis=dim)


def gather_all(x, axis_name, dim):
    count = lax.axis_size(axis_name)
    copies = jnp.broadcast_to(x[None], (count,) + x.shape)
    received = jnp.moveaxis(lax.all_to_all(copies, axis_name, 0, 0, tiled=True), 0, dim)
    return received.reshape(x.shape[:dim] + (count * x.shape[dim],) + x.shape[dim + 1 :])


def insert_kernel(start_ref, weight_ref, value_ref, out_ref):
    lines = ROWS
    rows = value_ref.shape[0]
    chunk = 512
    first_slot = pl.program_id(0) * lines
    slot = first_slot + lax.broadcasted_iota(jnp.int32, (lines, chunk), 0)
    total = jnp.zeros((lines, value_ref.shape[1]), jnp.float32)
    for part in range(rows // chunk):
        cols = pl.ds(part * chunk, chunk)
        start = start_ref[:, cols]
        weight = weight_ref[:, cols]
        rest = 1.0 - weight
        weight_high = weight.astype(jnp.bfloat16)
        weight_low = (weight - weight_high.astype(jnp.float32)).astype(jnp.bfloat16)
        rest_high = rest.astype(jnp.bfloat16)
        rest_low = (rest - rest_high.astype(jnp.float32)).astype(jnp.bfloat16)
        first = slot == start
        second = slot == start + 1
        zero = jnp.zeros((), jnp.bfloat16)
        high = jnp.where(first, weight_high, jnp.where(second, rest_high, zero))
        low = jnp.where(first, weight_low, jnp.where(second, rest_low, zero))
        block = value_ref[cols, :]
        total += jnp.dot(high, block, preferred_element_type=jnp.float32)
        total += jnp.dot(low, block, preferred_element_type=jnp.float32)
    out_ref[...] = total.reshape(out_ref.shape)


def insert_rows(values, start, weight, planes_here, chips, cores):
    rows, width = values.shape
    block = ROWS // (chips * cores)
    return pl.pallas_call(
        insert_kernel,
        grid=(planes_here,),
        in_specs=[
            pl.BlockSpec((1, rows), lambda q: (0, 0)),
            pl.BlockSpec((1, rows), lambda q: (0, 0)),
            pl.BlockSpec((rows, width), lambda q: (0, 0)),
        ],
        out_specs=pl.BlockSpec((chips, cores, 1, block, width), lambda q: (0, 0, q, 0, 0)),
        out_shape=jax.ShapeDtypeStruct((chips, cores, planes_here, block, width), jnp.float32),
        compiler_params=pltpu.CompilerParams(vmem_limit_bytes=48 * 1024 * 1024),
        cost_estimate=pl.CostEstimate(
            flops=4 * planes_here * ROWS * rows * width,
            bytes_accessed=rows * width * 2 + planes_here * ROWS * width * 4,
            transcendentals=0,
        ),
    )(start.reshape(1, rows), weight.reshape(1, rows), values)


def extract_kernel(start_ref, weight_ref, high_ref, middle_ref, low_ref, out_ref):
    rows = out_ref.shape[1]
    slots = high_ref.shape[0]
    chunk = 512
    start = start_ref[...]
    width = high_ref.shape[1]
    below = jnp.zeros((rows, width), jnp.float32)
    above = jnp.zeros((rows, width), jnp.float32)
    for part in range(slots // chunk):
        slot = part * chunk + lax.broadcasted_iota(jnp.int32, (rows, chunk), 1)
        pick_below = (slot == start).astype(jnp.bfloat16)
        pick_above = (slot == start + 1).astype(jnp.bfloat16)
        cols = pl.ds(part * chunk, chunk)
        for piece_ref in (high_ref, middle_ref, low_ref):
            piece = piece_ref[cols, :]
            below += jnp.dot(pick_below, piece, preferred_element_type=jnp.float32)
            above += jnp.dot(pick_above, piece, preferred_element_type=jnp.float32)
    weight = weight_ref[...]
    for j in range(2):
        lower = below[:, j * COLS : (j + 1) * COLS]
        upper = above[:, j * COLS : (j + 1) * COLS]
        out_ref[j] = (weight * lower + (1.0 - weight) * upper).astype(out_ref.dtype)


def extract_share(volume, start, weight):
    slots = volume.shape[1] * ROWS
    flat = volume.reshape(2, slots, COLS)
    pairs = flat.transpose(1, 0, 2).reshape(slots, 2 * COLS)
    high = lax.reduce_precision(pairs, exponent_bits=8, mantissa_bits=7)
    rest = pairs - high
    middle = lax.reduce_precision(rest, exponent_bits=8, mantissa_bits=7)
    low = rest - middle
    high, middle, low = (x.astype(jnp.bfloat16) for x in (high, middle, low))
    rows = start.size
    return pl.pallas_call(
        extract_kernel,
        grid=(rows // (2 * ROWS),),
        in_specs=[
            pl.BlockSpec((2 * ROWS, 1), lambda q: (q, 0)),
            pl.BlockSpec((2 * ROWS, 1), lambda q: (q, 0)),
            pl.BlockSpec((slots, 2 * COLS), lambda q: (0, 0)),
            pl.BlockSpec((slots, 2 * COLS), lambda q: (0, 0)),
            pl.BlockSpec((slots, 2 * COLS), lambda q: (0, 0)),
        ],
        out_specs=pl.BlockSpec((2, 2 * ROWS, COLS), lambda q: (0, q, 0)),
        out_shape=jax.ShapeDtypeStruct((2, rows, COLS), jnp.bfloat16),
        compiler_params=pltpu.CompilerParams(vmem_limit_bytes=48 * 1024 * 1024),
        cost_estimate=pl.CostEstimate(
            flops=24 * rows * slots * COLS,
            bytes_accessed=3 * slots * 2 * COLS * 2 + 2 * rows * COLS * 2,
            transcendentals=0,
        ),
    )(start.reshape(rows, 1), weight.reshape(rows, 1), high, middle, low)


def staged_sum(x, dim, outer, inner, outer_first):
    outer_count = lax.axis_size(outer)
    inner_count = lax.axis_size(inner)
    shape = x.shape
    block = shape[dim] // (outer_count * inner_count)
    split = x.reshape(shape[:dim] + (outer_count, inner_count, block) + shape[dim + 1 :])
    if outer_first:
        split = scatter_sum(scatter_sum(split, outer, dim), inner, dim + 1)
    else:
        split = scatter_sum(scatter_sum(split, inner, dim + 1), outer, dim)
    return split.reshape(shape[:dim] + (block,) + shape[dim + 1 :])


def body(
    images,
    defocus,
    candidates,
    counts,
    noise_weight,
    volume,
    row_plane,
    row_line,
    row_weight,
    regularizer,
):
    local_rows = noise_weight.shape[0]
    slab_id = lax.axis_index("vy") * lax.axis_size("vz") + lax.axis_index("vz")
    global_rows = slab_id * local_rows + jnp.arange(local_rows)
    row_freq = (global_rows.astype(jnp.float32) - ROWS // 2) / ROWS
    col_freq = jnp.arange(COLS).astype(jnp.float32) / (2 * COLS)
    img_count = lax.axis_size("ix") * lax.axis_size("ic")
    group_id = lax.axis_index("ix") * lax.axis_size("ic") + lax.axis_index("ic")
    share = K // img_count
    first = group_id * share
    plane_share = lax.dynamic_slice_in_dim(row_plane, first, share, 0)
    line_share = lax.dynamic_slice_in_dim(row_line, first, share, 0)
    weight_share = lax.dynamic_slice_in_dim(row_weight, first, share, 0)
    planes_here = volume.shape[1]
    local_plane = plane_share - slab_id * planes_here
    in_slab = (local_plane >= 0) & (local_plane < planes_here)
    start = jnp.where(in_slab, local_plane * ROWS + line_share, -2)
    masked = extract_share(volume, start.reshape(-1), weight_share.reshape(-1))
    own_rows = staged_sum(masked.reshape(2, share, ROWS, COLS), 2, "vy", "vz", True)
    slices = gather_all(own_rows, ("ix", "ic"), 1)
    cosine, sine = shift_phases(row_freq, col_freq, TRANS)
    shifted, power = make_references(slices, cosine, sine)
    contrast = contrast_of(defocus, row_freq, col_freq)
    weighted = ((contrast * noise_weight)[None] * images).astype(jnp.bfloat16)
    squared = (contrast * contrast * noise_weight).astype(jnp.bfloat16)
    cross = jnp.einsum("jbrc,tkjrc->btk", weighted, shifted, preferred_element_type=jnp.float32)
    quadratic = jnp.einsum("brc,krc->bk", squared, power, preferred_element_type=jnp.float32)
    partial_logits = cross - 0.5 * quadratic[:, None, :]
    orientation = jnp.arange(K, dtype=jnp.int32)
    pick = candidates[:, :, None] == orientation[None, None, :]
    chosen = jnp.sum(
        jnp.where(pick[:, None, :, :], partial_logits[:, :, None, :], 0.0), axis=3
    )
    logits = gather_all(scatter_sum(chosen, ("vy", "vz"), 0), ("vy", "vz"), 0)
    listed = posterior_of(logits, counts)
    weights = jnp.sum(
        jnp.where(pick[:, None, :, :], listed[:, :, :, None], jnp.zeros((), jnp.bfloat16)),
        axis=2,
    )
    y_part = jnp.einsum("btk,jbrc->tkrjc", weights, weighted, preferred_element_type=jnp.float32)
    d_part = jnp.einsum("btk,brc->tkrc", weights, squared, preferred_element_type=jnp.float32)
    num_re = jnp.sum(
        cosine[:, None] * y_part[:, :, :, 0] + sine[:, None] * y_part[:, :, :, 1], axis=0
    )
    num_im = jnp.sum(
        cosine[:, None] * y_part[:, :, :, 1] - sine[:, None] * y_part[:, :, :, 0], axis=0
    )
    stacked = jnp.stack([num_re, num_im, jnp.sum(d_part, axis=0)], axis=2)
    chips = lax.axis_size("ix")
    cores = lax.axis_size("ic")
    split = stacked.reshape((chips, cores, K // (chips * cores)) + stacked.shape[1:])
    within = scatter_sum(split, "ic", 1).astype(jnp.bfloat16)
    received = lax.all_to_all(within, "ix", 0, 0, tiled=True)
    partial_value = jnp.sum(received.astype(jnp.float32), axis=0).reshape(
        (K // (chips * cores),) + stacked.shape[1:]
    )
    piece = gather_all(gather_all(partial_value.astype(jnp.bfloat16), "vz", 1), "vy", 1)
    inserted = insert_rows(
        piece.reshape(share * ROWS, 3 * COLS),
        start.reshape(-1),
        weight_share.reshape(-1),
        planes_here,
        chips,
        cores,
    )
    within = scatter_sum(inserted, "ic", 1).astype(jnp.bfloat16)
    received = lax.all_to_all(within, "ix", 0, 0, tiled=True)
    summed = jnp.sum(received.astype(jnp.float32), axis=0).reshape(
        planes_here, ROWS // (chips * cores), 3, COLS
    )
    denom = summed[:, :, 2] + regularizer
    return jnp.stack([summed[:, :, 0] / denom, summed[:, :, 1] / denom], axis=0)


def solution(mesh):
    chips = dict(zip(mesh.axis_names, mesh.devices.shape))["img"] // 2
    rings = mesh.devices.shape[1] // 8
    return jax.shard_map(
        body,
        mesh=Mesh(mesh.devices.reshape(chips, -1, rings, mesh.devices.shape[1] // rings), ("ix", "ic", "vy", "vz")),
        in_specs=(
            P(None, ("ix", "ic"), ("vy", "vz"), None),
            P(("ix", "ic")),
            P(("ix", "ic"), None),
            P(("ix", "ic")),
            P(("vy", "vz"), None),
            P(None, ("vy", "vz"), None, None),
            P(),
            P(),
            P(),
            P(("vy", "vz"), ("ix", "ic"), None),
        ),
        out_specs=P(None, ("vy", "vz"), ("ix", "ic"), None),
        check_vma=False,
    )
```
